256 devices in a mesh: px: 8 (over y, core), pz: 16 (over z, x_lo), tr: 2 (over x_hi).
Axes of the slice: x: 4 (x_hi: 2, x_lo: 2; x = x_hi * 2 + x_lo), y: 4, z: 8, core: 2. Of those that a mesh axis runs over, the one named last changes fastest.
Arguments:
- velocity: float32 [1024, 64, 3, 256], P('pz', ('px', 'tr')), may hold values from -6 to 6
- viscosity: float32 [1024, 64, 256], P('pz', ('px', 'tr')), may hold values from 0.5 to 2
- implicit_inverse: float32 [1024, 1024], replicated, may hold values from -0.1875 to 0.1875
- row_index: int32 [8, 16, 2, 32, 24], P('px', 'pz', 'tr'), may hold values from 0 to 255, as said below
- row_counts: int32 [8, 16, 2, 32], P('px', 'pz', 'tr'), may hold values from 0 to 24, as said below
- weight_in: bfloat16 [32, 768, 1024], P(('pz', 'tr')), may hold values from -0.21875 to 0.21875
- weight_out: bfloat16 [32, 1024, 768], P(('pz', 'tr')), may hold values from -0.1875 to 0.1875
Outputs:
- velocity_out: float32 [1024, 64, 3, 256], P('pz', ('px', 'tr'))
- grad_in: float32 [32, 768, 1024], P(('pz', 'tr'), 'px')
- grad_out: float32 [32, 1024, 768], P(('pz', 'tr'), 'px')
The draws below stay inside these ranges and needn't reach their ends.
Inputs may be any that keep to these rules, and one draw needn't show every extreme that they name: `row_index`: A slot's row number within its source device's block of 64 x 4 rows: wall-normal offset times 4 plus spanwise offset; on the first pz index rows lean toward the lower wall, on the last toward the upper wall; slots at or beyond the count are read but unused. `row_counts`: the first pz index, the last one, and every member whose number is a multiple of 8 have all 24 slots live.
All inputs are finite; a program needn't handle non-finite values.
Results may differ from the reference program's by a relative error of at most 0.02.
Values may be sent and summed in bfloat16 or wider, within the bound.
No kernel may reach another device: no remote copies, remote signals or barrier semaphores. Data moves between devices by JAX's collectives and lax.ppermute only.
A program may use at most 64 MiB of HBM per device.

```python
import math
import jax
import jax.numpy as jnp
from jax import lax

NY = 1024
NX = 256
ZL = 4
HID = 1024
SLOTS_DEV = 768
YL = 64
NZ = 64
IN = 768
MEMBERS = 32
CAP = 24
N_PX = 8
N_PZ = 16
N_TR = 2


def draw_row_counts(key, part):
    base_counts = jax.random.randint(key, (N_PX, N_PZ, N_TR, MEMBERS), 0, CAP)
    plane_index = jnp.arange(N_PZ, dtype=jnp.int32)[None, :, None, None]
    member_index = jnp.arange(MEMBERS, dtype=jnp.int32)[None, None, None, :]
    full_slots = (plane_index == 0) | (plane_index == N_PZ - 1) | (member_index % 8 == 0)
    return jnp.where(full_slots, CAP, base_counts).astype(jnp.int32)


def draw_row_index(key, part):
    first_key = jax.random.fold_in(key, 101)
    second_key = jax.random.fold_in(key, 202)
    shape = (N_PX, N_PZ, N_TR, MEMBERS, CAP)
    first_draw = jax.random.randint(first_key, shape, 0, YL * ZL)
    second_draw = jax.random.randint(second_key, shape, 0, YL * ZL)
    plane_index = jnp.arange(N_PZ, dtype=jnp.int32)[None, :, None, None, None]
    slot_index = jnp.arange(CAP, dtype=jnp.int32)[None, None, None, None, :]
    member_index = jnp.arange(MEMBERS, dtype=jnp.int32)[None, None, None, :, None]
    lower_wall = plane_index == 0
    upper_wall = plane_index == N_PZ - 1
    chosen = jnp.where(lower_wall, jnp.minimum(first_draw, second_draw), first_draw)
    chosen = jnp.where(upper_wall, jnp.maximum(first_draw, second_draw), chosen)
    corner = (slot_index == 0) & (member_index == 0)
    chosen = jnp.where(corner & lower_wall, 0, chosen)
    chosen = jnp.where(corner & upper_wall, YL * ZL - 1, chosen)
    return chosen.astype(jnp.int32)


def levels(key, extent, cuts, least, high):
    level = 1.0
    for axis_at, shards_of in cuts:
        heights = jax.random.uniform(jax.random.fold_in(jax.random.fold_in(key, 6), axis_at), (shards_of,), jnp.float32, least / len(cuts), high / len(cuts))
        level = level * jnp.repeat(jnp.exp(heights), extent[axis_at] // shards_of).reshape((-1,) + (1,) * (len(extent) - 1 - axis_at))
    return level


def bell_draw(own_key, extent, scale, reach, pieces=(), kind=jnp.bfloat16):
    level = levels(own_key, extent, pieces, -0.22, 0.18) if pieces else 1.0
    values = jax.random.normal(own_key, extent, jnp.float32) * scale * level
    return jnp.minimum(jnp.maximum(values, -reach), reach).astype(kind)


def setup_inputs(seed: int = 0) -> dict:
    arg_keys = jax.random.split(jax.random.key(seed), 8)
    return {
        "velocity": bell_draw(arg_keys[0], (NY, NZ, 3, NX), 1.0, 6.0, ((0, 16), (1, 16)), jnp.float32),
        "viscosity": jnp.clip(jnp.exp(math.log(2.0) - 1.3862944 * jax.random.uniform(arg_keys[1], (NY, NZ, NX), jnp.float32) ** levels(arg_keys[1], (NY, NZ, NX), ((0, 16), (1, 16)), -0.2, 0.2)), 0.5, 2.0),
        "implicit_inverse": bell_draw(arg_keys[2], (NY, NY), NY ** -0.5, 0.1875, (), jnp.float32),
        "row_index": draw_row_index(jax.random.fold_in(arg_keys[7], 71), 0),
        "row_counts": draw_row_counts(jax.random.fold_in(arg_keys[7], 71), 0),
        "weight_in": bell_draw(arg_keys[5], (MEMBERS, IN, HID), IN ** -0.5, 0.21875, ((0, 32),)),
        "weight_out": bell_draw(arg_keys[6], (MEMBERS, HID, IN), HID ** -0.5, 0.1875, ((0, 32),)),
    }


diffusion_factor = 0.08

def laplace(current):
    padded = jnp.pad(current, ((1, 1), (0, 0), (0, 0), (0, 0)))
    neighbours = padded[2:] + padded[:-2]
    neighbours = neighbours + jnp.roll(current, 1, 1) + jnp.roll(current, -1, 1)
    neighbours = neighbours + jnp.roll(current, 1, 3) + jnp.roll(current, -1, 3)
    return neighbours - 6.0 * current

def substep(current, viscosity, implicit_inverse):
    explicit = current + diffusion_factor * viscosity[:, :, None, :] * laplace(current)
    mixed_cols = jnp.dot(implicit_inverse, explicit.reshape(NY, -1), precision=lax.Precision.HIGHEST, preferred_element_type=jnp.float32)
    return mixed_cols.reshape(current.shape)

def reference(velocity, viscosity, implicit_inverse, row_index, row_counts, weight_in, weight_out):
    after_one = substep(velocity, viscosity, implicit_inverse)
    after_two = substep(after_one, viscosity, implicit_inverse)
    plane_index = jnp.arange(N_PZ, dtype=jnp.int32)[None, :, None, None, None]
    span_index = jnp.arange(N_PX, dtype=jnp.int32)[:, None, None, None, None] * N_TR + jnp.arange(N_TR, dtype=jnp.int32)[None, None, :, None, None]
    wall_row = plane_index * YL + row_index // ZL
    span_row = span_index * ZL + row_index % ZL
    table_index = (wall_row * NZ + span_row).reshape(-1).astype(jnp.int32)
    live_slot = (jnp.arange(CAP, dtype=jnp.int32)[None, None, None, None, :] < row_counts[..., None]).reshape(-1, 1)
    inputs = jnp.where(live_slot, jnp.take(after_one.reshape(NY * NZ, IN), table_index, axis=0), 0.0).astype(jnp.bfloat16)
    targets = jnp.where(live_slot, jnp.take(after_two.reshape(NY * NZ, IN), table_index, axis=0), 0.0).astype(jnp.bfloat16)
    inputs = inputs.reshape(N_PX, N_PZ * N_TR, MEMBERS, CAP, IN).transpose(2, 0, 1, 3, 4).reshape(MEMBERS, N_PX, SLOTS_DEV, IN)
    targets = targets.reshape(N_PX, N_PZ * N_TR, MEMBERS, CAP, IN).transpose(2, 0, 1, 3, 4).reshape(MEMBERS, N_PX, SLOTS_DEV, IN)
    loss_scale = 1.0 / math.sqrt(N_PX * SLOTS_DEV)

    def member_grads(member_args):
        batches_in, batches_target, member_in, member_out = member_args

        def device_part(batch_pair):
            batch_in, batch_target = batch_pair
            preact = jnp.dot(batch_in, member_in, preferred_element_type=jnp.float32)
            logistic = jax.nn.sigmoid(preact)
            hidden = (preact * logistic).astype(jnp.bfloat16)
            predicted = jnp.dot(hidden, member_out, preferred_element_type=jnp.float32)
            delta_out = ((predicted - batch_target.astype(jnp.float32)) * loss_scale).astype(jnp.bfloat16)
            back_hidden = jnp.dot(delta_out, member_out.T, preferred_element_type=jnp.float32)
            delta_in = (back_hidden * logistic * (1.0 + preact * (1.0 - logistic))).astype(jnp.bfloat16)
            part_in = jnp.dot(batch_in.T, delta_in, preferred_element_type=jnp.float32).astype(jnp.bfloat16)
            part_out = jnp.dot(hidden.T, delta_out, preferred_element_type=jnp.float32).astype(jnp.bfloat16)
            return lax.optimization_barrier((part_in, part_out))
        parts_in, parts_out = lax.map(device_part, (batches_in, batches_target))
        return (lax.optimization_barrier(jnp.sum(parts_in.astype(jnp.float32), axis=0)), lax.optimization_barrier(jnp.sum(parts_out.astype(jnp.float32), axis=0)))
    grad_in, grad_out = lax.map(member_grads, (inputs, targets, weight_in, weight_out))
    return (after_two, grad_in, grad_out)
```

```python
import math

import jax
import jax.numpy as jnp
from jax import lax
from jax.experimental import pallas as pl
from jax.experimental.pallas import tpu as pltpu
from jax.sharding import PartitionSpec as P

diffusion_factor = 0.08
F32 = jnp.float32
BF16 = jnp.bfloat16
MIB = 1 << 20


def call(kernel, out_shape, args, scratch=(), flops=1e6, vmem=48):
    outs = jax.tree.leaves(out_shape)
    moved = sum(math.prod(x.shape) * x.dtype.itemsize for x in list(args) + outs)
    return pl.pallas_call(
        kernel,
        out_shape=out_shape,
        in_specs=[pl.BlockSpec(memory_space=pltpu.VMEM)] * len(args),
        out_specs=jax.tree.map(lambda _: pl.BlockSpec(memory_space=pltpu.VMEM), out_shape),
        scratch_shapes=list(scratch),
        compiler_params=pltpu.CompilerParams(vmem_limit_bytes=vmem * MIB),
        cost_estimate=pl.CostEstimate(
            flops=int(flops), bytes_accessed=int(moved), transcendentals=0
        ),
    )(*args)


def shaped(shape, dtype):
    return jax.ShapeDtypeStruct(shape, dtype)


def shift(array, axis, wrap=True):
    last, first = array
    size = lax.axis_size(axis)
    up = [(i, (i + 1) % size) for i in range(size if wrap else size - 1)]
    down = [(j, i) for i, j in up]
    return lax.ppermute(last, axis, up), lax.ppermute(first, axis, down)


def explicit_kernel(v, w, zlo, zhi, ylo, yhi, out):
    comps, zn, yn, xn = v.shape
    peers = out.shape[0]
    xl = xn // peers
    row = lax.broadcasted_iota(jnp.int32, (yn, xn), 0)
    y_before = ylo[...].astype(F32)
    y_after = yhi[...].astype(F32)
    half = (comps + 1) * xl
    for zh in range(zn // 2):
        for c in range(comps + 1):
            pair = []
            for z in (2 * zh, 2 * zh + 1):
                if c == comps:
                    pair.append(w[z])
                    continue
                cur = v[c, z]
                r = c * zn + z
                total = v[c, z - 1] if z > 0 else zlo[c].astype(F32)
                total = total + (v[c, z + 1] if z < zn - 1 else zhi[c].astype(F32))
                total = total + jnp.where(row == 0, y_before[r : r + 1], pltpu.roll(cur, 1, 0))
                total = total + jnp.where(
                    row == yn - 1, y_after[r : r + 1], pltpu.roll(cur, yn - 1, 0)
                )
                total = total + pltpu.roll(cur, 1, 1) + pltpu.roll(cur, xn - 1, 1)
                pair.append(cur + diffusion_factor * w[z] * (total - 6.0 * cur))
            turned = jnp.concatenate(pair, axis=0).T.astype(BF16)
            base = zh * half + c * xl
            for q in range(peers):
                out[q, base : base + xl, :] = turned[q * xl : (q + 1) * xl]


def solve(e, a):
    return lax.dot_general(
        e[...], a[...], (((1,), (1,)), ((), ())), preferred_element_type=F32
    )


def pack_columns(u, packed, zn):
    peers, rows, lanes = packed.shape
    f = rows // (zn // 2)
    yn = lanes // 2
    low = lax.broadcasted_iota(jnp.int32, (f, lanes), 1) < yn
    for j in range(peers // 2):
        for zh in range(zn // 2):
            first = u[(2 * zh) * f : (2 * zh + 1) * f, j * lanes : (j + 1) * lanes]
            second = u[(2 * zh + 1) * f : (2 * zh + 2) * f, j * lanes : (j + 1) * lanes]
            even = jnp.where(low, first, pltpu.roll(second, yn, 1))
            odd = jnp.where(low, pltpu.roll(first, yn, 1), second)
            packed[2 * j, zh * f : (zh + 1) * f, :] = even.astype(BF16)
            packed[2 * j + 1, zh * f : (zh + 1) * f, :] = odd.astype(BF16)


def first_solve_kernel(got, a, u, w, packed, zlo, zhi, xlo, xhi, e):
    peers, rows, lanes = got.shape
    yn = lanes // 2
    zn = 4
    half = rows // 2
    xl = w.shape[0] // zn
    f = half - xl
    low = lax.broadcasted_iota(jnp.int32, (rows, lanes), 1) < yn
    for j in range(peers // 2):
        one = got[2 * j].astype(F32)
        two = got[2 * j + 1].astype(F32)
        sides = (
            jnp.where(low, one, pltpu.roll(two, yn, 1)),
            jnp.where(low, pltpu.roll(one, yn, 1), two),
        )
        at = slice(j * lanes, (j + 1) * lanes)
        for zh in range(zn // 2):
            for side in range(2):
                z = 2 * zh + side
                e[z * f : (z + 1) * f, at] = sides[side][zh * half : zh * half + f].astype(BF16)
                w[z * xl : (z + 1) * xl, at] = sides[side][zh * half + f : (zh + 1) * half]
    u[...] = solve(e, a)
    zlo[...] = u[0:f].astype(BF16)
    zhi[...] = u[(zn - 1) * f : zn * f].astype(BF16)
    groups = u.shape[0] // xl
    xlo[...] = jnp.concatenate([u[r * xl : r * xl + 1] for r in range(groups)], axis=0).astype(BF16)
    xhi[...] = jnp.concatenate(
        [u[(r + 1) * xl - 1 : (r + 1) * xl] for r in range(groups)], axis=0
    ).astype(BF16)
    pack_columns(u, packed, zn)


def second_solve_kernel(u, w, zlo, zhi, xlo, xhi, a, packed, e, out):
    cols = u.shape[1]
    f = zlo.shape[0]
    zn = u.shape[0] // f
    xl = w.shape[0] // zn
    comps = f // xl
    row = lax.broadcasted_iota(jnp.int32, (xl, cols), 0)
    lane = lax.broadcasted_iota(jnp.int32, (xl, cols), 1)
    x_before = xlo[...].astype(F32)
    x_after = xhi[...].astype(F32)
    for z in range(zn):
        for c in range(comps):
            r = z * comps + c
            at = slice(r * xl, (r + 1) * xl)
            cur = u[at]
            if z > 0:
                total = u[(r - comps) * xl : (r - comps + 1) * xl]
            else:
                total = zlo[c * xl : (c + 1) * xl].astype(F32)
            if z < zn - 1:
                total = total + u[(r + comps) * xl : (r + comps + 1) * xl]
            else:
                total = total + zhi[c * xl : (c + 1) * xl].astype(F32)
            total = total + jnp.where(row == 0, x_before[r : r + 1], pltpu.roll(cur, 1, 0))
            total = total + jnp.where(row == xl - 1, x_after[r : r + 1], pltpu.roll(cur, xl - 1, 0))
            total = total + jnp.where(lane == 0, 0.0, pltpu.roll(cur, 1, 1))
            total = total + jnp.where(lane == cols - 1, 0.0, pltpu.roll(cur, cols - 1, 1))
            step = diffusion_factor * w[z * xl : (z + 1) * xl] * (total - 6.0 * cur)
            e[at] = (cur + step).astype(BF16)
    out[...] = solve(e, a)
    pack_columns(out, packed, zn)


GROUP = 8


def sample_kernel(packed, ids, out, picked):
    peers, rows, lanes = packed.shape
    f = rows // 2
    yn = lanes // 2
    blocks = picked.shape[2] // lanes
    r = lax.broadcasted_iota(jnp.int32, (2 * lanes, lanes), 0)
    row_id = (r % yn) * 4 + r // yn
    for q in range(peers):
        table = jnp.concatenate([packed[q, 0:f], packed[q, f:rows]], axis=1)
        wanted = pltpu.roll(ids[q], (GROUP * q) % lanes, 1) if q else ids[q]
        for b in range(blocks):
            hot = jnp.where(row_id == wanted[b : b + 1], 1.0, 0.0).astype(BF16)
            picked[q, :, b * lanes : (b + 1) * lanes] = jnp.dot(
                table, hot, preferred_element_type=F32
            )
    group = lax.broadcasted_iota(jnp.int32, (f, lanes), 1) // GROUP
    per = lanes // GROUP
    halves = out.shape[0] // per
    for b in range(blocks):
        kg, mh = b // halves, b % halves
        held = [picked[q, :, b * lanes : (b + 1) * lanes] for q in range(peers)]
        step = 1
        while step < peers:
            take = (group // step) % 2 == 1
            held = [jnp.where(take, held[(i + step) % peers], held[i]) for i in range(peers)]
            step *= 2
        for ml in range(per):
            out[mh * per + ml, :, kg * lanes : (kg + 1) * lanes] = held[(-ml) % peers].astype(BF16)


def slot_table(row_index, row_counts):
    members, slots = row_index.shape[3:]
    index = row_index.reshape(members, slots)
    counts = row_counts.reshape(members, 1)
    live = jnp.arange(slots, dtype=jnp.int32)[None, :] < counts
    index = jnp.where(live, index, -1)
    per = 128 // GROUP
    index = index.reshape(members // per, per, slots // GROUP, GROUP).transpose(2, 0, 1, 3)
    index = index.reshape(-1, 128)
    index = jnp.concatenate([index, jnp.full((8 - index.shape[0], 128), -1, jnp.int32)], axis=0)
    return lax.all_gather(index, "pz")


def gather_rows(got, turned, comps=3):
    sources, f, slots = got.shape
    sides = 2
    peers = sources // sides
    xl = f // comps
    for q in range(peers):
        for side in range(sides):
            for c in range(comps):
                at = (c * peers + q) * xl
                turned[at : at + xl, side * slots : (side + 1) * slots] = got[
                    q * sides + side, c * xl : (c + 1) * xl
                ]


def forward_kernel(got, w_in, w_out, x_out, hidden, slope, predicted, x):
    gather_rows(got, x)
    x_out[...] = x[...]
    wide = 256
    count = hidden.shape[0] // wide

    def chunk(i, carry):
        at = pl.ds(pl.multiple_of(i * wide, wide), wide)
        pre = jnp.dot(w_in[at, :], x[...], preferred_element_type=F32)
        logistic = jax.nn.sigmoid(pre)
        hidden[at, :] = (pre * logistic).astype(BF16)
        slope[at, :] = (logistic * (1.0 + pre * (1.0 - logistic))).astype(slope.dtype)
        return carry

    lax.fori_loop(0, count, chunk, 0)

    def second(i, carry):
        at = pl.ds(pl.multiple_of(i * wide, wide), wide)
        predicted[at, :] = jnp.dot(w_out[at, :], hidden[...], preferred_element_type=F32)
        return carry

    lax.fori_loop(0, predicted.shape[0] // wide, second, 0)


def backward_kernel(scale, got, predicted, hidden, slope, x, w_out, part_out, part_in, d, din):
    wide = 256
    gather_rows(got, d)
    d[...] = ((predicted[...] - d[...].astype(F32)) * scale).astype(BF16)
    contract_rows = (((1,), (1,)), ((), ()))

    def first(i, carry):
        at = pl.ds(pl.multiple_of(i * wide, wide), wide)
        part_out[at, :] = lax.dot_general(
            hidden[at, :], d[...], contract_rows, preferred_element_type=F32
        ).astype(BF16)
        back = jnp.dot(w_out[at, :], d[...], preferred_element_type=F32)
        din[at, :] = (back * slope[at, :].astype(F32)).astype(BF16)
        return carry

    lax.fori_loop(0, hidden.shape[0] // wide, first, 0)

    def second(i, carry):
        at = pl.ds(pl.multiple_of(i * wide, wide), wide)
        part_in[at, :] = lax.dot_general(
            x[at, :], din[...], contract_rows, preferred_element_type=F32
        ).astype(BF16)
        return carry

    lax.fori_loop(0, x.shape[0] // wide, second, 0)


def planes_kernel(got, out):
    comps, zn, yn, xn = out.shape
    peers = got.shape[0]
    xl = xn // peers
    f = comps * xl
    for zh in range(zn // 2):
        for c in range(comps):
            base = zh * f + c * xl
            block = jnp.concatenate(
                [got[q, base : base + xl, :] for q in range(peers)], axis=0
            ).astype(F32)
            turned = block.T
            out[c, 2 * zh] = turned[0:yn]
            out[c, 2 * zh + 1] = turned[yn : 2 * yn]


def exchange(array, axis):
    return lax.all_to_all(array, axis, split_axis=0, concat_axis=0, tiled=True)


def sum_shares(part, axis):
    size = lax.axis_size(axis)
    shares = exchange(part.reshape(size, part.shape[0] // size, part.shape[1]), axis)
    return jnp.sum(shares.astype(F32), axis=0)


def per_device(velocity, viscosity, implicit_inverse, row_index, row_counts, weight_in, weight_out):
    yn, zn, comps, xn = velocity.shape
    peers = lax.axis_size("pz")
    total_y = yn * peers
    xl = xn // peers
    f = comps * xl
    lanes = 2 * yn
    members, slots = row_index.shape[3:]

    v = velocity.transpose(2, 1, 0, 3)
    edges = velocity.astype(BF16)
    z_edge = lambda z: edges[:, z].transpose(1, 0, 2)
    y_edge = lambda y: edges[y].transpose(1, 0, 2).reshape(comps * zn, xn)
    zlo, zhi = shift((z_edge(zn - 1), z_edge(0)), ("px", "tr"))
    ylo, yhi = shift((y_edge(yn - 1), y_edge(0)), "pz", wrap=False)
    sent = call(
        explicit_kernel,
        shaped((peers, 2 * (f + xl), lanes), BF16),
        (v, viscosity.transpose(1, 0, 2), zlo, zhi, ylo, yhi),
        flops=2e7,
    )
    ids = slot_table(row_index, row_counts)
    inverse = implicit_inverse.astype(BF16)
    got = exchange(sent, "pz")
    solve_flops = 2 * zn * f * total_y * total_y
    u, w, packed, zlo, zhi, xlo, xhi = call(
        first_solve_kernel,
        (
            shaped((zn * f, total_y), F32),
            shaped((zn * xl, total_y), F32),
            shaped((peers, 2 * f, lanes), BF16),
            shaped((f, total_y), BF16),
            shaped((f, total_y), BF16),
            shaped((zn * comps, total_y), BF16),
            shaped((zn * comps, total_y), BF16),
        ),
        (got, inverse),
        scratch=[pltpu.VMEM((zn * f, total_y), BF16)],
        flops=solve_flops,
    )
    zlo, zhi = shift((zhi, zlo), ("px", "tr"))
    xlo, xhi = shift((xhi, xlo), "pz")

    def sample(packed):
        sent = call(
            sample_kernel,
            shaped((members, f, peers * slots), BF16),
            (packed, ids),
            scratch=[pltpu.VMEM((peers, f, members * slots), F32)],
            flops=2 * peers * 256 * 256 * members * slots,
        )
        return exchange(sent, ("pz", "tr"))

    rows_in = sample(packed)
    packed = call(
        second_solve_kernel,
        shaped((peers, 2 * f, lanes), BF16),
        (u, w, zlo, zhi, xlo, xhi, inverse),
        scratch=[pltpu.VMEM((zn * f, total_y), BF16), pltpu.VMEM((zn * f, total_y), F32)],
        flops=solve_flops,
    )
    rows_target = sample(packed)
    planes = exchange(packed, "pz")

    member_in = weight_in[0]
    member_out = weight_out[0]
    width, hid = member_in.shape
    batch = 2 * peers * slots
    loss_scale = 1.0 / math.sqrt(lax.axis_size("px") * batch)
    x, hidden, slope, predicted = call(
        forward_kernel,
        (
            shaped((width, batch), BF16),
            shaped((hid, batch), BF16),
            shaped((hid, batch), F32),
            shaped((width, batch), F32),
        ),
        (rows_in, member_in.T, member_out.T),
        scratch=[pltpu.VMEM((width, batch), BF16)],
        flops=4 * hid * width * batch,
    )

    def backward(*refs):
        backward_kernel(loss_scale, *refs)

    part_out, part_in = call(
        backward,
        (shaped((hid, width), BF16), shaped((width, hid), BF16)),
        (rows_target, predicted, hidden, slope, x, member_out),
        scratch=[pltpu.VMEM((width, batch), BF16), pltpu.VMEM((hid, batch), BF16)],
        flops=6 * hid * width * batch,
    )
    share_out = sum_shares(part_out, "px")
    share_in = sum_shares(part_in, "px")
    result = call(planes_kernel, shaped((comps, zn, yn, xn), F32), (planes,), flops=1e6)
    return (result.transpose(2, 1, 0, 3), share_in[None], share_out[None])


def solution(mesh):
    in_specs = (
        P("pz", ("px", "tr"), None, None),
        P("pz", ("px", "tr"), None),
        P(),
        P("px", "pz", "tr", None, None),
        P("px", "pz", "tr", None),
        P(("pz", "tr"), None, None),
        P(("pz", "tr"), None, None),
    )
    out_specs = (
        P("pz", ("px", "tr"), None, None),
        P(("pz", "tr"), "px", None),
        P(("pz", "tr"), "px", None),
    )
    return jax.shard_map(
        per_device, mesh=mesh, in_specs=in_specs, out_specs=out_specs, check_vma=False
    )
```

```python
import math

import jax
import jax.numpy as jnp
from jax import lax
from jax.experimental import pallas as pl
from jax.experimental.pallas import tpu as pltpu
from jax.sharding import PartitionSpec as P

diffusion_factor = 0.08
F32 = jnp.float32
BF16 = jnp.bfloat16
MIB = 1 << 20


def call(kernel, out_shape, args, scratch=(), flops=1e6):
    outs = jax.tree.leaves(out_shape)
    size = lambda x: math.prod(x.shape) * x.dtype.itemsize
    moved = sum(size(x) for x in list(args) + outs)
    held = moved + sum(math.prod(x.shape) * jnp.dtype(x.dtype).itemsize for x in scratch)
    scalars = lambda x: x.ndim == 1
    return pl.pallas_call(
        kernel,
        out_shape=out_shape,
        in_specs=[
            pl.BlockSpec(memory_space=pltpu.SMEM if scalars(x) else pltpu.VMEM) for x in args
        ],
        out_specs=jax.tree.map(lambda _: pl.BlockSpec(memory_space=pltpu.VMEM), out_shape),
        scratch_shapes=list(scratch),
        compiler_params=pltpu.CompilerParams(vmem_limit_bytes=held + 6 * MIB),
        cost_estimate=pl.CostEstimate(
            flops=int(flops), bytes_accessed=int(moved), transcendentals=0
        ),
    )(*args)


def shaped(shape, dtype):
    return jax.ShapeDtypeStruct(shape, dtype)


def shift(array, axis, wrap=True):
    last, first = array
    size = lax.axis_size(axis)
    up = [(i, (i + 1) % size) for i in range(size if wrap else size - 1)]
    down = [(j, i) for i, j in up]
    return lax.ppermute(last, axis, up), lax.ppermute(first, axis, down)


def explicit_kernel(v, w, zlo, zhi, ylo, yhi, ids, out):
    comps, zn, yn, xn = v.shape
    peers = out.shape[0]
    xl = xn // peers
    row = lax.broadcasted_iota(jnp.int32, (yn, xn), 0)
    y_before = ylo[...].astype(F32)
    y_after = yhi[...].astype(F32)
    half = (comps + 1) * xl
    for zh in range(zn // 2):
        for c in range(comps + 1):
            pair = []
            for z in (2 * zh, 2 * zh + 1):
                if c == comps:
                    pair.append(w[z])
                    continue
                cur = v[c, z]
                r = c * zn + z
                total = v[c, z - 1] if z > 0 else zlo[c].astype(F32)
                total = total + (v[c, z + 1] if z < zn - 1 else zhi[c].astype(F32))
                total = total + jnp.where(row == 0, y_before[r : r + 1], pltpu.roll(cur, 1, 0))
                total = total + jnp.where(
                    row == yn - 1, y_after[r : r + 1], pltpu.roll(cur, yn - 1, 0)
                )
                total = total + pltpu.roll(cur, 1, 1) + pltpu.roll(cur, xn - 1, 1)
                pair.append(cur + diffusion_factor * w[z] * (total - 6.0 * cur))
            turned = jnp.concatenate(pair, axis=0).T.astype(BF16)
            base = zh * half + c * xl
            for q in range(peers):
                out[q, base : base + xl, :] = turned[q * xl : (q + 1) * xl]
    numbers = ids[...].astype(F32).astype(BF16)
    for q in range(peers):
        out[q, (zn // 2) * half : (zn // 2) * half + ids.shape[0], :] = numbers


def solve(e, a):
    return lax.dot_general(
        e[...], a[...], (((1,), (1,)), ((), ())), preferred_element_type=F32
    )


def pack_columns(u, packed, zn):
    peers, rows, lanes = packed.shape
    f = rows // (zn // 2)
    yn = lanes // 2
    low = lax.broadcasted_iota(jnp.int32, (f, lanes), 1) < yn
    for j in range(peers // 2):
        for zh in range(zn // 2):
            first = u[(2 * zh) * f : (2 * zh + 1) * f, j * lanes : (j + 1) * lanes]
            second = u[(2 * zh + 1) * f : (2 * zh + 2) * f, j * lanes : (j + 1) * lanes]
            even = jnp.where(low, first, pltpu.roll(second, yn, 1))
            odd = jnp.where(low, pltpu.roll(first, yn, 1), second)
            packed[2 * j, zh * f : (zh + 1) * f, :] = even.astype(BF16)
            packed[2 * j + 1, zh * f : (zh + 1) * f, :] = odd.astype(BF16)


def first_solve_kernel(got, a, u, w, packed, zlo, zhi, xlo, xhi, ids, e):
    peers, rows, lanes = got.shape
    rows = rows - ids.shape[1]
    ids[...] = got[:, rows:, :].astype(F32).astype(jnp.int32)
    yn = lanes // 2
    zn = 4
    half = rows // 2
    xl = w.shape[0] // zn
    f = half - xl
    low = lax.broadcasted_iota(jnp.int32, (rows, lanes), 1) < yn
    for j in range(peers // 2):
        one = got[2 * j, 0:rows].astype(F32)
        two = got[2 * j + 1, 0:rows].astype(F32)
        sides = (
            jnp.where(low, one, pltpu.roll(two, yn, 1)),
            jnp.where(low, pltpu.roll(one, yn, 1), two),
        )
        at = slice(j * lanes, (j + 1) * lanes)
        for zh in range(zn // 2):
            for side in range(2):
                z = 2 * zh + side
                e[z * f : (z + 1) * f, at] = sides[side][zh * half : zh * half + f].astype(BF16)
                w[z * xl : (z + 1) * xl, at] = sides[side][zh * half + f : (zh + 1) * half]
    u[...] = solve(e, a)
    zlo[...] = u[0:f].astype(BF16)
    zhi[...] = u[(zn - 1) * f : zn * f].astype(BF16)
    groups = u.shape[0] // xl
    xlo[...] = jnp.concatenate([u[r * xl : r * xl + 1] for r in range(groups)], axis=0).astype(BF16)
    xhi[...] = jnp.concatenate(
        [u[(r + 1) * xl - 1 : (r + 1) * xl] for r in range(groups)], axis=0
    ).astype(BF16)
    pack_columns(u, packed, zn)


def second_solve_kernel(u, w, zlo, zhi, xlo, xhi, a, packed, e, out):
    cols = u.shape[1]
    f = zlo.shape[0]
    zn = u.shape[0] // f
    xl = w.shape[0] // zn
    comps = f // xl
    row = lax.broadcasted_iota(jnp.int32, (xl, cols), 0)
    lane = lax.broadcasted_iota(jnp.int32, (xl, cols), 1)
    x_before = xlo[...].astype(F32)
    x_after = xhi[...].astype(F32)
    for z in range(zn):
        for c in range(comps):
            r = z * comps + c
            at = slice(r * xl, (r + 1) * xl)
            cur = u[at]
            if z > 0:
                total = u[(r - comps) * xl : (r - comps + 1) * xl]
            else:
                total = zlo[c * xl : (c + 1) * xl].astype(F32)
            if z < zn - 1:
                total = total + u[(r + comps) * xl : (r + comps + 1) * xl]
            else:
                total = total + zhi[c * xl : (c + 1) * xl].astype(F32)
            total = total + jnp.where(row == 0, x_before[r : r + 1], pltpu.roll(cur, 1, 0))
            total = total + jnp.where(row == xl - 1, x_after[r : r + 1], pltpu.roll(cur, xl - 1, 0))
            total = total + jnp.where(lane == 0, 0.0, pltpu.roll(cur, 1, 1))
            total = total + jnp.where(lane == cols - 1, 0.0, pltpu.roll(cur, cols - 1, 1))
            step = diffusion_factor * w[z * xl : (z + 1) * xl] * (total - 6.0 * cur)
            e[at] = (cur + step).astype(BF16)
    out[...] = solve(e, a)
    pack_columns(out, packed, zn)


GROUP = 8


def sample_kernel(packed, ids, out, picked):
    peers, rows, lanes = packed.shape
    f = rows // 2
    yn = lanes // 2
    blocks = picked.shape[2] // lanes
    r = lax.broadcasted_iota(jnp.int32, (2 * lanes, lanes), 0)
    row_id = (r % yn) * 4 + r // yn
    for q in range(peers):
        table = jnp.concatenate([packed[q, 0:f], packed[q, f:rows]], axis=1)
        wanted = pltpu.roll(ids[q], (GROUP * q) % lanes, 1) if q else ids[q]
        for b in range(blocks):
            hot = jnp.where(row_id == wanted[b : b + 1], 1.0, 0.0).astype(BF16)
            picked[q, :, b * lanes : (b + 1) * lanes] = jnp.dot(
                table, hot, preferred_element_type=F32
            )
    group = lax.broadcasted_iota(jnp.int32, (f, lanes), 1) // GROUP
    per = lanes // GROUP
    halves = out.shape[0] // per
    for b in range(blocks):
        kg, mh = b // halves, b % halves
        held = [picked[q, :, b * lanes : (b + 1) * lanes] for q in range(peers)]
        step = 1
        while step < peers:
            take = (group // step) % 2 == 1
            held = [jnp.where(take, held[(i + step) % peers], held[i]) for i in range(peers)]
            step *= 2
        for ml in range(per):
            out[mh * per + ml, :, kg * lanes : (kg + 1) * lanes] = held[(-ml) % peers].astype(BF16)


def slot_table(row_index, row_counts):
    members, slots = row_index.shape[3:]
    index = row_index.reshape(members, slots)
    counts = row_counts.reshape(members, 1)
    live = jnp.arange(slots, dtype=jnp.int32)[None, :] < counts
    index = jnp.where(live, index, -1)
    per = 128 // GROUP
    index = index.reshape(members // per, per, slots // GROUP, GROUP).transpose(2, 0, 1, 3)
    index = index.reshape(-1, 128)
    fill = jnp.full((8 - index.shape[0], 128), -1, jnp.int32)
    return jnp.concatenate([index, fill], axis=0)


def gather_rows(got, turned, comps=3):
    sources, f, slots = got.shape
    sides = 2
    peers = sources // sides
    xl = f // comps
    for q in range(peers):
        for side in range(sides):
            for c in range(comps):
                at = (c * peers + q) * xl
                turned[at : at + xl, side * slots : (side + 1) * slots] = got[
                    q * sides + side, c * xl : (c + 1) * xl
                ]


CONTRACT_ROWS = (((1,), (1,)), ((), ()))


def over_rows(left, right):
    return lax.dot_general(left, right, CONTRACT_ROWS, preferred_element_type=F32)


def forward_kernel(got, w_in, w_out, x, hidden, slope, predicted):
    gather_rows(got, x)
    wide = 256

    def chunk(i, carry):
        at = pl.ds(pl.multiple_of(i * wide, wide), wide)
        pre = jnp.dot(w_in[at, :], x[...], preferred_element_type=F32)
        logistic = jax.nn.sigmoid(pre)
        hidden[at, :] = (pre * logistic).astype(BF16)
        slope[at, :] = (logistic * (1.0 + pre * (1.0 - logistic))).astype(slope.dtype)
        return carry

    lax.fori_loop(0, hidden.shape[0] // wide, chunk, 0)

    def second(i, carry):
        at = pl.ds(pl.multiple_of(i * wide, wide), wide)
        predicted[at, :] = jnp.dot(w_out[at, :], hidden[...], preferred_element_type=F32)
        return carry

    lax.fori_loop(0, predicted.shape[0] // wide, second, 0)


def block_rows(array, y, core, rows):
    return array[pl.ds(pl.multiple_of((2 * y + core) * rows, rows), rows), :]


def away_blocks(array, right, core, away, rows):
    for pair in range(away.shape[0] // (2 * rows)):
        left = jnp.concatenate(
            [block_rows(array, 2 * pair + k, 1 - core, rows) for k in range(2)], axis=0
        )
        away[2 * pair * rows : 2 * (pair + 1) * rows] = over_rows(left, right[...]).astype(BF16)


def delta_out_kernel(scale, place, got, predicted, hidden, d, away):
    gather_rows(got, d)
    d[...] = ((predicted[...] - d[...].astype(F32)) * scale).astype(BF16)
    away_blocks(hidden, d, place[0], away, away.shape[0] // 4)


def delta_in_kernel(place, d, slope, w_out, x, din, away):
    wide = 256

    def chunk(i, carry):
        at = pl.ds(pl.multiple_of(i * wide, wide), wide)
        back = jnp.dot(w_out[at, :], d[...], preferred_element_type=F32)
        din[at, :] = (back * slope[at, :].astype(F32)).astype(BF16)
        return carry

    lax.fori_loop(0, din.shape[0] // wide, chunk, 0)
    away_blocks(x, din, place[0], away, away.shape[0] // 4)


def fold(block, rows, width):
    extra = rows - block.shape[0]
    pieces = [
        block[g * extra : (g + 1) * extra, width:] for g in range(block.shape[0] // extra)
    ]
    return jnp.concatenate([block[:, :width], jnp.concatenate(pieces, axis=1)], axis=0)


def unfold(block, rows):
    extra = block.shape[0] - rows
    count = rows // extra
    wide = block.shape[1] // count
    pieces = [block[rows:, g * wide : (g + 1) * wide] for g in range(count)]
    return jnp.concatenate([block[:rows], jnp.concatenate(pieces, axis=0)], axis=1)


def keep_kernel(place, hidden, d, x, din, got_out, got_in, own, plus, minus, top, bottom):
    core, y = place[0], place[1]
    rows, width = own.shape[1:]
    half = rows // 2

    def put(which, k, block):
        if k == 0:
            own[which] = block
        elif k == 1:
            plus[which] = block.astype(BF16)
        elif k == 3:
            minus[which] = block.astype(BF16)
        else:
            top[which] = block[:half].astype(BF16)
            bottom[which] = block[half:].astype(BF16)

    for which, (left, right, got) in enumerate(((hidden, d, got_out), (x, din, got_in))):
        size = got.shape[0] // 4
        for ks in ((2, 1), (3, 0)):
            ys = [lax.rem(y + k, 4) for k in ks]
            blocks = jnp.concatenate([block_rows(left, at, core, size) for at in ys], axis=0)
            value = over_rows(blocks, right[...])
            for n, (k, at) in enumerate(zip(ks, ys)):
                block = value[n * size : (n + 1) * size]
                block = block + got[pl.ds(pl.multiple_of(at * size, size), size), :].astype(F32)
                put(which, k, block if which == 0 else fold(block, rows, width))


def relay_kernel(plus, minus, from_before, from_after, plus_out, minus_out):
    half = from_before.shape[1]
    for which in range(plus.shape[0]):
        plus_out[which, :half] = (
            plus[which, :half].astype(F32) + from_before[which].astype(F32)
        ).astype(BF16)
        plus_out[which, half:] = plus[which, half:]
        minus_out[which, :half] = minus[which, :half]
        minus_out[which, half:] = (
            minus[which, half:].astype(F32) + from_after[which].astype(F32)
        ).astype(BF16)


def finish_kernel(own, from_before, from_after, share_out, share_in):
    total = [
        own[k] + from_before[k].astype(F32) + from_after[k].astype(F32) for k in range(2)
    ]
    share_out[...] = total[0]
    share_in[...] = unfold(total[1], share_in.shape[0])


def planes_kernel(got, out):
    comps, zn, yn, xn = out.shape
    peers = got.shape[0]
    xl = xn // peers
    f = comps * xl
    for zh in range(zn // 2):
        for c in range(comps):
            base = zh * f + c * xl
            block = jnp.concatenate(
                [got[q, base : base + xl, :] for q in range(peers)], axis=0
            ).astype(F32)
            turned = block.T
            out[c, 2 * zh] = turned[0:yn]
            out[c, 2 * zh + 1] = turned[yn : 2 * yn]


def exchange(array, axis):
    return lax.all_to_all(array, axis, split_axis=0, concat_axis=0, tiled=True)


def swap_cores(array):
    size = lax.axis_size("px")
    return lax.ppermute(array, "px", [(i, i ^ 1) for i in range(size)])


def shift_chips(forward, backward):
    size = lax.axis_size("px")
    up = [(i, (i + 2) % size) for i in range(size)]
    down = [(j, i) for i, j in up]
    return lax.ppermute(forward, "px", up), lax.ppermute(backward, "px", down)


def per_device(velocity, viscosity, implicit_inverse, row_index, row_counts, weight_in, weight_out):
    yn, zn, comps, xn = velocity.shape
    peers = lax.axis_size("pz")
    total_y = yn * peers
    xl = xn // peers
    f = comps * xl
    lanes = 2 * yn
    members, slots = row_index.shape[3:]

    v = velocity.transpose(2, 1, 0, 3)
    edges = velocity.astype(BF16)
    z_edge = lambda z: edges[:, z].transpose(1, 0, 2)
    y_edge = lambda y: edges[y].transpose(1, 0, 2).reshape(comps * zn, xn)
    zlo, zhi = shift((z_edge(zn - 1), z_edge(0)), ("px", "tr"))
    ylo, yhi = shift((y_edge(yn - 1), y_edge(0)), "pz", wrap=False)
    ids = slot_table(row_index, row_counts)
    sent = call(
        explicit_kernel,
        shaped((peers, 2 * (f + xl) + ids.shape[0], lanes), BF16),
        (v, viscosity.transpose(1, 0, 2), zlo, zhi, ylo, yhi, ids),
        flops=2e7,
    )
    inverse = implicit_inverse.astype(BF16)
    got = exchange(sent, "pz")
    solve_flops = 2 * zn * f * total_y * total_y
    u, w, packed, zlo, zhi, xlo, xhi, ids = call(
        first_solve_kernel,
        (
            shaped((zn * f, total_y), F32),
            shaped((zn * xl, total_y), F32),
            shaped((peers, 2 * f, lanes), BF16),
            shaped((f, total_y), BF16),
            shaped((f, total_y), BF16),
            shaped((zn * comps, total_y), BF16),
            shaped((zn * comps, total_y), BF16),
            shaped((peers,) + ids.shape, jnp.int32),
        ),
        (got, inverse),
        scratch=[pltpu.VMEM((zn * f, total_y), BF16)],
        flops=solve_flops,
    )
    zlo, zhi = shift((zhi, zlo), ("px", "tr"))
    xlo, xhi = shift((xhi, xlo), "pz")

    def sample(packed):
        sent = call(
            sample_kernel,
            shaped((members, f, peers * slots), BF16),
            (packed, ids),
            scratch=[pltpu.VMEM((peers, f, members * slots), F32)],
            flops=2 * peers * 256 * 256 * members * slots,
        )
        return exchange(sent, ("pz", "tr"))

    rows_in = sample(packed)
    packed = call(
        second_solve_kernel,
        shaped((peers, 2 * f, lanes), BF16),
        (u, w, zlo, zhi, xlo, xhi, inverse),
        scratch=[pltpu.VMEM((zn * f, total_y), BF16), pltpu.VMEM((zn * f, total_y), F32)],
        flops=solve_flops,
    )
    rows_target = sample(packed)
    member_in = weight_in[0]
    member_out = weight_out[0]
    width, hid = member_in.shape
    batch = 2 * peers * slots
    spots = lax.axis_size("px")
    loss_scale = 1.0 / math.sqrt(spots * batch)
    matmul_flops = 2 * hid * width * batch
    x, hidden, slope, predicted = call(
        forward_kernel,
        (
            shaped((width, batch), BF16),
            shaped((hid, batch), BF16),
            shaped((hid, batch), BF16),
            shaped((width, batch), F32),
        ),
        (rows_in, member_in.T, member_out.T),
        flops=2 * matmul_flops,
    )
    position = lax.axis_index("px")
    place = jnp.stack([position % 2, position // 2]).astype(jnp.int32)

    def delta_out(*refs):
        delta_out_kernel(loss_scale, *refs)

    d, away_out = call(
        delta_out,
        (shaped((width, batch), BF16), shaped((hid // 2, width), BF16)),
        (place, rows_target, predicted, hidden),
        flops=matmul_flops // 2,
    )
    got_out = swap_cores(away_out)
    din, away_in = call(
        delta_in_kernel,
        (shaped((hid, batch), BF16), shaped((width // 2, hid), BF16)),
        (place, d, slope, member_out, x),
        flops=matmul_flops * 3 // 2,
    )
    got_in = swap_cores(away_in)
    packed, away_in = lax.optimization_barrier((packed, away_in))
    planes = exchange(packed, "pz")
    rows = hid // spots
    own, plus, minus, top, bottom = call(
        keep_kernel,
        (
            shaped((2, rows, width), F32),
            shaped((2, rows, width), BF16),
            shaped((2, rows, width), BF16),
            shaped((2, rows // 2, width), BF16),
            shaped((2, rows // 2, width), BF16),
        ),
        (place, hidden, d, x, din, got_out, got_in),
        flops=matmul_flops,
    )
    from_before, from_after = shift_chips(top, bottom)
    plus, minus = call(
        relay_kernel,
        (shaped(plus.shape, BF16), shaped(minus.shape, BF16)),
        (plus, minus, from_before, from_after),
    )
    from_before, from_after = shift_chips(plus, minus)
    share_out, share_in = call(
        finish_kernel,
        (shaped((rows, width), F32), shaped((width // spots, hid), F32)),
        (own, from_before, from_after),
    )
    result = call(planes_kernel, shaped((comps, zn, yn, xn), F32), (planes,))
    return (result.transpose(2, 1, 0, 3), share_in[None], share_out[None])


def solution(mesh):
    in_specs = (
        P("pz", ("px", "tr"), None, None),
        P("pz", ("px", "tr"), None),
        P(),
        P("px", "pz", "tr", None, None),
        P("px", "pz", "tr", None),
        P(("pz", "tr"), None, None),
        P(("pz", "tr"), None, None),
    )
    out_specs = (
        P("pz", ("px", "tr"), None, None),
        P(("pz", "tr"), "px", None),
        P(("pz", "tr"), "px", None),
    )
    return jax.shard_map(
        per_device, mesh=mesh, in_specs=in_specs, out_specs=out_specs, check_vma=False
    )
```

```python
import math

import jax
import jax.numpy as jnp
from jax import lax
from jax.experimental import pallas as pl
from jax.experimental.pallas import tpu as pltpu
from jax.sharding import PartitionSpec as P

diffusion_factor = 0.08
F32 = jnp.float32
BF16 = jnp.bfloat16
MIB = 1 << 20


def call(kernel, out_shape, args, scratch=(), flops=1e6, far_in=(), far_out=()):
    outs = jax.tree.leaves(out_shape)
    size = lambda x: math.prod(x.shape) * jnp.dtype(x.dtype).itemsize
    near = [x for k, x in enumerate(args) if k not in far_in]
    near += [x for k, x in enumerate(outs) if k not in far_out]
    held = sum(size(x) for x in near) + sum(size(x) for x in scratch if x.dtype in (F32, BF16, jnp.int32))

    def spec(k, far, scalar=False):
        space = pltpu.HBM if k in far else pltpu.SMEM if scalar else pltpu.VMEM
        return pl.BlockSpec(memory_space=space)

    out_specs = tuple(spec(k, far_out) for k in range(len(outs)))
    return pl.pallas_call(
        kernel,
        out_shape=out_shape,
        in_specs=[spec(k, far_in, x.ndim == 1) for k, x in enumerate(args)],
        out_specs=out_specs if isinstance(out_shape, tuple) else out_specs[0],
        scratch_shapes=list(scratch),
        compiler_params=pltpu.CompilerParams(vmem_limit_bytes=held + 6 * MIB),
        cost_estimate=pl.CostEstimate(
            flops=int(flops),
            bytes_accessed=int(sum(size(x) for x in list(args) + outs)),
            transcendentals=0,
        ),
    )(*args)


class Copies:
    def __init__(self, sems):
        self.sems, self.used, self.open = sems, 0, []

    def start(self, source, target):
        copy = pltpu.make_async_copy(source, target, self.sems.at[self.used])
        copy.start()
        self.used += 1
        self.open.append(copy)
        return copy

    def finish(self):
        for copy in self.open:
            copy.wait()
        self.open = []

    def wait(self, copy):
        copy.wait()
        self.open.remove(copy)


def shaped(shape, dtype):
    return jax.ShapeDtypeStruct(shape, dtype)


def shift(array, axis, wrap=True):
    last, first = array
    size = lax.axis_size(axis)
    up = [(i, (i + 1) % size) for i in range(size if wrap else size - 1)]
    down = [(j, i) for i, j in up]
    return lax.ppermute(last, axis, up), lax.ppermute(first, axis, down)


HALO_ROWS = 24


def columns_kernel(v, w, ids, out, edge):
    comps, zn, yn, xn = v.shape
    peers = out.shape[0]
    xl = xn // peers
    half = (comps + 1) * xl
    for zh in range(zn // 2):
        for c in range(comps + 1):
            source = w if c == comps else v.at[c]
            pair = [source[z].astype(F32) for z in (2 * zh, 2 * zh + 1)]
            turned = jnp.concatenate(pair, axis=0).T
            base = zh * half + c * xl
            for q in range(peers):
                out[q, base : base + xl, :] = turned[q * xl : (q + 1) * xl].astype(BF16)
            if c == comps:
                continue
            for q in range(peers):
                before = (q * xl - 1) % xn
                after = (q + 1) * xl % xn
                r = q * HALO_ROWS + zh * comps + c
                edge[r : r + 1] = turned[before : before + 1]
                edge[r + zn // 2 * comps : r + zn // 2 * comps + 1] = turned[after : after + 1]
    start = zn // 2 * half
    numbers = ids[...].astype(F32)
    for q in range(peers):
        edge[(q + 1) * HALO_ROWS - 8 : (q + 1) * HALO_ROWS] = numbers
        out[q, start : start + HALO_ROWS, :] = edge[
            q * HALO_ROWS : (q + 1) * HALO_ROWS
        ].astype(BF16)


def solve(e, a):
    return lax.dot_general(
        e[...], a[...], (((1,), (1,)), ((), ())), preferred_element_type=F32
    )


def pack_columns(u, packed, zn):
    peers, rows, lanes = packed.shape
    f = rows // (zn // 2)
    yn = lanes // 2
    low = lax.broadcasted_iota(jnp.int32, (f, lanes), 1) < yn
    for j in range(peers // 2):
        for zh in range(zn // 2):
            first = u[(2 * zh) * f : (2 * zh + 1) * f, j * lanes : (j + 1) * lanes]
            second = u[(2 * zh + 1) * f : (2 * zh + 2) * f, j * lanes : (j + 1) * lanes]
            even = jnp.where(low, first, pltpu.roll(second, yn, 1))
            odd = jnp.where(low, pltpu.roll(first, yn, 1), second)
            packed[2 * j, zh * f : (zh + 1) * f, :] = even.astype(BF16)
            packed[2 * j + 1, zh * f : (zh + 1) * f, :] = odd.astype(BF16)


def spread_kernel(got, v, w, xlo, xhi, zlo, zhi, ids):
    peers, rows, lanes = got.shape
    ids[...] = got[:, rows - 8 :, :].astype(F32).astype(jnp.int32)
    yn = lanes // 2
    zn = 4
    half = (rows - HALO_ROWS) // 2
    xl = w.shape[0] // zn
    f = half - xl
    comps = f // xl
    low = lax.broadcasted_iota(jnp.int32, (rows, lanes), 1) < yn
    for j in range(peers // 2):
        one = got[2 * j].astype(F32)
        two = got[2 * j + 1].astype(F32)
        sides = (
            jnp.where(low, one, pltpu.roll(two, yn, 1)),
            jnp.where(low, pltpu.roll(one, yn, 1), two),
        )
        at = slice(j * lanes, (j + 1) * lanes)
        for zh in range(zn // 2):
            for side in range(2):
                z = 2 * zh + side
                whole = sides[side]
                v[z * f : (z + 1) * f, at] = whole[zh * half : zh * half + f].astype(BF16)
                w[z * xl : (z + 1) * xl, at] = whole[zh * half + f : (zh + 1) * half].astype(BF16)
                r = zn // 2 * half + zh * comps
                xlo[z * comps : (z + 1) * comps, at] = whole[r : r + comps]
                r = r + zn // 2 * comps
                xhi[z * comps : (z + 1) * comps, at] = whole[r : r + comps]
    zlo[...] = v[0:f]
    zhi[...] = v[(zn - 1) * f : zn * f]


def explicit_plane(z, u, w, zlo, zhi, x_before, x_after, e):
    f, cols = zlo.shape
    zn = u.shape[0] // f
    xl = w.shape[0] // zn
    comps = f // xl
    row = lax.broadcasted_iota(jnp.int32, (xl, cols), 0)
    lane = lax.broadcasted_iota(jnp.int32, (xl, cols), 1)
    factor = diffusion_factor * w[z * xl : (z + 1) * xl].astype(F32)
    for c in range(comps):
        r = z * comps + c
        at = slice(r * xl, (r + 1) * xl)
        cur = u[at].astype(F32)
        if z > 0:
            total = u[(r - comps) * xl : (r - comps + 1) * xl].astype(F32)
        else:
            total = zlo[c * xl : (c + 1) * xl].astype(F32)
        if z < zn - 1:
            total = total + u[(r + comps) * xl : (r + comps + 1) * xl].astype(F32)
        else:
            total = total + zhi[c * xl : (c + 1) * xl].astype(F32)
        total = total + jnp.where(row == 0, x_before[r : r + 1], pltpu.roll(cur, 1, 0))
        total = total + jnp.where(row == xl - 1, x_after[r : r + 1], pltpu.roll(cur, xl - 1, 0))
        total = total + jnp.where(lane == 0, 0.0, pltpu.roll(cur, 1, 1))
        total = total + jnp.where(lane == cols - 1, 0.0, pltpu.roll(cur, cols - 1, 1))
        e[at] = (cur + factor * (total - 6.0 * cur)).astype(BF16)


def first_kernel(
    v, w, xlo, xhi, zlo, zhi, ids, a,
    u_far, w_far, ids_far, zlo_far, zhi_far, xlo_far, xhi_far, sent_far,
    e, u, packed, picked, sent, z_edge, x_edge, sems,
):
    copies = Copies(sems)
    copies.start(w, w_far)
    copies.start(ids, ids_far)
    x_before, x_after = xlo[...], xhi[...]
    zn = 4
    for z in range(zn):
        explicit_plane(z, v, w, zlo, zhi, x_before, x_after, e)
    u[...] = solve(e, a)
    copies.start(u, u_far)
    f = zlo.shape[0]
    z_edge[0] = u[0:f].astype(BF16)
    z_edge[1] = u[(zn - 1) * f : zn * f].astype(BF16)
    xl = w.shape[0] // zn
    groups = u.shape[0] // xl
    for r in range(groups):
        x_edge[0, r : r + 1] = u[r * xl : r * xl + 1]
        x_edge[1, r : r + 1] = u[(r + 1) * xl - 1 : (r + 1) * xl]
    for k, (edge, far) in enumerate(
        ((z_edge, zlo_far), (z_edge, zhi_far), (x_edge, xlo_far), (x_edge, xhi_far))
    ):
        copies.start(edge.at[k % 2], far)
    pack_columns(u, packed, zn)
    sample(packed, ids, picked, sent, lambda part: copies.start(sent.at[part], sent_far.at[part]))
    copies.finish()


def second_kernel(
    u_far, w_far, ids_far, zlo, zhi, xlo, xhi, a, packed_far, sent_far,
    e, u, w, ids, packed, picked, sent, sems,
):
    copies = Copies(sems)
    f = zlo.shape[0]
    zn = u.shape[0] // f
    w_copy = copies.start(w_far, w)
    parts = [pl.ds(z * f, f) for z in range(zn)]
    arriving = [copies.start(u_far.at[part], u.at[part]) for part in parts]
    ids_copy = copies.start(ids_far, ids)
    copies.wait(w_copy)
    copies.wait(arriving[0])
    x_before, x_after = xlo[...], xhi[...]
    for z in range(zn):
        if z < zn - 1:
            copies.wait(arriving[z + 1])
        explicit_plane(z, u, w, zlo, zhi, x_before, x_after, e)
    u[...] = solve(e, a)
    pack_columns(u, packed, zn)
    copies.start(packed, packed_far)
    copies.wait(ids_copy)
    sample(packed, ids, picked, sent, lambda part: copies.start(sent.at[part], sent_far.at[part]))
    copies.finish()


GROUP = 8


def sample(packed, ids, picked, out, ready):
    peers, rows, lanes = packed.shape
    f = rows // 2
    yn = lanes // 2
    blocks = picked.shape[2] // lanes
    r = lax.broadcasted_iota(jnp.int32, (2 * lanes, lanes), 0)
    row_id = (r % yn) * 4 + r // yn
    for q in range(peers):
        table = jnp.concatenate([packed[q, 0:f], packed[q, f:rows]], axis=1)
        wanted = pltpu.roll(ids[q], (GROUP * q) % lanes, 1) if q else ids[q]
        for b in range(blocks):
            hot = jnp.where(row_id == wanted[b : b + 1], 1.0, 0.0).astype(BF16)
            picked[q, :, b * lanes : (b + 1) * lanes] = jnp.dot(
                table, hot, preferred_element_type=F32
            )
    group = lax.broadcasted_iota(jnp.int32, (f, lanes), 1) // GROUP
    per = lanes // GROUP
    halves = out.shape[0] // per
    for b in range(blocks):
        kg, mh = b // halves, b % halves
        held = [picked[q, :, b * lanes : (b + 1) * lanes] for q in range(peers)]
        step = 1
        while step < peers:
            take = (group // step) % 2 == 1
            held = [jnp.where(take, held[(i + step) % peers], held[i]) for i in range(peers)]
            step *= 2
        for ml in range(per):
            out[mh * per + ml, :, kg * lanes : (kg + 1) * lanes] = held[(-ml) % peers].astype(BF16)
        ready((pl.ds(mh * per, per), slice(None), pl.ds(kg * lanes, lanes)))


def slot_table(row_index, row_counts):
    members, slots = row_index.shape[3:]
    index = row_index.reshape(members, slots)
    counts = row_counts.reshape(members, 1)
    live = jnp.arange(slots, dtype=jnp.int32)[None, :] < counts
    index = jnp.where(live, index, -1)
    per = 128 // GROUP
    index = index.reshape(members // per, per, slots // GROUP, GROUP).transpose(2, 0, 1, 3)
    index = index.reshape(-1, 128)
    fill = jnp.full((8 - index.shape[0], 128), -1, jnp.int32)
    return jnp.concatenate([index, fill], axis=0)


def gather_rows(got, turned, comps=3):
    sources, f, slots = got.shape
    sides = 2
    peers = sources // sides
    xl = f // comps
    for q in range(peers):
        for side in range(sides):
            for c in range(comps):
                at = (c * peers + q) * xl
                turned[at : at + xl, side * slots : (side + 1) * slots] = got[
                    q * sides + side, c * xl : (c + 1) * xl
                ]


CONTRACT_ROWS = (((1,), (1,)), ((), ()))


def over_rows(left, right):
    return lax.dot_general(left, right, CONTRACT_ROWS, preferred_element_type=F32)


def forward_kernel(
    got, w_in, w_out, x_far, hidden_far, slope_far, predicted_far,
    x, hidden, slope, predicted, sems,
):
    copies = Copies(sems)
    gather_rows(got, x)
    copies.start(x, x_far)
    wide = 256

    def chunk(i, carry):
        at = pl.ds(pl.multiple_of(i * wide, wide), wide)
        pre = jnp.dot(w_in[at, :], x[...], preferred_element_type=F32)
        logistic = jax.nn.sigmoid(pre)
        hidden[at, :] = (pre * logistic).astype(BF16)
        slope[at, :] = (logistic * (1.0 + pre * (1.0 - logistic))).astype(slope.dtype)
        return carry

    lax.fori_loop(0, hidden.shape[0] // wide, chunk, 0)
    copies.start(hidden, hidden_far)
    copies.start(slope, slope_far)

    def second(i, carry):
        at = pl.ds(pl.multiple_of(i * wide, wide), wide)
        predicted[at, :] = jnp.dot(w_out[at, :], hidden[...], preferred_element_type=F32)
        return carry

    lax.fori_loop(0, predicted.shape[0] // wide, second, 0)
    copies.start(predicted, predicted_far)
    copies.finish()


def block_rows(array, y, core, rows):
    return array[pl.ds(pl.multiple_of((2 * y + core) * rows, rows), rows), :]


def away_blocks(array, right, core, away, rows):
    for pair in range(away.shape[0] // (2 * rows)):
        left = jnp.concatenate(
            [block_rows(array, 2 * pair + k, 1 - core, rows) for k in range(2)], axis=0
        )
        away[2 * pair * rows : 2 * (pair + 1) * rows] = over_rows(left, right[...]).astype(BF16)


def delta_out_kernel(scale, place, got, predicted_far, hidden_far, d, away, predicted, hidden, sems):
    copies = Copies(sems)
    count = 3
    rows = d.shape[0] // count
    parts = [pl.ds(k * rows, rows) for k in range(count)]
    arriving = [copies.start(predicted_far.at[part], predicted.at[part]) for part in parts]
    copies.start(hidden_far, hidden)
    gather_rows(got, d)
    for k in range(count):
        copies.wait(arriving[k])
        at = slice(k * rows, (k + 1) * rows)
        d[at] = ((predicted[at] - d[at].astype(F32)) * scale).astype(BF16)
    copies.finish()
    away_blocks(hidden, d, place[0], away, away.shape[0] // 4)


def delta_in_kernel(place, d, slope, w_out, x, din, away):
    wide = 256

    def chunk(i, carry):
        at = pl.ds(pl.multiple_of(i * wide, wide), wide)
        back = jnp.dot(w_out[at, :], d[...], preferred_element_type=F32)
        din[at, :] = (back * slope[at, :].astype(F32)).astype(BF16)
        return carry

    lax.fori_loop(0, din.shape[0] // wide, chunk, 0)
    away_blocks(x, din, place[0], away, away.shape[0] // 4)


def fold(block, rows, width):
    extra = rows - block.shape[0]
    pieces = [
        block[g * extra : (g + 1) * extra, width:] for g in range(block.shape[0] // extra)
    ]
    return jnp.concatenate([block[:, :width], jnp.concatenate(pieces, axis=1)], axis=0)


def unfold(block, rows):
    extra = block.shape[0] - rows
    count = rows // extra
    wide = block.shape[1] // count
    pieces = [block[rows:, g * wide : (g + 1) * wide] for g in range(count)]
    return jnp.concatenate([block[:rows], jnp.concatenate(pieces, axis=0)], axis=1)


def keep_kernel(place, hidden, d, x, din, got_out, got_in, own, plus, minus, top, bottom):
    core, y = place[0], place[1]
    rows, width = own.shape[1:]
    half = rows // 2

    def put(which, k, block):
        if k == 0:
            own[which] = block
        elif k == 1:
            plus[which] = block.astype(BF16)
        elif k == 3:
            minus[which] = block.astype(BF16)
        else:
            top[which] = block[:half].astype(BF16)
            bottom[which] = block[half:].astype(BF16)

    for which, (left, right, got) in enumerate(((hidden, d, got_out), (x, din, got_in))):
        size = got.shape[0] // 4
        for ks in ((2, 1), (3, 0)):
            ys = [lax.rem(y + k, 4) for k in ks]
            blocks = jnp.concatenate([block_rows(left, at, core, size) for at in ys], axis=0)
            value = over_rows(blocks, right[...])
            for n, (k, at) in enumerate(zip(ks, ys)):
                block = value[n * size : (n + 1) * size]
                block = block + got[pl.ds(pl.multiple_of(at * size, size), size), :].astype(F32)
                put(which, k, block if which == 0 else fold(block, rows, width))


def relay_kernel(plus, minus, from_before, from_after, plus_out, minus_out):
    half = from_before.shape[1]
    for which in range(plus.shape[0]):
        plus_out[which, :half] = (
            plus[which, :half].astype(F32) + from_before[which].astype(F32)
        ).astype(BF16)
        plus_out[which, half:] = plus[which, half:]
        minus_out[which, :half] = minus[which, :half]
        minus_out[which, half:] = (
            minus[which, half:].astype(F32) + from_after[which].astype(F32)
        ).astype(BF16)


def finish_kernel(own, from_before, from_after, share_out, share_in):
    total = [
        own[k] + from_before[k].astype(F32) + from_after[k].astype(F32) for k in range(2)
    ]
    share_out[...] = total[0]
    share_in[...] = unfold(total[1], share_in.shape[0])


def planes_kernel(got, out):
    comps, zn, yn, xn = out.shape
    peers = got.shape[0]
    xl = xn // peers
    f = comps * xl
    for zh in range(zn // 2):
        for c in range(comps):
            base = zh * f + c * xl
            block = jnp.concatenate(
                [got[q, base : base + xl, :] for q in range(peers)], axis=0
            ).astype(F32)
            turned = block.T
            out[c, 2 * zh] = turned[0:yn]
            out[c, 2 * zh + 1] = turned[yn : 2 * yn]


def exchange(array, axis):
    return lax.all_to_all(array, axis, split_axis=0, concat_axis=0, tiled=True)


def swap_cores(array):
    size = lax.axis_size("px")
    return lax.ppermute(array, "px", [(i, i ^ 1) for i in range(size)])


def shift_chips(forward, backward):
    size = lax.axis_size("px")
    up = [(i, (i + 2) % size) for i in range(size)]
    down = [(j, i) for i, j in up]
    return lax.ppermute(forward, "px", up), lax.ppermute(backward, "px", down)


def per_device(velocity, viscosity, implicit_inverse, row_index, row_counts, weight_in, weight_out):
    yn, zn, comps, xn = velocity.shape
    peers = lax.axis_size("pz")
    total_y = yn * peers
    xl = xn // peers
    f = comps * xl
    lanes = 2 * yn
    members, slots = row_index.shape[3:]

    v = velocity.astype(BF16).transpose(2, 1, 0, 3)
    ids = slot_table(row_index, row_counts)
    sent = call(
        columns_kernel,
        shaped((peers, 2 * (f + xl) + HALO_ROWS, lanes), BF16),
        (v, viscosity.astype(BF16).transpose(1, 0, 2), ids),
        scratch=[pltpu.VMEM((peers * HALO_ROWS, lanes), F32)],
    )
    inverse = implicit_inverse.astype(BF16)
    got = exchange(sent, "pz")
    solve_flops = 2 * zn * f * total_y * total_y
    edge = shaped((f, total_y), BF16)
    x_edge = shaped((zn * comps, total_y), F32)
    ids_all = shaped((peers,) + ids.shape, jnp.int32)
    v, w, xlo, xhi, zlo, zhi, ids = call(
        spread_kernel,
        (shaped((zn * f, total_y), BF16), shaped((zn * xl, total_y), BF16))
        + (x_edge, x_edge, edge, edge, ids_all),
        (got,),
    )
    zlo, zhi = shift((zhi, zlo), ("px", "tr"))
    message = shaped((members, f, peers * slots), BF16)
    sample_flops = 2 * peers * f * 256 * members * slots
    sampling = [
        pltpu.VMEM((peers, 2 * f, lanes), BF16),
        pltpu.VMEM((peers, f, members * slots), F32),
        pltpu.VMEM(message.shape, BF16),
    ]
    u, w, ids, zlo, zhi, xlo, xhi, sent = call(
        first_kernel,
        (shaped((zn * f, total_y), F32), shaped(w.shape, BF16), ids_all)
        + (edge, edge, x_edge, x_edge, message),
        (v, w, xlo, xhi, zlo, zhi, ids, inverse),
        scratch=[pltpu.VMEM((zn * f, total_y), BF16), pltpu.VMEM((zn * f, total_y), F32)]
        + sampling
        + [
            pltpu.VMEM((2, f, total_y), BF16),
            pltpu.VMEM((2, zn * comps, total_y), F32),
            pltpu.SemaphoreType.DMA((16,)),
        ],
        flops=solve_flops + sample_flops,
        far_out=range(8),
    )
    rows_in = exchange(sent, ("pz", "tr"))
    zlo, zhi = shift((zhi, zlo), ("px", "tr"))
    xlo, xhi = shift((xhi, xlo), "pz")
    packed, sent = call(
        second_kernel,
        (shaped((peers, 2 * f, lanes), BF16), message),
        (u, w, ids, zlo, zhi, xlo, xhi, inverse),
        scratch=[
            pltpu.VMEM((zn * f, total_y), BF16),
            pltpu.VMEM((zn * f, total_y), F32),
            pltpu.VMEM(w.shape, BF16),
            pltpu.VMEM(ids.shape, jnp.int32),
        ]
        + sampling
        + [pltpu.SemaphoreType.DMA((16,))],
        flops=solve_flops + sample_flops,
        far_in=(0, 1, 2),
        far_out=(0, 1),
    )
    rows_target = exchange(sent, ("pz", "tr"))

    member_in = weight_in[0]
    member_out = weight_out[0]
    width, hid = member_in.shape
    batch = 2 * peers * slots
    spots = lax.axis_size("px")
    loss_scale = 1.0 / math.sqrt(spots * batch)
    matmul_flops = 2 * hid * width * batch
    x, hidden, slope, predicted = call(
        forward_kernel,
        (
            shaped((width, batch), BF16),
            shaped((hid, batch), BF16),
            shaped((hid, batch), BF16),
            shaped((width, batch), F32),
        ),
        (rows_in, member_in.T, member_out.T),
        scratch=[
            pltpu.VMEM((width, batch), BF16),
            pltpu.VMEM((hid, batch), BF16),
            pltpu.VMEM((hid, batch), BF16),
            pltpu.VMEM((width, batch), F32),
            pltpu.SemaphoreType.DMA((4,)),
        ],
        flops=2 * matmul_flops,
        far_out=range(4),
    )
    position = lax.axis_index("px")
    place = jnp.stack([position % 2, position // 2]).astype(jnp.int32)

    def delta_out(*refs):
        delta_out_kernel(loss_scale, *refs)

    d, away_out = call(
        delta_out,
        (shaped((width, batch), BF16), shaped((hid // 2, width), BF16)),
        (place, rows_target, predicted, hidden),
        scratch=[
            pltpu.VMEM((width, batch), F32),
            pltpu.VMEM((hid, batch), BF16),
            pltpu.SemaphoreType.DMA((4,)),
        ],
        flops=matmul_flops // 2,
        far_in=(2, 3),
    )
    got_out = swap_cores(away_out)
    din, away_in = call(
        delta_in_kernel,
        (shaped((hid, batch), BF16), shaped((width // 2, hid), BF16)),
        (place, d, slope, member_out, x),
        flops=matmul_flops * 3 // 2,
    )
    got_in = swap_cores(away_in)
    rows = hid // spots
    own, plus, minus, top, bottom = call(
        keep_kernel,
        (
            shaped((2, rows, width), F32),
            shaped((2, rows, width), BF16),
            shaped((2, rows, width), BF16),
            shaped((2, rows // 2, width), BF16),
            shaped((2, rows // 2, width), BF16),
        ),
        (place, hidden, d, x, din, got_out, got_in),
        flops=matmul_flops,
    )
    packed, top = lax.optimization_barrier((packed, top))
    from_before, from_after = shift_chips(top, bottom)
    planes = exchange(packed, "pz")
    plus, minus = call(
        relay_kernel,
        (shaped(plus.shape, BF16), shaped(minus.shape, BF16)),
        (plus, minus, from_before, from_after),
    )
    from_before, from_after = shift_chips(plus, minus)
    share_out, share_in = call(
        finish_kernel,
        (shaped((rows, width), F32), shaped((width // spots, hid), F32)),
        (own, from_before, from_after),
    )
    result = call(planes_kernel, shaped((comps, zn, yn, xn), F32), (planes,))
    return (result.transpose(2, 1, 0, 3), share_in[None], share_out[None])


def solution(mesh):
    in_specs = (
        P("pz", ("px", "tr"), None, None),
        P("pz", ("px", "tr"), None),
        P(),
        P("px", "pz", "tr", None, None),
        P("px", "pz", "tr", None),
        P(("pz", "tr"), None, None),
        P(("pz", "tr"), None, None),
    )
    out_specs = (
        P("pz", ("px", "tr"), None, None),
        P(("pz", "tr"), "px", None),
        P(("pz", "tr"), "px", None),
    )
    return jax.shard_map(
        per_device, mesh=mesh, in_specs=in_specs, out_specs=out_specs, check_vma=False
    )
```

```python
import math

import jax
import jax.numpy as jnp
from jax import lax
from jax.experimental import pallas as pl
from jax.experimental.pallas import tpu as pltpu
from jax.sharding import PartitionSpec as P

diffusion_factor = 0.08
F32 = jnp.float32
BF16 = jnp.bfloat16
MIB = 1 << 20


def call(kernel, out_shape, args, scratch=(), flops=1e6, far_in=(), far_out=()):
    outs = jax.tree.leaves(out_shape)
    size = lambda x: math.prod(x.shape) * jnp.dtype(x.dtype).itemsize
    near = [x for k, x in enumerate(args) if k not in far_in]
    near += [x for k, x in enumerate(outs) if k not in far_out]
    held = sum(size(x) for x in near) + sum(size(x) for x in scratch if x.dtype in (F32, BF16, jnp.int32))

    def spec(k, far, scalar=False):
        space = pltpu.HBM if k in far else pltpu.SMEM if scalar else pltpu.VMEM
        return pl.BlockSpec(memory_space=space)

    out_specs = tuple(spec(k, far_out) for k in range(len(outs)))
    args = [
        pltpu.with_memory_space_constraint(x, pltpu.HBM) if k in far_in else x
        for k, x in enumerate(args)
    ]
    pinned = tuple(
        pltpu.HBM(x.shape, x.dtype) if k in far_out else x for k, x in enumerate(outs)
    )
    return pl.pallas_call(
        kernel,
        out_shape=pinned if isinstance(out_shape, tuple) else pinned[0],
        in_specs=[spec(k, far_in, x.ndim == 1) for k, x in enumerate(args)],
        out_specs=out_specs if isinstance(out_shape, tuple) else out_specs[0],
        scratch_shapes=list(scratch),
        compiler_params=pltpu.CompilerParams(vmem_limit_bytes=held + 6 * MIB),
        cost_estimate=pl.CostEstimate(
            flops=int(flops),
            bytes_accessed=int(sum(size(x) for x in list(args) + outs)),
            transcendentals=0,
        ),
    )(*args)


class Copies:
    def __init__(self, sems):
        self.sems, self.used, self.open = sems, 0, []

    def start(self, source, target):
        copy = pltpu.make_async_copy(source, target, self.sems.at[self.used])
        copy.start()
        self.used += 1
        self.open.append(copy)
        return copy

    def finish(self):
        for copy in self.open:
            copy.wait()
        self.open = []

    def wait(self, copy):
        copy.wait()
        self.open.remove(copy)


def shaped(shape, dtype):
    return jax.ShapeDtypeStruct(shape, dtype)


def shift(array, axis, wrap=True):
    last, first = array
    size = lax.axis_size(axis)
    up = [(i, (i + 1) % size) for i in range(size if wrap else size - 1)]
    down = [(j, i) for i, j in up]
    return lax.ppermute(last, axis, up), lax.ppermute(first, axis, down)


HALO_ROWS = 24
GROUP = 8


def columns_kernel(v, w, index, counts, out, edge):
    comps, zn, yn, xn = v.shape
    peers = out.shape[0]
    xl = xn // peers
    lanes_of = out.shape[2]
    half = (comps + 1) * xl
    for zh in range(zn // 2):
        for c in range(comps + 1):
            source = w if c == comps else v.at[c]
            pair = [source[z].astype(F32) for z in (2 * zh, 2 * zh + 1)]
            turned = jnp.concatenate(pair, axis=0).T
            base = zh * half + c * xl
            for q in range(peers):
                out[q, base : base + xl, :] = turned[q * xl : (q + 1) * xl].astype(BF16)
            if c == comps:
                continue
            for q in range(peers):
                before = (q * xl - 1) % xn
                after = (q + 1) * xl % xn
                r = q * HALO_ROWS + zh * comps + c
                edge[r : r + 1] = turned[before : before + 1]
                edge[r + zn // 2 * comps : r + zn // 2 * comps + 1] = turned[after : after + 1]
    start = zn // 2 * half
    slots, members = index.shape
    slot = lax.broadcasted_iota(jnp.int32, (slots, members), 0)
    live = jnp.where(slot < counts[...], index[...], -1).astype(F32)
    sides = lanes_of // members
    rows = slots // sides
    numbers = jnp.concatenate([live[k * rows : (k + 1) * rows] for k in range(sides)], axis=1)
    numbers = jnp.concatenate([numbers, jnp.zeros((8 - rows, lanes_of), F32)], axis=0)
    for q in range(peers):
        edge[(q + 1) * HALO_ROWS - 8 : (q + 1) * HALO_ROWS] = numbers
        out[q, start : start + HALO_ROWS, :] = edge[
            q * HALO_ROWS : (q + 1) * HALO_ROWS
        ].astype(BF16)


def solve(e, a):
    return lax.dot_general(
        e[...], a[...], (((1,), (1,)), ((), ())), preferred_element_type=F32
    )


def pack_columns(u, packed, zn):
    peers, rows, lanes = packed.shape
    f = rows // (zn // 2)
    yn = lanes // 2
    low = lax.broadcasted_iota(jnp.int32, (f, lanes), 1) < yn
    for j in range(peers // 2):
        for zh in range(zn // 2):
            first = u[(2 * zh) * f : (2 * zh + 1) * f, j * lanes : (j + 1) * lanes]
            second = u[(2 * zh + 1) * f : (2 * zh + 2) * f, j * lanes : (j + 1) * lanes]
            even = jnp.where(low, first, pltpu.roll(second, yn, 1))
            odd = jnp.where(low, pltpu.roll(first, yn, 1), second)
            packed[2 * j, zh * f : (zh + 1) * f, :] = even.astype(BF16)
            packed[2 * j + 1, zh * f : (zh + 1) * f, :] = odd.astype(BF16)


def spread_kernel(got, v, w, xlo, xhi, zlo, zhi, ids):
    peers, rows, lanes = got.shape
    table = got[:, rows - 8 :, :].astype(F32).reshape(peers * 8, lanes).astype(BF16)
    members = 32
    per = lanes // GROUP
    source = lax.broadcasted_iota(jnp.int32, (lanes, lanes), 0)
    lane = lax.broadcasted_iota(jnp.int32, (lanes, lanes), 1)
    late = lax.broadcasted_iota(jnp.int32, (1, lanes), 1) % GROUP >= GROUP // 2
    halves = members // per
    for mh in range(halves):
        wanted = (lane % (GROUP // 2)) * members + mh * per + lane // GROUP
        moved = jnp.dot(
            table, jnp.where(source == wanted, 1.0, 0.0).astype(BF16), preferred_element_type=F32
        )
        for q in range(peers):
            for kg in range(3):
                r = q * 8 + 2 * kg
                line = jnp.where(late, moved[r + 1 : r + 2], moved[r : r + 1])
                at = kg * halves + mh
                ids[q, at : at + 1, :] = line.astype(jnp.int32)
    yn = lanes // 2
    zn = 4
    half = (rows - HALO_ROWS) // 2
    xl = w.shape[0] // zn
    f = half - xl
    comps = f // xl
    low = lax.broadcasted_iota(jnp.int32, (rows, lanes), 1) < yn
    for j in range(peers // 2):
        one = got[2 * j].astype(F32)
        two = got[2 * j + 1].astype(F32)
        sides = (
            jnp.where(low, one, pltpu.roll(two, yn, 1)),
            jnp.where(low, pltpu.roll(one, yn, 1), two),
        )
        at = slice(j * lanes, (j + 1) * lanes)
        for zh in range(zn // 2):
            for side in range(2):
                z = 2 * zh + side
                whole = sides[side]
                v[z * f : (z + 1) * f, at] = whole[zh * half : zh * half + f].astype(BF16)
                w[z * xl : (z + 1) * xl, at] = whole[zh * half + f : (zh + 1) * half].astype(BF16)
                r = zn // 2 * half + zh * comps
                xlo[z * comps : (z + 1) * comps, at] = whole[r : r + comps]
                r = r + zn // 2 * comps
                xhi[z * comps : (z + 1) * comps, at] = whole[r : r + comps]
    zlo[...] = v[0:f]
    zhi[...] = v[(zn - 1) * f : zn * f]


def explicit_plane(z, u, w, zlo, zhi, x_before, x_after, e):
    f, cols = zlo.shape
    zn = u.shape[0] // f
    xl = w.shape[0] // zn
    comps = f // xl
    row = lax.broadcasted_iota(jnp.int32, (xl, cols), 0)
    lane = lax.broadcasted_iota(jnp.int32, (xl, cols), 1)
    factor = diffusion_factor * w[z * xl : (z + 1) * xl].astype(F32)
    for c in range(comps):
        r = z * comps + c
        at = slice(r * xl, (r + 1) * xl)
        cur = u[at].astype(F32)
        if z > 0:
            total = u[(r - comps) * xl : (r - comps + 1) * xl].astype(F32)
        else:
            total = zlo[c * xl : (c + 1) * xl].astype(F32)
        if z < zn - 1:
            total = total + u[(r + comps) * xl : (r + comps + 1) * xl].astype(F32)
        else:
            total = total + zhi[c * xl : (c + 1) * xl].astype(F32)
        total = total + jnp.where(row == 0, x_before[r : r + 1], pltpu.roll(cur, 1, 0))
        total = total + jnp.where(row == xl - 1, x_after[r : r + 1], pltpu.roll(cur, xl - 1, 0))
        total = total + jnp.where(lane == 0, 0.0, pltpu.roll(cur, 1, 1))
        total = total + jnp.where(lane == cols - 1, 0.0, pltpu.roll(cur, cols - 1, 1))
        e[at] = (cur + factor * (total - 6.0 * cur)).astype(BF16)


def first_kernel(
    v, w, xlo, xhi, zlo, zhi, ids, a_far,
    u_far, w_far, ids_far, packed, z_first, z_last, x_first, x_last,
    e, u, a, sems,
):
    copies = Copies(sems)
    a_copy = copies.start(a_far, a)
    copies.start(w, w_far)
    copies.start(ids, ids_far)
    x_before, x_after = xlo[...], xhi[...]
    zn = 4
    for z in range(zn):
        explicit_plane(z, v, w, zlo, zhi, x_before, x_after, e)
    copies.wait(a_copy)
    u[...] = solve(e, a)
    copies.start(u, u_far)
    f = zlo.shape[0]
    z_first[...] = u[0:f].astype(BF16)
    z_last[...] = u[(zn - 1) * f : zn * f].astype(BF16)
    xl = w.shape[0] // zn
    groups = u.shape[0] // xl
    for r in range(groups):
        x_first[r : r + 1] = u[r * xl : r * xl + 1]
        x_last[r : r + 1] = u[(r + 1) * xl - 1 : (r + 1) * xl]
    pack_columns(u, packed, zn)
    copies.finish()


def sample_kernel(packed, ids, sent_far, picked, sent, sems):
    copies = Copies(sems)
    sample(packed, ids, picked, sent, lambda part: copies.start(sent.at[part], sent_far.at[part]))
    copies.finish()


def second_kernel(
    u_far, w_far, ids_far, zlo_far, zhi_far, xlo_far, xhi_far, a_far, packed_far, sent_far,
    e, u, w, ids, zlo, zhi, xlo, xhi, a, packed, picked, sent, sems,
):
    copies = Copies(sems)
    f = zlo.shape[0]
    zn = u.shape[0] // f
    first = [
        copies.start(far, near)
        for far, near in (
            (w_far, w), (zlo_far, zlo), (xlo_far, xlo), (xhi_far, xhi),
        )
    ]
    parts = [pl.ds(z * f, f) for z in range(zn)]
    arriving = [copies.start(u_far.at[part], u.at[part]) for part in parts]
    zhi_copy = copies.start(zhi_far, zhi)
    a_copy = copies.start(a_far, a)
    ids_copy = copies.start(ids_far, ids)
    for copy in first + arriving[:1]:
        copies.wait(copy)
    x_before, x_after = xlo[...], xhi[...]
    for z in range(zn):
        copies.wait(arriving[z + 1] if z < zn - 1 else zhi_copy)
        explicit_plane(z, u, w, zlo, zhi, x_before, x_after, e)
    copies.wait(a_copy)
    u[...] = solve(e, a)
    pack_columns(u, packed, zn)
    copies.start(packed, packed_far)
    copies.wait(ids_copy)
    sample(packed, ids, picked, sent, lambda part: copies.start(sent.at[part], sent_far.at[part]))
    copies.finish()


def sample(packed, ids, picked, out, ready):
    peers, rows, lanes = packed.shape
    f = rows // 2
    yn = lanes // 2
    blocks = picked.shape[2] // lanes
    r = lax.broadcasted_iota(jnp.int32, (2 * lanes, lanes), 0)
    row_id = (r % yn) * 4 + r // yn
    for q in range(peers):
        table = jnp.concatenate([packed[q, 0:f], packed[q, f:rows]], axis=1)
        wanted = pltpu.roll(ids[q], (GROUP * q) % lanes, 1) if q else ids[q]
        for b in range(blocks):
            hot = jnp.where(row_id == wanted[b : b + 1], 1.0, 0.0).astype(BF16)
            picked[q, :, b * lanes : (b + 1) * lanes] = jnp.dot(
                table, hot, preferred_element_type=F32
            )
    group = lax.broadcasted_iota(jnp.int32, (f, lanes), 1) // GROUP
    per = lanes // GROUP
    halves = out.shape[0] // per
    for b in range(blocks):
        kg, mh = b // halves, b % halves
        held = [picked[q, :, b * lanes : (b + 1) * lanes] for q in range(peers)]
        step = 1
        while step < peers:
            take = (group // step) % 2 == 1
            held = [jnp.where(take, held[(i + step) % peers], held[i]) for i in range(peers)]
            step *= 2
        for ml in range(per):
            out[mh * per + ml, :, kg * lanes : (kg + 1) * lanes] = held[(-ml) % peers].astype(BF16)
        ready((pl.ds(mh * per, per), slice(None), pl.ds(kg * lanes, lanes)))


def gather_rows(got, turned, comps=3):
    sources, f, slots = got.shape
    sides = 2
    peers = sources // sides
    xl = f // comps
    for q in range(peers):
        for side in range(sides):
            for c in range(comps):
                at = (c * peers + q) * xl
                turned[at : at + xl, side * slots : (side + 1) * slots] = got[
                    q * sides + side, c * xl : (c + 1) * xl
                ]


CONTRACT_ROWS = (((1,), (1,)), ((), ()))


def over_rows(left, right):
    return lax.dot_general(left, right, CONTRACT_ROWS, preferred_element_type=F32)


def forward_kernel(
    got_far, w_in, w_out, x_far, hidden_far, slope_far, predicted_far,
    got, x, hidden, slope, predicted, sems,
):
    copies = Copies(sems)
    copies.wait(copies.start(got_far, got))
    gather_rows(got, x)
    copies.start(x, x_far)
    wide = 256

    def chunk(i, carry):
        at = pl.ds(pl.multiple_of(i * wide, wide), wide)
        pre = jnp.dot(w_in[at, :], x[...], preferred_element_type=F32)
        logistic = jax.nn.sigmoid(pre)
        hidden[at, :] = (pre * logistic).astype(BF16)
        slope[at, :] = (logistic * (1.0 + pre * (1.0 - logistic))).astype(slope.dtype)
        return carry

    lax.fori_loop(0, hidden.shape[0] // wide, chunk, 0)
    copies.start(hidden, hidden_far)
    copies.start(slope, slope_far)

    def second(i, carry):
        at = pl.ds(pl.multiple_of(i * wide, wide), wide)
        predicted[at, :] = jnp.dot(w_out[at, :], hidden[...], preferred_element_type=F32)
        return carry

    lax.fori_loop(0, predicted.shape[0] // wide, second, 0)
    copies.start(predicted, predicted_far)
    copies.finish()


def block_rows(array, y, core, rows):
    return array[pl.ds(pl.multiple_of((2 * y + core) * rows, rows), rows), :]


def away_blocks(array, right, core, away, rows):
    for pair in range(away.shape[0] // (2 * rows)):
        left = jnp.concatenate(
            [block_rows(array, 2 * pair + k, 1 - core, rows) for k in range(2)], axis=0
        )
        away[2 * pair * rows : 2 * (pair + 1) * rows] = over_rows(left, right[...]).astype(BF16)


def delta_out_kernel(
    scale, place, got_far, predicted_far, hidden_far, d, away,
    got, predicted, hidden, sems,
):
    copies = Copies(sems)
    got_copy = copies.start(got_far, got)
    count = 3
    rows = d.shape[0] // count
    parts = [pl.ds(k * rows, rows) for k in range(count)]
    arriving = [copies.start(predicted_far.at[part], predicted.at[part]) for part in parts]
    copies.start(hidden_far, hidden)
    copies.wait(got_copy)
    gather_rows(got, d)
    for k in range(count):
        copies.wait(arriving[k])
        at = slice(k * rows, (k + 1) * rows)
        d[at] = ((predicted[at] - d[at].astype(F32)) * scale).astype(BF16)
    copies.finish()
    away_blocks(hidden, d, place[0], away, away.shape[0] // 4)


def delta_in_kernel(place, d, slope, w_out, x, din, away):
    wide = 256

    def chunk(i, carry):
        at = pl.ds(pl.multiple_of(i * wide, wide), wide)
        back = jnp.dot(w_out[at, :], d[...], preferred_element_type=F32)
        din[at, :] = (back * slope[at, :].astype(F32)).astype(BF16)
        return carry

    lax.fori_loop(0, din.shape[0] // wide, chunk, 0)
    away_blocks(x, din, place[0], away, away.shape[0] // 4)


def keep_kernel(place, array, right, got, own, plus, minus, top, bottom):
    core, y = place[0], place[1]
    rows = own.shape[0]
    half = rows // 2
    for ks in ((2, 1), (3, 0)):
        ys = [lax.rem(y + k, 4) for k in ks]
        blocks = jnp.concatenate([block_rows(array, at, core, rows) for at in ys], axis=0)
        value = over_rows(blocks, right[...])
        for n, (k, at) in enumerate(zip(ks, ys)):
            block = value[n * rows : (n + 1) * rows]
            block = block + got[pl.ds(pl.multiple_of(at * rows, rows), rows), :].astype(F32)
            if k == 0:
                own[...] = block
            elif k == 1:
                plus[...] = block.astype(BF16)
            elif k == 3:
                minus[...] = block.astype(BF16)
            else:
                top[...] = block[:half].astype(BF16)
                bottom[...] = block[half:].astype(BF16)


def relay_kernel(plus, minus, from_before, from_after, plus_out, minus_out):
    half = from_before.shape[0]
    plus_out[:half] = (plus[:half].astype(F32) + from_before[...].astype(F32)).astype(BF16)
    plus_out[half:] = plus[half:]
    minus_out[:half] = minus[:half]
    minus_out[half:] = (minus[half:].astype(F32) + from_after[...].astype(F32)).astype(BF16)


def finish_kernel(own, from_before, from_after, share):
    share[...] = own[...] + from_before[...].astype(F32) + from_after[...].astype(F32)


def planes_kernel(got, out):
    comps, zn, yn, xn = out.shape
    peers = got.shape[0]
    xl = xn // peers
    f = comps * xl
    for zh in range(zn // 2):
        for c in range(comps):
            base = zh * f + c * xl
            block = jnp.concatenate(
                [got[q, base : base + xl, :] for q in range(peers)], axis=0
            ).astype(F32)
            turned = block.T
            out[c, 2 * zh] = turned[0:yn]
            out[c, 2 * zh + 1] = turned[yn : 2 * yn]


def exchange(array, axis):
    return lax.all_to_all(array, axis, split_axis=0, concat_axis=0, tiled=True)


def swap_cores(array):
    size = lax.axis_size("px")
    return lax.ppermute(array, "px", [(i, i ^ 1) for i in range(size)])


def shift_chips(forward, backward):
    size = lax.axis_size("px")
    up = [(i, (i + 2) % size) for i in range(size)]
    down = [(j, i) for i, j in up]
    return lax.ppermute(forward, "px", up), lax.ppermute(backward, "px", down)


def per_device(velocity, viscosity, implicit_inverse, row_index, row_counts, weight_in, weight_out):
    yn, zn, comps, xn = velocity.shape
    peers = lax.axis_size("pz")
    total_y = yn * peers
    xl = xn // peers
    f = comps * xl
    lanes = 2 * yn
    members, slots = row_index.shape[3:]

    v = velocity.astype(BF16).transpose(2, 1, 0, 3)
    sent = call(
        columns_kernel,
        shaped((peers, 2 * (f + xl) + HALO_ROWS, lanes), BF16),
        (
            v,
            viscosity.astype(BF16).transpose(1, 0, 2),
            row_index.reshape(members, slots).T,
            row_counts.reshape(1, members),
        ),
        scratch=[pltpu.VMEM((peers * HALO_ROWS, lanes), F32)],
    )
    inverse = implicit_inverse.astype(BF16)
    got = exchange(sent, "pz")
    solve_flops = 2 * zn * f * total_y * total_y
    edge = shaped((f, total_y), BF16)
    x_edge = shaped((zn * comps, total_y), F32)
    ids_all = shaped((peers, 8, lanes), jnp.int32)
    v, w, xlo, xhi, zlo, zhi, ids = call(
        spread_kernel,
        (shaped((zn * f, total_y), BF16), shaped((zn * xl, total_y), BF16))
        + (x_edge, x_edge, edge, edge, ids_all),
        (got,),
    )
    zlo, zhi = shift((zhi, zlo), ("px", "tr"))
    message = shaped((members, f, peers * slots), BF16)
    sample_flops = 2 * peers * f * 256 * members * slots
    sampling = [
        pltpu.VMEM((peers, 2 * f, lanes), BF16),
        pltpu.VMEM((peers, f, members * slots), F32),
        pltpu.VMEM(message.shape, BF16),
    ]
    u, w_far, ids_far, packed, z_first, z_last, x_first, x_last = call(
        first_kernel,
        (shaped((zn * f, total_y), F32), shaped(w.shape, BF16), ids_all)
        + (shaped((peers, 2 * f, lanes), BF16), edge, edge, x_edge, x_edge),
        (v, w, xlo, xhi, zlo, zhi, ids, inverse),
        scratch=[
            pltpu.VMEM((zn * f, total_y), BF16),
            pltpu.VMEM((zn * f, total_y), F32),
            pltpu.VMEM(inverse.shape, BF16),
            pltpu.SemaphoreType.DMA((4,)),
        ],
        flops=solve_flops,
        far_in=(7,),
        far_out=(0, 1, 2),
    )
    zlo, zhi = shift((z_last, z_first), ("px", "tr"))
    xlo, xhi = shift((x_last, x_first), "pz")
    sent = call(
        sample_kernel,
        message,
        (packed, ids),
        scratch=sampling[1:] + [pltpu.SemaphoreType.DMA((6,))],
        flops=sample_flops,
        far_out=(0,),
    )
    sent, zlo, zhi, xlo, xhi = lax.optimization_barrier((sent, zlo, zhi, xlo, xhi))
    rows_in = exchange(sent, ("pz", "tr"))
    packed, sent = call(
        second_kernel,
        (shaped((peers, 2 * f, lanes), BF16), message),
        (u, w_far, ids_far, zlo, zhi, xlo, xhi, inverse),
        scratch=[
            pltpu.VMEM((zn * f, total_y), BF16),
            pltpu.VMEM((zn * f, total_y), F32),
            pltpu.VMEM(w.shape, BF16),
            pltpu.VMEM(ids_all.shape, jnp.int32),
            pltpu.VMEM(edge.shape, BF16),
            pltpu.VMEM(edge.shape, BF16),
            pltpu.VMEM(x_edge.shape, F32),
            pltpu.VMEM(x_edge.shape, F32),
            pltpu.VMEM(inverse.shape, BF16),
        ]
        + sampling
        + [pltpu.SemaphoreType.DMA((20,))],
        flops=solve_flops + sample_flops,
        far_in=range(8),
        far_out=(0, 1),
    )
    sent, rows_in = lax.optimization_barrier((sent, rows_in))
    rows_target = exchange(sent, ("pz", "tr"))
    packed, rows_target = lax.optimization_barrier((packed, rows_target))
    planes = exchange(packed, "pz")

    member_in = weight_in[0]
    member_out = weight_out[0]
    width, hid = member_in.shape
    batch = 2 * peers * slots
    spots = lax.axis_size("px")
    loss_scale = 1.0 / math.sqrt(spots * batch)
    matmul_flops = 2 * hid * width * batch
    x, hidden, slope, predicted = call(
        forward_kernel,
        (
            shaped((width, batch), BF16),
            shaped((hid, batch), BF16),
            shaped((hid, batch), BF16),
            shaped((width, batch), F32),
        ),
        (rows_in, member_in.T, member_out.T),
        scratch=[
            pltpu.VMEM(message.shape, BF16),
            pltpu.VMEM((width, batch), BF16),
            pltpu.VMEM((hid, batch), BF16),
            pltpu.VMEM((hid, batch), BF16),
            pltpu.VMEM((width, batch), F32),
            pltpu.SemaphoreType.DMA((5,)),
        ],
        flops=2 * matmul_flops,
        far_in=(0,),
        far_out=range(4),
    )
    position = lax.axis_index("px")
    place = jnp.stack([position % 2, position // 2]).astype(jnp.int32)

    def delta_out(*refs):
        delta_out_kernel(loss_scale, *refs)

    d, away_out = call(
        delta_out,
        (shaped((width, batch), BF16), shaped((hid // 2, width), BF16)),
        (place, rows_target, predicted, hidden),
        scratch=[
            pltpu.VMEM(message.shape, BF16),
            pltpu.VMEM((width, batch), F32),
            pltpu.VMEM((hid, batch), BF16),
            pltpu.SemaphoreType.DMA((5,)),
        ],
        flops=matmul_flops // 2,
        far_in=(1, 2, 3),
    )
    got_out = swap_cores(away_out)
    din, away_in = call(
        delta_in_kernel,
        (shaped((hid, batch), BF16), shaped((width // 2, hid), BF16)),
        (place, d, slope, member_out, x),
        flops=matmul_flops * 3 // 2,
    )
    got_in = swap_cores(away_in)

    def keep(array, right, got):
        rows, wide = got.shape[0] // 4, got.shape[1]
        block = shaped((rows, wide), BF16)
        part = shaped((rows // 2, wide), BF16)
        return call(
            keep_kernel,
            (shaped((rows, wide), F32), block, block, part, part),
            (place, array, right, got),
            flops=matmul_flops // 2,
        )

    def relay(plus, minus, arrived):
        block = shaped(plus.shape, BF16)
        return call(relay_kernel, (block, block), (plus, minus, *arrived))

    def finish(own, arrived):
        return call(finish_kernel, shaped(own.shape, F32), (own, *arrived))

    own_out, *sides_out, top, bottom = keep(hidden, d, got_out)
    top, got_in = lax.optimization_barrier((top, got_in))
    arrived_out = shift_chips(top, bottom)
    own_in, *sides_in, top, bottom = keep(x, din, got_in)
    arrived_in = shift_chips(top, bottom)
    sides_out = relay(*sides_out, arrived_out)
    sides_out, arrived_in = lax.optimization_barrier((sides_out, arrived_in))
    arrived_out = shift_chips(*sides_out)
    arrived_in = shift_chips(*relay(*sides_in, arrived_in))
    share_out = finish(own_out, arrived_out)
    share_in = finish(own_in, arrived_in)
    result = call(planes_kernel, shaped((comps, zn, yn, xn), F32), (planes,))
    return (result.transpose(2, 1, 0, 3), share_in[None], share_out[None])


def solution(mesh):
    in_specs = (
        P("pz", ("px", "tr"), None, None),
        P("pz", ("px", "tr"), None),
        P(),
        P("px", "pz", "tr", None, None),
        P("px", "pz", "tr", None),
        P(("pz", "tr"), None, None),
        P(("pz", "tr"), None, None),
    )
    out_specs = (
        P("pz", ("px", "tr"), None, None),
        P(("pz", "tr"), "px", None),
        P(("pz", "tr"), "px", None),
    )
    return jax.shard_map(
        per_device, mesh=mesh, in_specs=in_specs, out_specs=out_specs, check_vma=False
    )
```

```python
import math

import jax
import jax.numpy as jnp
from jax import lax
from jax.experimental import pallas as pl
from jax.experimental.pallas import tpu as pltpu
from jax.sharding import PartitionSpec as P

diffusion_factor = 0.08
F32 = jnp.float32
BF16 = jnp.bfloat16
MIB = 1 << 20


def call(kernel, out_shape, args, scratch=(), flops=1e6, far_in=(), far_out=(), aliases=None):
    outs = jax.tree.leaves(out_shape)
    size = lambda x: math.prod(x.shape) * jnp.dtype(x.dtype).itemsize
    near = [x for k, x in enumerate(args) if k not in far_in]
    near += [x for k, x in enumerate(outs) if k not in far_out]
    held = sum(size(x) for x in near) + sum(size(x) for x in scratch if x.dtype in (F32, BF16, jnp.int32))

    def spec(k, far, scalar=False):
        space = pltpu.HBM if k in far else pltpu.SMEM if scalar else pltpu.VMEM
        return pl.BlockSpec(memory_space=space)

    out_specs = tuple(spec(k, far_out) for k in range(len(outs)))
    args = [
        pltpu.with_memory_space_constraint(x, pltpu.HBM) if k in far_in else x
        for k, x in enumerate(args)
    ]
    pinned = tuple(
        pltpu.HBM(x.shape, x.dtype) if k in far_out else x for k, x in enumerate(outs)
    )
    return pl.pallas_call(
        kernel,
        out_shape=pinned if isinstance(out_shape, tuple) else pinned[0],
        in_specs=[spec(k, far_in, x.ndim == 1) for k, x in enumerate(args)],
        out_specs=out_specs if isinstance(out_shape, tuple) else out_specs[0],
        scratch_shapes=list(scratch),
        input_output_aliases=aliases or {},
        compiler_params=pltpu.CompilerParams(vmem_limit_bytes=held + 6 * MIB),
        cost_estimate=pl.CostEstimate(
            flops=int(flops),
            bytes_accessed=int(sum(size(x) for x in list(args) + outs)),
            transcendentals=0,
        ),
    )(*args)


class Copies:
    def __init__(self, sems):
        self.sems, self.used, self.open = sems, 0, []

    def start(self, source, target):
        copy = pltpu.make_async_copy(source, target, self.sems.at[self.used])
        copy.start()
        self.used += 1
        self.open.append(copy)
        return copy

    def finish(self):
        for copy in self.open:
            copy.wait()
        self.open = []

    def wait(self, copy):
        copy.wait()
        self.open.remove(copy)


def shaped(shape, dtype):
    return jax.ShapeDtypeStruct(shape, dtype)


def shift(array, axis, wrap=True):
    last, first = array
    size = lax.axis_size(axis)
    up = [(i, (i + 1) % size) for i in range(size if wrap else size - 1)]
    down = [(j, i) for i, j in up]
    return lax.ppermute(last, axis, up), lax.ppermute(first, axis, down)


HALO_ROWS = 24
GROUP = 8


def columns_kernel(v, w, index, counts, out, edge):
    comps, zn, yn, xn = v.shape
    peers = out.shape[0]
    xl = xn // peers
    lanes_of = out.shape[2]
    half = (comps + 1) * xl
    for zh in range(zn // 2):
        for c in range(comps + 1):
            source = w if c == comps else v.at[c]
            pair = [source[z].astype(F32) for z in (2 * zh, 2 * zh + 1)]
            turned = jnp.concatenate(pair, axis=0).T
            base = zh * half + c * xl
            for q in range(peers):
                out[q, base : base + xl, :] = turned[q * xl : (q + 1) * xl].astype(BF16)
            if c == comps:
                continue
            for q in range(peers):
                before = (q * xl - 1) % xn
                after = (q + 1) * xl % xn
                r = q * HALO_ROWS + zh * comps + c
                edge[r : r + 1] = turned[before : before + 1]
                edge[r + zn // 2 * comps : r + zn // 2 * comps + 1] = turned[after : after + 1]
    start = zn // 2 * half
    slots, members = index.shape
    slot = lax.broadcasted_iota(jnp.int32, (slots, members), 0)
    live = jnp.where(slot < counts[...], index[...], -1).astype(F32)
    sides = lanes_of // members
    rows = slots // sides
    numbers = jnp.concatenate([live[k * rows : (k + 1) * rows] for k in range(sides)], axis=1)
    numbers = jnp.concatenate([numbers, jnp.zeros((8 - rows, lanes_of), F32)], axis=0)
    for q in range(peers):
        edge[(q + 1) * HALO_ROWS - 8 : (q + 1) * HALO_ROWS] = numbers
        out[q, start : start + HALO_ROWS, :] = edge[
            q * HALO_ROWS : (q + 1) * HALO_ROWS
        ].astype(BF16)


def solve(e, a):
    return lax.dot_general(
        e[...], a[...], (((1,), (1,)), ((), ())), preferred_element_type=F32
    )


def pack_columns(u, packed, zn):
    pairs, _, rows, lanes = packed.shape
    f = rows // (zn // 2)
    yn = lanes // 2
    low = lax.broadcasted_iota(jnp.int32, (f, lanes), 1) < yn
    for j in range(pairs):
        for zh in range(zn // 2):
            first = u[(2 * zh) * f : (2 * zh + 1) * f, j * lanes : (j + 1) * lanes]
            second = u[(2 * zh + 1) * f : (2 * zh + 2) * f, j * lanes : (j + 1) * lanes]
            even = jnp.where(low, first, pltpu.roll(second, yn, 1))
            odd = jnp.where(low, pltpu.roll(first, yn, 1), second)
            packed[j, 0, zh * f : (zh + 1) * f, :] = even.astype(BF16)
            packed[j, 1, zh * f : (zh + 1) * f, :] = odd.astype(BF16)


def spread_kernel(got, v, w, xlo, xhi, zlo, zhi, ids):
    peers, rows, lanes = got.shape
    table = got[:, rows - 8 :, :].astype(F32).reshape(peers * 8, lanes).astype(BF16)
    members = 32
    per = lanes // GROUP
    source = lax.broadcasted_iota(jnp.int32, (lanes, lanes), 0)
    lane = lax.broadcasted_iota(jnp.int32, (lanes, lanes), 1)
    late = lax.broadcasted_iota(jnp.int32, (1, lanes), 1) % GROUP >= GROUP // 2
    halves = members // per
    for mh in range(halves):
        wanted = (lane % (GROUP // 2)) * members + mh * per + lane // GROUP
        moved = jnp.dot(
            table, jnp.where(source == wanted, 1.0, 0.0).astype(BF16), preferred_element_type=F32
        )
        for q in range(peers):
            for kg in range(3):
                r = q * 8 + 2 * kg
                line = jnp.where(late, moved[r + 1 : r + 2], moved[r : r + 1])
                at = kg * halves + mh
                ids[q, at : at + 1, :] = line.astype(jnp.int32)
    yn = lanes // 2
    zn = 4
    half = (rows - HALO_ROWS) // 2
    xl = w.shape[0] // zn
    f = half - xl
    comps = f // xl
    low = lax.broadcasted_iota(jnp.int32, (rows, lanes), 1) < yn
    for j in range(peers // 2):
        one = got[2 * j].astype(F32)
        two = got[2 * j + 1].astype(F32)
        sides = (
            jnp.where(low, one, pltpu.roll(two, yn, 1)),
            jnp.where(low, pltpu.roll(one, yn, 1), two),
        )
        at = slice(j * lanes, (j + 1) * lanes)
        for zh in range(zn // 2):
            for side in range(2):
                z = 2 * zh + side
                whole = sides[side]
                v[z * f : (z + 1) * f, at] = whole[zh * half : zh * half + f].astype(BF16)
                w[z * xl : (z + 1) * xl, at] = whole[zh * half + f : (zh + 1) * half].astype(BF16)
                r = zn // 2 * half + zh * comps
                xlo[z * comps : (z + 1) * comps, at] = whole[r : r + comps]
                r = r + zn // 2 * comps
                xhi[z * comps : (z + 1) * comps, at] = whole[r : r + comps]
    zlo[...] = v[0:f]
    zhi[...] = v[(zn - 1) * f : zn * f]


def explicit_plane(z, u, w, zlo, zhi, x_before, x_after, e):
    f, cols = zlo.shape
    zn = u.shape[0] // f
    xl = w.shape[0] // zn
    comps = f // xl
    row = lax.broadcasted_iota(jnp.int32, (xl, cols), 0)
    lane = lax.broadcasted_iota(jnp.int32, (xl, cols), 1)
    factor = diffusion_factor * w[z * xl : (z + 1) * xl].astype(F32)
    for c in range(comps):
        r = z * comps + c
        at = slice(r * xl, (r + 1) * xl)
        cur = u[at].astype(F32)
        if z > 0:
            total = u[(r - comps) * xl : (r - comps + 1) * xl].astype(F32)
        else:
            total = zlo[c * xl : (c + 1) * xl].astype(F32)
        if z < zn - 1:
            total = total + u[(r + comps) * xl : (r + comps + 1) * xl].astype(F32)
        else:
            total = total + zhi[c * xl : (c + 1) * xl].astype(F32)
        total = total + jnp.where(row == 0, x_before[r : r + 1], pltpu.roll(cur, 1, 0))
        total = total + jnp.where(row == xl - 1, x_after[r : r + 1], pltpu.roll(cur, xl - 1, 0))
        total = total + jnp.where(lane == 0, 0.0, pltpu.roll(cur, 1, 1))
        total = total + jnp.where(lane == cols - 1, 0.0, pltpu.roll(cur, cols - 1, 1))
        e[at] = (cur + factor * (total - 6.0 * cur)).astype(BF16)


def first_kernel(
    v, w, xlo, xhi, zlo, zhi, a, u, packed, z_first, z_last, x_first, x_last, e
):
    x_before, x_after = xlo[...], xhi[...]
    zn = 4
    for z in range(zn):
        explicit_plane(z, v, w, zlo, zhi, x_before, x_after, e)
    u[...] = solve(e, a)
    f = zlo.shape[0]
    z_first[...] = u[0:f].astype(BF16)
    z_last[...] = u[(zn - 1) * f : zn * f].astype(BF16)
    xl = w.shape[0] // zn
    groups = u.shape[0] // xl
    for r in range(groups):
        x_first[r : r + 1] = u[r * xl : r * xl + 1]
        x_last[r : r + 1] = u[(r + 1) * xl - 1 : (r + 1) * xl]
    pack_columns(u, packed, zn)


def sample_kernel(packed, ids, sent_far, picked, sent, sems):
    copies = Copies(sems)
    sample(packed, ids, picked, sent, message_part(copies, sent, sent_far, 0))
    copies.finish()


def message_part(copies, sent, far, which):
    f = sent.shape[1]

    def ready(part):
        members, _, lanes = part
        copies.start(sent.at[part], far.at[members, pl.ds(which * f, f), lanes])

    return ready


def second_kernel(
    u, w, ids, zlo, zhi, xlo, xhi, a, sent_in, packed_far, sent_far,
    e, after, packed, picked, sent, sems,
):
    del sent_in
    copies = Copies(sems)
    zn = u.shape[0] // zlo.shape[0]
    x_before, x_after = xlo[...], xhi[...]
    for z in range(zn):
        explicit_plane(z, u, w, zlo, zhi, x_before, x_after, e)
    after[...] = solve(e, a)
    pack_columns(after, packed, zn)
    copies.start(packed, packed_far)
    sample(packed, ids, picked, sent, message_part(copies, sent, sent_far, 1))
    copies.finish()


def sample(packed, ids, picked, out, ready):
    pairs, _, rows, lanes = packed.shape
    peers = 2 * pairs
    f = rows // 2
    yn = lanes // 2
    blocks = picked.shape[2] // lanes
    r = lax.broadcasted_iota(jnp.int32, (2 * lanes, lanes), 0)
    row_id = (r % yn) * 4 + r // yn
    for q in range(peers):
        at = (q // 2, q % 2)
        table = jnp.concatenate([packed[(*at, slice(0, f))], packed[(*at, slice(f, rows))]], axis=1)
        wanted = pltpu.roll(ids[q], (GROUP * q) % lanes, 1) if q else ids[q]
        for b in range(blocks):
            hot = jnp.where(row_id == wanted[b : b + 1], 1.0, 0.0).astype(BF16)
            picked[q, :, b * lanes : (b + 1) * lanes] = jnp.dot(
                table, hot, preferred_element_type=F32
            )
    group = lax.broadcasted_iota(jnp.int32, (f, lanes), 1) // GROUP
    per = lanes // GROUP
    halves = out.shape[0] // per
    for b in range(blocks):
        kg, mh = b // halves, b % halves
        held = [picked[q, :, b * lanes : (b + 1) * lanes] for q in range(peers)]
        step = 1
        while step < peers:
            take = (group // step) % 2 == 1
            held = [jnp.where(take, held[(i + step) % peers], held[i]) for i in range(peers)]
            step *= 2
        for ml in range(per):
            out[mh * per + ml, :, kg * lanes : (kg + 1) * lanes] = held[(-ml) % peers].astype(BF16)
        ready((pl.ds(mh * per, per), slice(None), pl.ds(kg * lanes, lanes)))


def gather_rows(got, start, turned, comps=3):
    sources, both, slots = got.shape
    sides = 2
    peers = sources // sides
    xl = both // 2 // comps
    for q in range(peers):
        for side in range(sides):
            for c in range(comps):
                at = (c * peers + q) * xl
                turned[at : at + xl, side * slots : (side + 1) * slots] = got[
                    q * sides + side, start + c * xl : start + (c + 1) * xl
                ]


CONTRACT_ROWS = (((1,), (1,)), ((), ()))


def over_rows(left, right):
    return lax.dot_general(left, right, CONTRACT_ROWS, preferred_element_type=F32)


def forward_kernel(
    scale, place, got_far, w_in_far, w_out_far, x, hidden, slope, d, away,
    got, w_in, w_out, sems,
):
    copies = Copies(sems)
    f = got.shape[1] // 2
    input_part = (slice(None), pl.ds(0, f), slice(None))
    target_part = (slice(None), pl.ds(f, f), slice(None))
    first = [copies.start(got_far.at[input_part], got.at[input_part])]
    wide = 256
    count = hidden.shape[0] // wide
    for i in range(count):
        at = pl.ds(i * wide, wide)
        first.append(copies.start(w_in_far.at[at], w_in.at[at]))
    w_out_copy = copies.start(w_out_far, w_out)
    target_copy = copies.start(got_far.at[target_part], got.at[target_part])
    copies.wait(first[0])
    gather_rows(got, 0, x)
    for i in range(count):
        copies.wait(first[1 + i])
        at = slice(i * wide, (i + 1) * wide)
        pre = jnp.dot(w_in[at, :], x[...], preferred_element_type=F32)
        logistic = jax.nn.sigmoid(pre)
        hidden[at, :] = (pre * logistic).astype(BF16)
        slope[at, :] = (logistic * (1.0 + pre * (1.0 - logistic))).astype(slope.dtype)
    copies.wait(w_out_copy)
    copies.wait(target_copy)
    gather_rows(got, f, d)
    for i in range(d.shape[0] // wide):
        at = slice(i * wide, (i + 1) * wide)
        predicted = jnp.dot(w_out[at, :], hidden[...], preferred_element_type=F32)
        d[at] = ((predicted - d[at].astype(F32)) * scale).astype(BF16)
    away_blocks(hidden, d, place[0], away, away.shape[0] // 4)


def block_rows(array, y, core, rows):
    return array[pl.ds(pl.multiple_of((2 * y + core) * rows, rows), rows), :]


def away_blocks(array, right, core, away, rows):
    left = jnp.concatenate([block_rows(array, y, 1 - core, rows) for y in range(4)], axis=0)
    away[...] = over_rows(left, right[...]).astype(BF16)


def delta_in_kernel(place, d, slope, w_out, x, din, away):
    wide = 256

    def chunk(i, carry):
        at = pl.ds(pl.multiple_of(i * wide, wide), wide)
        back = jnp.dot(w_out[at, :], d[...], preferred_element_type=F32)
        din[at, :] = (back * slope[at, :].astype(F32)).astype(BF16)
        return carry

    lax.fori_loop(0, din.shape[0] // wide, chunk, 0)
    away_blocks(x, din, place[0], away, away.shape[0] // 4)


def keep_kernel(place, array, right, got, own, plus, minus, top, bottom):
    core, y = place[0], place[1]
    rows = own.shape[0]
    half = rows // 2
    for ks in ((2, 1, 3, 0),):
        ys = [lax.rem(y + k, 4) for k in ks]
        blocks = jnp.concatenate([block_rows(array, at, core, rows) for at in ys], axis=0)
        value = over_rows(blocks, right[...])
        for n, (k, at) in enumerate(zip(ks, ys)):
            block = value[n * rows : (n + 1) * rows]
            block = block + got[pl.ds(pl.multiple_of(at * rows, rows), rows), :].astype(F32)
            if k == 0:
                own[...] = block
            elif k == 1:
                plus[...] = block.astype(BF16)
            elif k == 3:
                minus[...] = block.astype(BF16)
            else:
                top[...] = block[:half].astype(BF16)
                bottom[...] = block[half:].astype(BF16)


def relay_kernel(plus, minus, from_before, from_after, plus_out, minus_out):
    half = from_before.shape[0]
    plus_out[:half] = (plus[:half].astype(F32) + from_before[...].astype(F32)).astype(BF16)
    plus_out[half:] = plus[half:]
    minus_out[:half] = minus[:half]
    minus_out[half:] = (minus[half:].astype(F32) + from_after[...].astype(F32)).astype(BF16)


def finish_kernel(own, from_before, from_after, share):
    share[...] = own[...] + from_before[...].astype(F32) + from_after[...].astype(F32)


def planes_kernel(got, out):
    comps, zn, yn, xn = out.shape
    peers = got.shape[0]
    xl = xn // peers
    f = comps * xl
    for zh in range(zn // 2):
        for c in range(comps):
            base = zh * f + c * xl
            block = jnp.concatenate(
                [got[q, base : base + xl, :] for q in range(peers)], axis=0
            ).astype(F32)
            turned = block.T
            out[c, 2 * zh] = turned[0:yn]
            out[c, 2 * zh + 1] = turned[yn : 2 * yn]


def exchange(array, axis):
    return lax.all_to_all(array, axis, split_axis=0, concat_axis=0, tiled=True)


def swap_cores(array):
    size = lax.axis_size("px")
    return lax.ppermute(array, "px", [(i, i ^ 1) for i in range(size)])


def shift_chips(forward, backward):
    size = lax.axis_size("px")
    up = [(i, (i + 2) % size) for i in range(size)]
    down = [(j, i) for i, j in up]
    return lax.ppermute(forward, "px", up), lax.ppermute(backward, "px", down)


def per_device(velocity, viscosity, implicit_inverse, row_index, row_counts, weight_in, weight_out):
    yn, zn, comps, xn = velocity.shape
    peers = lax.axis_size("pz")
    total_y = yn * peers
    xl = xn // peers
    f = comps * xl
    lanes = 2 * yn
    members, slots = row_index.shape[3:]

    v = velocity.astype(BF16).transpose(2, 1, 0, 3)
    sent = call(
        columns_kernel,
        shaped((peers, 2 * (f + xl) + HALO_ROWS, lanes), BF16),
        (
            v,
            viscosity.astype(BF16).transpose(1, 0, 2),
            row_index.reshape(members, slots).T,
            row_counts.reshape(1, members),
        ),
        scratch=[pltpu.VMEM((peers * HALO_ROWS, lanes), F32)],
    )
    inverse = implicit_inverse.astype(BF16)
    got = exchange(sent, "pz")
    solve_flops = 2 * zn * f * total_y * total_y
    edge = shaped((f, total_y), BF16)
    x_edge = shaped((zn * comps, total_y), F32)
    ids_all = shaped((peers, 8, lanes), jnp.int32)
    v, w, xlo, xhi, zlo, zhi, ids = call(
        spread_kernel,
        (shaped((zn * f, total_y), BF16), shaped((zn * xl, total_y), BF16))
        + (x_edge, x_edge, edge, edge, ids_all),
        (got,),
    )
    zlo, zhi = shift((zhi, zlo), ("px", "tr"))
    message = shaped((members, f, peers * slots), BF16)
    both = shaped((members, 2 * f, peers * slots), BF16)
    sample_flops = 2 * peers * f * 256 * members * slots
    sampling = [
        pltpu.VMEM((peers, 2 * f, lanes), BF16),
        pltpu.VMEM((peers, f, members * slots), F32),
        pltpu.VMEM(message.shape, BF16),
    ]
    blocks = shaped((peers // 2, 2, 2 * f, lanes), BF16)
    half_blocks = shaped((peers // 2, 2 * f, lanes), BF16)
    sampling[0] = pltpu.VMEM(blocks.shape, BF16)
    u, packed, z_first, z_last, x_first, x_last = call(
        first_kernel,
        (shaped((zn * f, total_y), F32), blocks, edge, edge, x_edge, x_edge),
        (v, w, xlo, xhi, zlo, zhi, inverse),
        scratch=[pltpu.VMEM((zn * f, total_y), BF16)],
        flops=solve_flops,
    )
    zlo, zhi = shift((z_last, z_first), ("px", "tr"))
    xlo, xhi = shift((x_last, x_first), "pz")
    sent = call(
        sample_kernel,
        both,
        (packed, ids),
        scratch=sampling[1:] + [pltpu.SemaphoreType.DMA((6,))],
        flops=sample_flops,
        far_out=(0,),
    )
    packed, sent = call(
        second_kernel,
        (blocks, both),
        (u, w, ids, zlo, zhi, xlo, xhi, inverse, sent),
        scratch=[pltpu.VMEM((zn * f, total_y), BF16), pltpu.VMEM((zn * f, total_y), F32)]
        + sampling
        + [pltpu.SemaphoreType.DMA((7,))],
        flops=solve_flops + sample_flops,
        far_in=(8,),
        far_out=(0, 1),
        aliases={8: 1},
    )
    rows_all = exchange(sent, ("pz", "tr"))
    packed, rows_all = lax.optimization_barrier((packed, rows_all))
    planes = exchange(packed.reshape(peers, 2 * f, lanes), "pz")

    member_in = weight_in[0]
    member_out = weight_out[0]
    width, hid = member_in.shape
    batch = 2 * peers * slots
    spots = lax.axis_size("px")
    loss_scale = 1.0 / math.sqrt(spots * batch)
    matmul_flops = 2 * hid * width * batch
    position = lax.axis_index("px")
    place = jnp.stack([position & 1, position >> 1]).astype(jnp.int32)

    def forward(*refs):
        forward_kernel(loss_scale, *refs)

    x, hidden, slope, d, away_out = call(
        forward,
        (
            shaped((width, batch), BF16),
            shaped((hid, batch), BF16),
            shaped((hid, batch), BF16),
            shaped((width, batch), BF16),
            shaped((hid // 2, width), BF16),
        ),
        (place, rows_all, member_in.T, member_out.T),
        scratch=[
            pltpu.VMEM(both.shape, BF16),
            pltpu.VMEM((hid, width), BF16),
            pltpu.VMEM((width, hid), BF16),
            pltpu.SemaphoreType.DMA((8,)),
        ],
        flops=matmul_flops * 5 // 2,
        far_in=(1, 2, 3),
    )
    got_out = swap_cores(away_out)
    din, away_in = call(
        delta_in_kernel,
        (shaped((hid, batch), BF16), shaped((width // 2, hid), BF16)),
        (place, d, slope, member_out, x),
        flops=matmul_flops * 3 // 2,
    )
    got_in = swap_cores(away_in)
    planes, got_out = lax.optimization_barrier((planes, got_out))

    def keep(array, right, got):
        rows, wide = got.shape[0] // 4, got.shape[1]
        block = shaped((rows, wide), BF16)
        part = shaped((rows // 2, wide), BF16)
        return call(
            keep_kernel,
            (shaped((rows, wide), F32), block, block, part, part),
            (place, array, right, got),
            flops=matmul_flops // 2,
        )

    def relay(plus, minus, arrived):
        block = shaped(plus.shape, BF16)
        return call(relay_kernel, (block, block), (plus, minus, *arrived))

    def finish(own, arrived):
        return call(finish_kernel, shaped(own.shape, F32), (own, *arrived))

    own_out, *sides_out, top, bottom = keep(hidden, d, got_out)
    top, got_in = lax.optimization_barrier((top, got_in))
    arrived_out = shift_chips(top, bottom)
    own_in, *sides_in, top, bottom = keep(x, din, got_in)
    arrived_in = shift_chips(top, bottom)
    sides_out = relay(*sides_out, arrived_out)
    sides_out, arrived_in = lax.optimization_barrier((sides_out, arrived_in))
    arrived_out = shift_chips(*sides_out)
    arrived_in = shift_chips(*relay(*sides_in, arrived_in))
    share_out = finish(own_out, arrived_out)
    share_in = finish(own_in, arrived_in)
    result = call(planes_kernel, shaped((comps, zn, yn, xn), F32), (planes,), flops=3e10)
    return (result.transpose(2, 1, 0, 3), share_in[None], share_out[None])


def solution(mesh):
    in_specs = (
        P("pz", ("px", "tr"), None, None),
        P("pz", ("px", "tr"), None),
        P(),
        P("px", "pz", "tr", None, None),
        P("px", "pz", "tr", None),
        P(("pz", "tr"), None, None),
        P(("pz", "tr"), None, None),
    )
    out_specs = (
        P("pz", ("px", "tr"), None, None),
        P(("pz", "tr"), "px", None),
        P(("pz", "tr"), "px", None),
    )
    return jax.shard_map(
        per_device, mesh=mesh, in_specs=in_specs, out_specs=out_specs, check_vma=False
    )
```

```python
import math

import jax
import jax.numpy as jnp
from jax import lax
from jax.experimental import pallas as pl
from jax.experimental.pallas import tpu as pltpu
from jax.sharding import PartitionSpec as P

diffusion_factor = 0.08
F32 = jnp.float32
BF16 = jnp.bfloat16
MIB = 1 << 20


def call(kernel, out_shape, args, scratch=(), flops=1e6, far_in=(), far_out=(), aliases=None):
    outs = jax.tree.leaves(out_shape)
    size = lambda x: math.prod(x.shape) * jnp.dtype(x.dtype).itemsize
    near = [x for k, x in enumerate(args) if k not in far_in]
    near += [x for k, x in enumerate(outs) if k not in far_out]
    held = sum(size(x) for x in near) + sum(size(x) for x in scratch if x.dtype in (F32, BF16, jnp.int32))

    def spec(k, far, scalar=False):
        space = pltpu.HBM if k in far else pltpu.SMEM if scalar else pltpu.VMEM
        return pl.BlockSpec(memory_space=space)

    out_specs = tuple(spec(k, far_out) for k in range(len(outs)))
    args = [
        pltpu.with_memory_space_constraint(x, pltpu.HBM) if k in far_in else x
        for k, x in enumerate(args)
    ]
    pinned = tuple(
        pltpu.HBM(x.shape, x.dtype) if k in far_out else x for k, x in enumerate(outs)
    )
    return pl.pallas_call(
        kernel,
        out_shape=pinned if isinstance(out_shape, tuple) else pinned[0],
        in_specs=[spec(k, far_in, x.ndim == 1) for k, x in enumerate(args)],
        out_specs=out_specs if isinstance(out_shape, tuple) else out_specs[0],
        scratch_shapes=list(scratch),
        input_output_aliases=aliases or {},
        compiler_params=pltpu.CompilerParams(vmem_limit_bytes=held + 6 * MIB),
        cost_estimate=pl.CostEstimate(
            flops=int(flops),
            bytes_accessed=int(sum(size(x) for x in list(args) + outs)),
            transcendentals=0,
        ),
    )(*args)


class Copies:
    def __init__(self, sems):
        self.sems, self.used, self.open = sems, 0, []

    def start(self, source, target):
        copy = pltpu.make_async_copy(source, target, self.sems.at[self.used])
        copy.start()
        self.used += 1
        self.open.append(copy)
        return copy

    def finish(self):
        for copy in self.open:
            copy.wait()
        self.open = []

    def wait(self, copy):
        copy.wait()
        self.open.remove(copy)


def shaped(shape, dtype):
    return jax.ShapeDtypeStruct(shape, dtype)


def shift(array, axis, wrap=True):
    last, first = array
    size = lax.axis_size(axis)
    up = [(i, (i + 1) % size) for i in range(size if wrap else size - 1)]
    down = [(j, i) for i, j in up]
    return lax.ppermute(last, axis, up), lax.ppermute(first, axis, down)


HALO_ROWS = 24
GROUP = 8


def columns_kernel(v_far, w_far, index_far, counts_far, out, v, w, index, counts, edge, sems):
    copies = Copies(sems)
    for far, near in ((index_far, index), (counts_far, counts), (w_far, w), (v_far, v)):
        copies.start(far, near)
    copies.finish()
    yn, comps, zn, xn = v.shape
    peers = out.shape[0]
    xl = xn // peers
    lanes_of = out.shape[2]
    half = (comps + 1) * xl
    for zh in range(zn // 2):
        for c in range(comps + 1):
            pair = [w[:, z, :] if c == comps else v[:, c, z, :] for z in (2 * zh, 2 * zh + 1)]
            turned = jnp.concatenate(pair, axis=0).T
            base = zh * half + c * xl
            for q in range(peers):
                out[q, base : base + xl, :] = turned[q * xl : (q + 1) * xl].astype(BF16)
            if c == comps:
                continue
            for q in range(peers):
                before = (q * xl - 1) % xn
                after = (q + 1) * xl % xn
                r = q * HALO_ROWS + zh * comps + c
                edge[r : r + 1] = turned[before : before + 1]
                edge[r + zn // 2 * comps : r + zn // 2 * comps + 1] = turned[after : after + 1]
    start = zn // 2 * half
    slots, members = index.shape
    slot = lax.broadcasted_iota(jnp.int32, (slots, members), 0)
    live = jnp.where(slot < counts[...], index[...], -1).astype(F32)
    sides = lanes_of // members
    rows = slots // sides
    numbers = jnp.concatenate([live[k * rows : (k + 1) * rows] for k in range(sides)], axis=1)
    numbers = jnp.concatenate([numbers, jnp.zeros((8 - rows, lanes_of), F32)], axis=0)
    for q in range(peers):
        edge[(q + 1) * HALO_ROWS - 8 : (q + 1) * HALO_ROWS] = numbers
        out[q, start : start + HALO_ROWS, :] = edge[
            q * HALO_ROWS : (q + 1) * HALO_ROWS
        ].astype(BF16)


def solve(e, a):
    return lax.dot_general(
        e[...], a[...], (((1,), (1,)), ((), ())), preferred_element_type=F32
    )


def pack_columns(u, packed, zn):
    pairs, _, rows, lanes = packed.shape
    f = rows // (zn // 2)
    yn = lanes // 2
    low = lax.broadcasted_iota(jnp.int32, (f, lanes), 1) < yn
    for j in range(pairs):
        for zh in range(zn // 2):
            first = u[(2 * zh) * f : (2 * zh + 1) * f, j * lanes : (j + 1) * lanes]
            second = u[(2 * zh + 1) * f : (2 * zh + 2) * f, j * lanes : (j + 1) * lanes]
            even = jnp.where(low, first, pltpu.roll(second, yn, 1))
            odd = jnp.where(low, pltpu.roll(first, yn, 1), second)
            packed[j, 0, zh * f : (zh + 1) * f, :] = even.astype(BF16)
            packed[j, 1, zh * f : (zh + 1) * f, :] = odd.astype(BF16)


def spread_kernel(got, v, w, xlo, xhi, zlo, zhi, ids):
    peers, rows, lanes = got.shape
    table = got[:, rows - 8 :, :].astype(F32).reshape(peers * 8, lanes).astype(BF16)
    members = 32
    per = lanes // GROUP
    source = lax.broadcasted_iota(jnp.int32, (lanes, lanes), 0)
    lane = lax.broadcasted_iota(jnp.int32, (lanes, lanes), 1)
    late = lax.broadcasted_iota(jnp.int32, (1, lanes), 1) % GROUP >= GROUP // 2
    halves = members // per
    for mh in range(halves):
        wanted = (lane % (GROUP // 2)) * members + mh * per + lane // GROUP
        moved = jnp.dot(
            table, jnp.where(source == wanted, 1.0, 0.0).astype(BF16), preferred_element_type=F32
        )
        for q in range(peers):
            for kg in range(3):
                r = q * 8 + 2 * kg
                line = jnp.where(late, moved[r + 1 : r + 2], moved[r : r + 1])
                at = kg * halves + mh
                ids[q, at : at + 1, :] = line.astype(jnp.int32)
    yn = lanes // 2
    zn = 4
    half = (rows - HALO_ROWS) // 2
    xl = w.shape[0] // zn
    f = half - xl
    comps = f // xl
    low = lax.broadcasted_iota(jnp.int32, (rows, lanes), 1) < yn
    for j in range(peers // 2):
        one = got[2 * j].astype(F32)
        two = got[2 * j + 1].astype(F32)
        sides = (
            jnp.where(low, one, pltpu.roll(two, yn, 1)),
            jnp.where(low, pltpu.roll(one, yn, 1), two),
        )
        at = slice(j * lanes, (j + 1) * lanes)
        for zh in range(zn // 2):
            for side in range(2):
                z = 2 * zh + side
                whole = sides[side]
                v[z * f : (z + 1) * f, at] = whole[zh * half : zh * half + f].astype(BF16)
                w[z * xl : (z + 1) * xl, at] = whole[zh * half + f : (zh + 1) * half].astype(BF16)
                r = zn // 2 * half + zh * comps
                xlo[z * comps : (z + 1) * comps, at] = whole[r : r + comps]
                r = r + zn // 2 * comps
                xhi[z * comps : (z + 1) * comps, at] = whole[r : r + comps]
    zlo[...] = v[0:f]
    zhi[...] = v[(zn - 1) * f : zn * f]


def explicit_plane(z, u, w, zlo, zhi, x_before, x_after, e):
    f, cols = zlo.shape
    zn = u.shape[0] // f
    xl = w.shape[0] // zn
    comps = f // xl
    row = lax.broadcasted_iota(jnp.int32, (xl, cols), 0)
    lane = lax.broadcasted_iota(jnp.int32, (xl, cols), 1)
    factor = diffusion_factor * w[z * xl : (z + 1) * xl].astype(F32)
    for c in range(comps):
        r = z * comps + c
        at = slice(r * xl, (r + 1) * xl)
        cur = u[at].astype(F32)
        if z > 0:
            total = u[(r - comps) * xl : (r - comps + 1) * xl].astype(F32)
        else:
            total = zlo[c * xl : (c + 1) * xl].astype(F32)
        if z < zn - 1:
            total = total + u[(r + comps) * xl : (r + comps + 1) * xl].astype(F32)
        else:
            total = total + zhi[c * xl : (c + 1) * xl].astype(F32)
        total = total + jnp.where(row == 0, x_before[r : r + 1], pltpu.roll(cur, 1, 0))
        total = total + jnp.where(row == xl - 1, x_after[r : r + 1], pltpu.roll(cur, xl - 1, 0))
        total = total + jnp.where(lane == 0, 0.0, pltpu.roll(cur, 1, 1))
        total = total + jnp.where(lane == cols - 1, 0.0, pltpu.roll(cur, cols - 1, 1))
        e[at] = (cur + factor * (total - 6.0 * cur)).astype(BF16)


def first_kernel(
    v, w, xlo, xhi, zlo, zhi, a, u, packed, z_first, z_last, x_first, x_last, e
):
    x_before, x_after = xlo[...], xhi[...]
    zn = 4
    for z in range(zn):
        explicit_plane(z, v, w, zlo, zhi, x_before, x_after, e)
    u[...] = solve(e, a)
    f = zlo.shape[0]
    z_first[...] = u[0:f].astype(BF16)
    z_last[...] = u[(zn - 1) * f : zn * f].astype(BF16)
    xl = w.shape[0] // zn
    groups = u.shape[0] // xl
    for r in range(groups):
        x_first[r : r + 1] = u[r * xl : r * xl + 1]
        x_last[r : r + 1] = u[(r + 1) * xl - 1 : (r + 1) * xl]
    pack_columns(u, packed, zn)


def sample_kernel(packed, ids, sent_far, picked, sent, sems):
    copies = Copies(sems)
    sample(packed, ids, picked, sent, message_part(copies, sent, sent_far, 0))
    copies.finish()


def message_part(copies, sent, far, which):
    f = sent.shape[1]

    def ready(part):
        members, _, lanes = part
        copies.start(sent.at[part], far.at[members, pl.ds(which * f, f), lanes])

    return ready


def second_kernel(
    u, w, ids, zlo, zhi, xlo, xhi, a, sent_in, packed_far, sent_far,
    e, after, packed, picked, sent, sems,
):
    del sent_in
    copies = Copies(sems)
    zn = u.shape[0] // zlo.shape[0]
    x_before, x_after = xlo[...], xhi[...]
    for z in range(zn):
        explicit_plane(z, u, w, zlo, zhi, x_before, x_after, e)
    after[...] = solve(e, a)
    pack_columns(after, packed, zn)
    copies.start(packed, packed_far)
    sample(packed, ids, picked, sent, message_part(copies, sent, sent_far, 1))
    copies.finish()


def sample(packed, ids, picked, out, ready):
    pairs, _, rows, lanes = packed.shape
    peers = 2 * pairs
    f = rows // 2
    yn = lanes // 2
    blocks = picked.shape[2] // lanes
    r = lax.broadcasted_iota(jnp.int32, (2 * lanes, lanes), 0)
    row_id = (r % yn) * 4 + r // yn
    for q in range(peers):
        at = (q // 2, q % 2)
        table = jnp.concatenate([packed[(*at, slice(0, f))], packed[(*at, slice(f, rows))]], axis=1)
        wanted = pltpu.roll(ids[q], (GROUP * q) % lanes, 1) if q else ids[q]
        for b in range(blocks):
            hot = jnp.where(row_id == wanted[b : b + 1], 1.0, 0.0).astype(BF16)
            picked[q, :, b * lanes : (b + 1) * lanes] = jnp.dot(
                table, hot, preferred_element_type=F32
            )
    group = lax.broadcasted_iota(jnp.int32, (f, lanes), 1) // GROUP
    per = lanes // GROUP
    halves = out.shape[0] // per
    for b in range(blocks):
        kg, mh = b // halves, b % halves
        held = [picked[q, :, b * lanes : (b + 1) * lanes] for q in range(peers)]
        step = 1
        while step < peers:
            take = (group // step) % 2 == 1
            held = [jnp.where(take, held[(i + step) % peers], held[i]) for i in range(peers)]
            step *= 2
        for ml in range(per):
            out[mh * per + ml, :, kg * lanes : (kg + 1) * lanes] = held[(-ml) % peers].astype(BF16)
        ready((pl.ds(mh * per, per), slice(None), pl.ds(kg * lanes, lanes)))


def gather_rows(got, start, turned, comps=3):
    sources, both, slots = got.shape
    sides = 2
    peers = sources // sides
    xl = both // 2 // comps
    for q in range(peers):
        for side in range(sides):
            for c in range(comps):
                at = (c * peers + q) * xl
                turned[at : at + xl, side * slots : (side + 1) * slots] = got[
                    q * sides + side, start + c * xl : start + (c + 1) * xl
                ]


CONTRACT_ROWS = (((1,), (1,)), ((), ()))


def over_rows(left, right):
    return lax.dot_general(left, right, CONTRACT_ROWS, preferred_element_type=F32)


def forward_kernel(
    scale, place, got_far, w_in_far, w_out_far, x, hidden, slope, d, away,
    got, w_in, w_out, sems,
):
    copies = Copies(sems)
    f = got.shape[1] // 2
    input_part = (slice(None), pl.ds(0, f), slice(None))
    target_part = (slice(None), pl.ds(f, f), slice(None))
    first = [copies.start(got_far.at[input_part], got.at[input_part])]
    wide = 256
    count = hidden.shape[0] // wide
    for i in range(count):
        at = pl.ds(i * wide, wide)
        first.append(copies.start(w_in_far.at[at], w_in.at[at]))
    w_out_copy = copies.start(w_out_far, w_out)
    target_copy = copies.start(got_far.at[target_part], got.at[target_part])
    copies.wait(first[0])
    gather_rows(got, 0, x)
    for i in range(count):
        copies.wait(first[1 + i])
        at = slice(i * wide, (i + 1) * wide)
        pre = jnp.dot(w_in[at, :], x[...], preferred_element_type=F32)
        logistic = jax.nn.sigmoid(pre)
        hidden[at, :] = (pre * logistic).astype(BF16)
        slope[at, :] = (logistic * (1.0 + pre * (1.0 - logistic))).astype(slope.dtype)
    copies.wait(w_out_copy)
    copies.wait(target_copy)
    gather_rows(got, f, d)
    for i in range(d.shape[0] // wide):
        at = slice(i * wide, (i + 1) * wide)
        predicted = jnp.dot(w_out[at, :], hidden[...], preferred_element_type=F32)
        d[at] = ((predicted - d[at].astype(F32)) * scale).astype(BF16)
    away_blocks(hidden, d, place[0], away, away.shape[0] // 4)


def block_rows(array, y, core, rows):
    return array[pl.ds(pl.multiple_of((2 * y + core) * rows, rows), rows), :]


def away_blocks(array, right, core, away, rows):
    left = jnp.concatenate([block_rows(array, y, 1 - core, rows) for y in range(4)], axis=0)
    away[...] = over_rows(left, right[...]).astype(BF16)


def delta_in_kernel(place, d, slope, w_out, x, din, away):
    wide = 256

    def chunk(i, carry):
        at = pl.ds(pl.multiple_of(i * wide, wide), wide)
        back = jnp.dot(w_out[at, :], d[...], preferred_element_type=F32)
        din[at, :] = (back * slope[at, :].astype(F32)).astype(BF16)
        return carry

    lax.fori_loop(0, din.shape[0] // wide, chunk, 0)
    away_blocks(x, din, place[0], away, away.shape[0] // 4)


def fold(block, rows, width):
    extra = rows - block.shape[0]
    pieces = [block[g * extra : (g + 1) * extra, width:] for g in range(block.shape[0] // extra)]
    return jnp.concatenate([block[:, :width], jnp.concatenate(pieces, axis=1)], axis=0)


def unfold(block, rows):
    extra = block.shape[0] - rows
    count = rows // extra
    wide = block.shape[1] // count
    pieces = [block[rows:, g * wide : (g + 1) * wide] for g in range(count)]
    return jnp.concatenate([block[:rows], jnp.concatenate(pieces, axis=0)], axis=1)


def own_blocks(place, copies, array_far, left):
    core, y = place[0], place[1]
    rows = left.shape[0] // 4
    started = []
    for n, k in enumerate((2, 1, 3, 0)):
        at = (2 * lax.rem(y + k, 4) + core) * rows
        source = array_far.at[pl.ds(pl.multiple_of(at, rows), rows)]
        started.append(copies.start(source, left.at[pl.ds(n * rows, rows)]))
    return started


def add_other_core(place, value, got, n, k):
    rows = value.shape[0] // 4
    at = pl.multiple_of(lax.rem(place[1] + k, 4) * rows, rows)
    return value[n * rows : (n + 1) * rows] + got[pl.ds(at, rows), :].astype(F32)


def keep_out_kernel(place, hidden_far, d_far, got, own, plus, minus, far, left, d, sems):
    copies = Copies(sems)
    copies.start(d_far, d)
    own_blocks(place, copies, hidden_far, left)
    copies.finish()
    value = over_rows(left[...], d[...])
    far[...] = add_other_core(place, value, got, 0, 2).astype(BF16)
    plus[...] = add_other_core(place, value, got, 1, 1).astype(BF16)
    minus[...] = add_other_core(place, value, got, 2, 3).astype(BF16)
    own[...] = add_other_core(place, value, got, 3, 0)


def keep_in_kernel(
    place, x_far, din, got, plus_out, minus_out, far_out, own, plus, minus, top, bottom, left, sems
):
    copies = Copies(sems)
    own_blocks(place, copies, x_far, left)
    rows, width = plus_out.shape
    half = rows // 2
    plus[0] = plus_out[...]
    minus[0] = minus_out[...]
    top[0] = far_out[:half]
    bottom[0] = far_out[half:]
    copies.finish()
    value = over_rows(left[...], din[...])
    far = fold(add_other_core(place, value, got, 0, 2), rows, width).astype(BF16)
    top[1] = far[:half]
    bottom[1] = far[half:]
    plus[1] = fold(add_other_core(place, value, got, 1, 1), rows, width).astype(BF16)
    minus[1] = fold(add_other_core(place, value, got, 2, 3), rows, width).astype(BF16)
    own[...] = add_other_core(place, value, got, 3, 0)


def relay_kernel(plus, minus, from_before, from_after, plus_out, minus_out):
    half = from_before.shape[1]
    for which in range(plus.shape[0]):
        plus_out[which, :half] = (
            plus[which, :half].astype(F32) + from_before[which].astype(F32)
        ).astype(BF16)
        plus_out[which, half:] = plus[which, half:]
        minus_out[which, :half] = minus[which, :half]
        minus_out[which, half:] = (
            minus[which, half:].astype(F32) + from_after[which].astype(F32)
        ).astype(BF16)


def finish_kernel(own_out, own_in, from_before, from_after, share_out, share_in):
    total = [from_before[k].astype(F32) + from_after[k].astype(F32) for k in range(2)]
    share_out[...] = own_out[...] + total[0]
    share_in[...] = own_in[...] + unfold(total[1], share_in.shape[0])


def planes_kernel(got, out):
    yn, comps, zn, xn = out.shape
    peers = got.shape[0]
    xl = xn // peers
    f = comps * xl
    for zh in range(zn // 2):
        for c in range(comps):
            base = zh * f + c * xl
            block = jnp.concatenate(
                [got[q, base : base + xl, :] for q in range(peers)], axis=0
            ).astype(F32)
            turned = block.T
            out[:, c, 2 * zh, :] = turned[0:yn]
            out[:, c, 2 * zh + 1, :] = turned[yn : 2 * yn]


def exchange(array, axis):
    return lax.all_to_all(array, axis, split_axis=0, concat_axis=0, tiled=True)


def swap_cores(array):
    size = lax.axis_size("px")
    return lax.ppermute(array, "px", [(i, i ^ 1) for i in range(size)])


def shift_chips(forward, backward):
    size = lax.axis_size("px")
    up = [(i, (i + 2) % size) for i in range(size)]
    down = [(j, i) for i, j in up]
    return lax.ppermute(forward, "px", up), lax.ppermute(backward, "px", down)


def per_device(velocity, viscosity, implicit_inverse, row_index, row_counts, weight_in, weight_out):
    yn, zn, comps, xn = velocity.shape
    peers = lax.axis_size("pz")
    total_y = yn * peers
    xl = xn // peers
    f = comps * xl
    lanes = 2 * yn
    members, slots = row_index.shape[3:]

    sent = call(
        columns_kernel,
        shaped((peers, 2 * (f + xl) + HALO_ROWS, lanes), BF16),
        (
            velocity.transpose(0, 2, 1, 3),
            viscosity,
            row_index.reshape(members, slots).T,
            row_counts.reshape(1, members),
        ),
        scratch=[
            pltpu.VMEM((yn, comps, zn, xn), F32),
            pltpu.VMEM((yn, zn, xn), F32),
            pltpu.VMEM((slots, members), jnp.int32),
            pltpu.VMEM((1, members), jnp.int32),
            pltpu.VMEM((peers * HALO_ROWS, lanes), F32),
            pltpu.SemaphoreType.DMA((4,)),
        ],
        far_in=range(4),
    )
    inverse = implicit_inverse.astype(BF16)
    got = exchange(sent, "pz")
    solve_flops = 2 * zn * f * total_y * total_y
    edge = shaped((f, total_y), BF16)
    x_edge = shaped((zn * comps, total_y), F32)
    ids_all = shaped((peers, 8, lanes), jnp.int32)
    v, w, xlo, xhi, zlo, zhi, ids = call(
        spread_kernel,
        (shaped((zn * f, total_y), BF16), shaped((zn * xl, total_y), BF16))
        + (x_edge, x_edge, edge, edge, ids_all),
        (got,),
    )
    zlo, zhi = shift((zhi, zlo), ("px", "tr"))
    message = shaped((members, f, peers * slots), BF16)
    both = shaped((members, 2 * f, peers * slots), BF16)
    sample_flops = 2 * peers * f * 256 * members * slots
    sampling = [
        pltpu.VMEM((peers, 2 * f, lanes), BF16),
        pltpu.VMEM((peers, f, members * slots), F32),
        pltpu.VMEM(message.shape, BF16),
    ]
    blocks = shaped((peers // 2, 2, 2 * f, lanes), BF16)
    half_blocks = shaped((peers // 2, 2 * f, lanes), BF16)
    sampling[0] = pltpu.VMEM(blocks.shape, BF16)
    u, packed, z_first, z_last, x_first, x_last = call(
        first_kernel,
        (shaped((zn * f, total_y), F32), blocks, edge, edge, x_edge, x_edge),
        (v, w, xlo, xhi, zlo, zhi, inverse),
        scratch=[pltpu.VMEM((zn * f, total_y), BF16)],
        flops=solve_flops,
    )
    zlo, zhi = shift((z_last, z_first), ("px", "tr"))
    xlo, xhi = shift((x_last, x_first), "pz")
    sent = call(
        sample_kernel,
        both,
        (packed, ids),
        scratch=sampling[1:] + [pltpu.SemaphoreType.DMA((6,))],
        flops=sample_flops,
        far_out=(0,),
    )
    packed, sent = call(
        second_kernel,
        (blocks, both),
        (u, w, ids, zlo, zhi, xlo, xhi, inverse, sent),
        scratch=[pltpu.VMEM((zn * f, total_y), BF16), pltpu.VMEM((zn * f, total_y), F32)]
        + sampling
        + [pltpu.SemaphoreType.DMA((7,))],
        flops=solve_flops + sample_flops,
        far_in=(8,),
        far_out=(0, 1),
        aliases={8: 1},
    )
    rows_all = exchange(sent, ("pz", "tr"))
    packed, rows_all = lax.optimization_barrier((packed, rows_all))
    planes = exchange(packed.reshape(peers, 2 * f, lanes), "pz")

    member_in = weight_in[0]
    member_out = weight_out[0]
    width, hid = member_in.shape
    batch = 2 * peers * slots
    spots = lax.axis_size("px")
    loss_scale = 1.0 / math.sqrt(spots * batch)
    matmul_flops = 2 * hid * width * batch
    position = lax.axis_index("px")
    place = jnp.stack([position & 1, position >> 1]).astype(jnp.int32)

    def forward(*refs):
        forward_kernel(loss_scale, *refs)

    x, hidden, slope, d, away_out = call(
        forward,
        (
            shaped((width, batch), BF16),
            shaped((hid, batch), BF16),
            shaped((hid, batch), BF16),
            shaped((width, batch), BF16),
            shaped((hid // 2, width), BF16),
        ),
        (place, rows_all, member_in.T, member_out.T),
        scratch=[
            pltpu.VMEM(both.shape, BF16),
            pltpu.VMEM((hid, width), BF16),
            pltpu.VMEM((width, hid), BF16),
            pltpu.SemaphoreType.DMA((8,)),
        ],
        flops=matmul_flops * 5 // 2,
        far_in=(1, 2, 3),
    )
    got_out = swap_cores(away_out)
    din, away_in = call(
        delta_in_kernel,
        (shaped((hid, batch), BF16), shaped((width // 2, hid), BF16)),
        (place, d, slope, member_out, x),
        flops=matmul_flops * 3 // 2,
    )
    got_in = swap_cores(away_in)
    planes, got_out = lax.optimization_barrier((planes, got_out))

    rows_out, rows_in = hid // spots, width // spots
    block = shaped((rows_out, width), BF16)
    own_out, plus, minus, far = call(
        keep_out_kernel,
        (shaped((rows_out, width), F32), block, block, block),
        (place, hidden, d, got_out),
        scratch=[
            pltpu.VMEM((hid // 2, batch), BF16),
            pltpu.VMEM((width, batch), BF16),
            pltpu.SemaphoreType.DMA((5,)),
        ],
        flops=matmul_flops // 2,
        far_in=(1, 2),
    )
    block = shaped((2, rows_out, width), BF16)
    part = shaped((2, rows_out // 2, width), BF16)
    own_in, plus, minus, top, bottom = call(
        keep_in_kernel,
        (shaped((rows_in, hid), F32), block, block, part, part),
        (place, x, din, got_in, plus, minus, far),
        scratch=[pltpu.VMEM((width // 2, batch), BF16), pltpu.SemaphoreType.DMA((4,))],
        flops=matmul_flops // 2,
        far_in=(1,),
    )
    arrived = shift_chips(top, bottom)
    plus, minus = call(relay_kernel, (block, block), (plus, minus, *arrived))
    arrived = shift_chips(plus, minus)
    share_out, share_in = call(
        finish_kernel,
        (shaped((rows_out, width), F32), shaped((rows_in, hid), F32)),
        (own_out, own_in, *arrived),
    )
    result = call(planes_kernel, shaped((yn, comps, zn, xn), F32), (planes,))
    return (result.transpose(0, 2, 1, 3), share_in[None], share_out[None])


def solution(mesh):
    in_specs = (
        P("pz", ("px", "tr"), None, None),
        P("pz", ("px", "tr"), None),
        P(),
        P("px", "pz", "tr", None, None),
        P("px", "pz", "tr", None),
        P(("pz", "tr"), None, None),
        P(("pz", "tr"), None, None),
    )
    out_specs = (
        P("pz", ("px", "tr"), None, None),
        P(("pz", "tr"), "px", None),
        P(("pz", "tr"), "px", None),
    )
    return jax.shard_map(
        per_device, mesh=mesh, in_specs=in_specs, out_specs=out_specs, check_vma=False
    )
```

```python
import math

import jax
import jax.numpy as jnp
from jax import lax
from jax.experimental import pallas as pl
from jax.experimental.pallas import tpu as pltpu
from jax.sharding import PartitionSpec as P

diffusion_factor = 0.08
F32 = jnp.float32
BF16 = jnp.bfloat16
MIB = 1 << 20


def call(kernel, out_shape, args, scratch=(), flops=1e6, far_in=(), far_out=(), aliases=None):
    outs = jax.tree.leaves(out_shape)
    size = lambda x: math.prod(x.shape) * jnp.dtype(x.dtype).itemsize
    near = [x for k, x in enumerate(args) if k not in far_in]
    near += [x for k, x in enumerate(outs) if k not in far_out]
    held = sum(size(x) for x in near) + sum(size(x) for x in scratch if x.dtype in (F32, BF16, jnp.int32))

    def spec(k, far, scalar=False):
        space = pltpu.HBM if k in far else pltpu.SMEM if scalar else pltpu.VMEM
        return pl.BlockSpec(memory_space=space)

    out_specs = tuple(spec(k, far_out) for k in range(len(outs)))
    args = [
        pltpu.with_memory_space_constraint(x, pltpu.HBM) if k in far_in else x
        for k, x in enumerate(args)
    ]
    pinned = tuple(
        pltpu.HBM(x.shape, x.dtype) if k in far_out else x for k, x in enumerate(outs)
    )
    return pl.pallas_call(
        kernel,
        out_shape=pinned if isinstance(out_shape, tuple) else pinned[0],
        in_specs=[spec(k, far_in, x.ndim == 1) for k, x in enumerate(args)],
        out_specs=out_specs if isinstance(out_shape, tuple) else out_specs[0],
        scratch_shapes=list(scratch),
        input_output_aliases=aliases or {},
        compiler_params=pltpu.CompilerParams(vmem_limit_bytes=held + 6 * MIB),
        cost_estimate=pl.CostEstimate(
            flops=int(flops),
            bytes_accessed=int(sum(size(x) for x in list(args) + outs)),
            transcendentals=0,
        ),
    )(*args)


class Copies:
    def __init__(self, sems):
        self.sems, self.used, self.open = sems, 0, []

    def start(self, source, target):
        copy = pltpu.make_async_copy(source, target, self.sems.at[self.used])
        copy.start()
        self.used += 1
        self.open.append(copy)
        return copy

    def finish(self):
        for copy in self.open:
            copy.wait()
        self.open = []

    def wait(self, copy):
        copy.wait()
        self.open.remove(copy)


def shaped(shape, dtype):
    return jax.ShapeDtypeStruct(shape, dtype)


def shift(array, axis, wrap=True):
    last, first = array
    size = lax.axis_size(axis)
    up = [(i, (i + 1) % size) for i in range(size if wrap else size - 1)]
    down = [(j, i) for i, j in up]
    return lax.ppermute(last, axis, up), lax.ppermute(first, axis, down)


HALO_ROWS = 24
GROUP = 8


def columns_kernel(v_far, w_far, index_far, counts_far, out, v, w, index, counts, edge, sems):
    copies = Copies(sems)
    for far, near in ((index_far, index), (counts_far, counts), (w_far, w), (v_far, v)):
        copies.start(far, near)
    copies.finish()
    yn, comps, zn, xn = v.shape
    peers = out.shape[0]
    xl = xn // peers
    lanes_of = out.shape[2]
    half = (comps + 1) * xl
    for zh in range(zn // 2):
        for c in range(comps + 1):
            pair = [w[:, z, :] if c == comps else v[:, c, z, :] for z in (2 * zh, 2 * zh + 1)]
            turned = jnp.concatenate(pair, axis=0).T
            base = zh * half + c * xl
            for q in range(peers):
                out[q, base : base + xl, :] = turned[q * xl : (q + 1) * xl].astype(BF16)
            if c == comps:
                continue
            for q in range(peers):
                before = (q * xl - 1) % xn
                after = (q + 1) * xl % xn
                r = q * HALO_ROWS + zh * comps + c
                edge[r : r + 1] = turned[before : before + 1]
                edge[r + zn // 2 * comps : r + zn // 2 * comps + 1] = turned[after : after + 1]
    start = zn // 2 * half
    slots, members = index.shape
    slot = lax.broadcasted_iota(jnp.int32, (slots, members), 0)
    live = jnp.where(slot < counts[...], index[...], -1).astype(F32)
    sides = lanes_of // members
    rows = slots // sides
    numbers = jnp.concatenate([live[k * rows : (k + 1) * rows] for k in range(sides)], axis=1)
    numbers = jnp.concatenate([numbers, jnp.zeros((8 - rows, lanes_of), F32)], axis=0)
    for q in range(peers):
        edge[(q + 1) * HALO_ROWS - 8 : (q + 1) * HALO_ROWS] = numbers
        out[q, start : start + HALO_ROWS, :] = edge[
            q * HALO_ROWS : (q + 1) * HALO_ROWS
        ].astype(BF16)


def solve(e, a):
    return lax.dot_general(
        e[...], a[...], (((1,), (1,)), ((), ())), preferred_element_type=F32
    )


def pack_columns(u, packed, zn):
    pairs, _, rows, lanes = packed.shape
    f = rows // (zn // 2)
    yn = lanes // 2
    low = lax.broadcasted_iota(jnp.int32, (f, lanes), 1) < yn
    for j in range(pairs):
        for zh in range(zn // 2):
            first = u[(2 * zh) * f : (2 * zh + 1) * f, j * lanes : (j + 1) * lanes]
            second = u[(2 * zh + 1) * f : (2 * zh + 2) * f, j * lanes : (j + 1) * lanes]
            even = jnp.where(low, first, pltpu.roll(second, yn, 1))
            odd = jnp.where(low, pltpu.roll(first, yn, 1), second)
            packed[j, 0, zh * f : (zh + 1) * f, :] = even.astype(BF16)
            packed[j, 1, zh * f : (zh + 1) * f, :] = odd.astype(BF16)


def spread_kernel(got, v, w, xlo, xhi, zlo, zhi, ids):
    peers, rows, lanes = got.shape
    table = got[:, rows - 8 :, :].astype(F32).reshape(peers * 8, lanes).astype(BF16)
    members = 32
    per = lanes // GROUP
    source = lax.broadcasted_iota(jnp.int32, (lanes, lanes), 0)
    lane = lax.broadcasted_iota(jnp.int32, (lanes, lanes), 1)
    late = lax.broadcasted_iota(jnp.int32, (1, lanes), 1) % GROUP >= GROUP // 2
    halves = members // per
    for mh in range(halves):
        wanted = (lane % (GROUP // 2)) * members + mh * per + lane // GROUP
        moved = jnp.dot(
            table, jnp.where(source == wanted, 1.0, 0.0).astype(BF16), preferred_element_type=F32
        )
        for q in range(peers):
            for kg in range(3):
                r = q * 8 + 2 * kg
                line = jnp.where(late, moved[r + 1 : r + 2], moved[r : r + 1])
                at = kg * halves + mh
                ids[q, at : at + 1, :] = line.astype(jnp.int32)
    yn = lanes // 2
    zn = 4
    half = (rows - HALO_ROWS) // 2
    xl = w.shape[0] // zn
    f = half - xl
    comps = f // xl
    low = lax.broadcasted_iota(jnp.int32, (rows, lanes), 1) < yn
    for j in range(peers // 2):
        one = got[2 * j].astype(F32)
        two = got[2 * j + 1].astype(F32)
        sides = (
            jnp.where(low, one, pltpu.roll(two, yn, 1)),
            jnp.where(low, pltpu.roll(one, yn, 1), two),
        )
        at = slice(j * lanes, (j + 1) * lanes)
        for zh in range(zn // 2):
            for side in range(2):
                z = 2 * zh + side
                whole = sides[side]
                v[z * f : (z + 1) * f, at] = whole[zh * half : zh * half + f].astype(BF16)
                w[z * xl : (z + 1) * xl, at] = whole[zh * half + f : (zh + 1) * half].astype(BF16)
                r = zn // 2 * half + zh * comps
                xlo[z * comps : (z + 1) * comps, at] = whole[r : r + comps]
                r = r + zn // 2 * comps
                xhi[z * comps : (z + 1) * comps, at] = whole[r : r + comps]
    zlo[...] = v[0:f]
    zhi[...] = v[(zn - 1) * f : zn * f]


def explicit_plane(z, u, w, zlo, zhi, x_before, x_after, e):
    f, cols = zlo.shape
    zn = u.shape[0] // f
    xl = w.shape[0] // zn
    comps = f // xl
    row = lax.broadcasted_iota(jnp.int32, (xl, cols), 0)
    lane = lax.broadcasted_iota(jnp.int32, (xl, cols), 1)
    factor = diffusion_factor * w[z * xl : (z + 1) * xl].astype(F32)
    for c in range(comps):
        r = z * comps + c
        at = slice(r * xl, (r + 1) * xl)
        cur = u[at].astype(F32)
        if z > 0:
            total = u[(r - comps) * xl : (r - comps + 1) * xl].astype(F32)
        else:
            total = zlo[c * xl : (c + 1) * xl].astype(F32)
        if z < zn - 1:
            total = total + u[(r + comps) * xl : (r + comps + 1) * xl].astype(F32)
        else:
            total = total + zhi[c * xl : (c + 1) * xl].astype(F32)
        total = total + jnp.where(row == 0, x_before[r : r + 1], pltpu.roll(cur, 1, 0))
        total = total + jnp.where(row == xl - 1, x_after[r : r + 1], pltpu.roll(cur, xl - 1, 0))
        total = total + jnp.where(lane == 0, 0.0, pltpu.roll(cur, 1, 1))
        total = total + jnp.where(lane == cols - 1, 0.0, pltpu.roll(cur, cols - 1, 1))
        e[at] = (cur + factor * (total - 6.0 * cur)).astype(BF16)


def first_kernel(
    v, w, xlo, xhi, zlo, zhi, a, u, packed, z_first, z_last, x_first, x_last, e
):
    x_before, x_after = xlo[...], xhi[...]
    zn = 4
    for z in range(zn):
        explicit_plane(z, v, w, zlo, zhi, x_before, x_after, e)
    u[...] = solve(e, a)
    f = zlo.shape[0]
    z_first[...] = u[0:f].astype(BF16)
    z_last[...] = u[(zn - 1) * f : zn * f].astype(BF16)
    xl = w.shape[0] // zn
    groups = u.shape[0] // xl
    for r in range(groups):
        x_first[r : r + 1] = u[r * xl : r * xl + 1]
        x_last[r : r + 1] = u[(r + 1) * xl - 1 : (r + 1) * xl]
    pack_columns(u, packed, zn)


def sample_kernel(packed, ids, sent_far, picked, sent, sems):
    copies = Copies(sems)
    sample(packed, ids, picked, sent, message_part(copies, sent, sent_far, 0))
    copies.finish()


def message_part(copies, sent, far, which):
    f = sent.shape[1]

    def ready(part):
        members, _, lanes = part
        copies.start(sent.at[part], far.at[members, pl.ds(which * f, f), lanes])

    return ready


def second_kernel(
    u, w, ids, zlo, zhi, xlo, xhi, a, sent_in, packed_far, sent_far,
    e, after, packed, picked, sent, sems,
):
    del sent_in
    copies = Copies(sems)
    zn = u.shape[0] // zlo.shape[0]
    x_before, x_after = xlo[...], xhi[...]
    for z in range(zn):
        explicit_plane(z, u, w, zlo, zhi, x_before, x_after, e)
    after[...] = solve(e, a)
    pack_columns(after, packed, zn)
    copies.start(packed, packed_far)
    sample(packed, ids, picked, sent, message_part(copies, sent, sent_far, 1))
    copies.finish()


def sample(packed, ids, picked, out, ready):
    pairs, _, rows, lanes = packed.shape
    peers = 2 * pairs
    f = rows // 2
    yn = lanes // 2
    blocks = picked.shape[2] // lanes
    r = lax.broadcasted_iota(jnp.int32, (2 * lanes, lanes), 0)
    row_id = (r % yn) * 4 + r // yn
    for q in range(peers):
        at = (q // 2, q % 2)
        table = jnp.concatenate([packed[(*at, slice(0, f))], packed[(*at, slice(f, rows))]], axis=1)
        wanted = pltpu.roll(ids[q], (GROUP * q) % lanes, 1) if q else ids[q]
        for b in range(blocks):
            hot = jnp.where(row_id == wanted[b : b + 1], 1.0, 0.0).astype(BF16)
            picked[q, :, b * lanes : (b + 1) * lanes] = jnp.dot(
                table, hot, preferred_element_type=F32
            )
    group = lax.broadcasted_iota(jnp.int32, (f, lanes), 1) // GROUP
    per = lanes // GROUP
    halves = out.shape[0] // per
    for b in range(blocks):
        kg, mh = b // halves, b % halves
        held = [picked[q, :, b * lanes : (b + 1) * lanes] for q in range(peers)]
        step = 1
        while step < peers:
            take = (group // step) % 2 == 1
            held = [jnp.where(take, held[(i + step) % peers], held[i]) for i in range(peers)]
            step *= 2
        for ml in range(per):
            out[mh * per + ml, :, kg * lanes : (kg + 1) * lanes] = held[(-ml) % peers].astype(BF16)
        ready((pl.ds(mh * per, per), slice(None), pl.ds(kg * lanes, lanes)))


def gather_rows(got, start, turned, comps=3):
    sources, both, slots = got.shape
    sides = 2
    peers = sources // sides
    xl = both // 2 // comps
    for q in range(peers):
        for side in range(sides):
            for c in range(comps):
                at = (c * peers + q) * xl
                turned[at : at + xl, side * slots : (side + 1) * slots] = got[
                    q * sides + side, start + c * xl : start + (c + 1) * xl
                ]


CONTRACT_ROWS = (((1,), (1,)), ((), ()))


def over_rows(left, right):
    return lax.dot_general(left, right, CONTRACT_ROWS, preferred_element_type=F32)


def over_first(left, right):
    return lax.dot_general(left, right, (((0,), (0,)), ((), ())), preferred_element_type=F32)


def forward_kernel(scale, place, got, w_in, w_out, x, hidden, slope, d, away):
    f = got.shape[1] // 2
    gather_rows(got, 0, x)
    wide = 512
    for i in range(hidden.shape[0] // wide):
        at = slice(i * wide, (i + 1) * wide)
        pre = over_first(w_in[:, at], x[...])
        logistic = jax.nn.sigmoid(pre)
        hidden[at, :] = (pre * logistic).astype(BF16)
        slope[at, :] = (logistic * (1.0 + pre * (1.0 - logistic))).astype(slope.dtype)
    gather_rows(got, f, d)
    predicted = over_first(w_out[...], hidden[...])
    d[...] = ((predicted - d[...].astype(F32)) * scale).astype(BF16)
    away_blocks(hidden, d, place[0], away, away.shape[0] // 4)


def block_rows(array, y, core, rows):
    return array[pl.ds(pl.multiple_of((2 * y + core) * rows, rows), rows), :]


def away_blocks(array, right, core, away, rows):
    left = jnp.concatenate([block_rows(array, y, 1 - core, rows) for y in range(4)], axis=0)
    away[...] = over_rows(left, right[...]).astype(BF16)


def delta_in_kernel(place, d, slope, w_out, x, din, away):
    wide = 512
    for i in range(din.shape[0] // wide):
        at = slice(i * wide, (i + 1) * wide)
        back = jnp.dot(w_out[at, :], d[...], preferred_element_type=F32)
        din[at, :] = (back * slope[at, :].astype(F32)).astype(BF16)
    away_blocks(x, din, place[0], away, away.shape[0] // 4)


def fold(block, rows, width):
    extra = rows - block.shape[0]
    pieces = [block[g * extra : (g + 1) * extra, width:] for g in range(block.shape[0] // extra)]
    return jnp.concatenate([block[:, :width], jnp.concatenate(pieces, axis=1)], axis=0)


def unfold(block, rows):
    extra = block.shape[0] - rows
    count = rows // extra
    wide = block.shape[1] // count
    pieces = [block[rows:, g * wide : (g + 1) * wide] for g in range(count)]
    return jnp.concatenate([block[:rows], jnp.concatenate(pieces, axis=0)], axis=1)


def own_blocks(place, array, rows):
    core, y = place[0], place[1]
    return jnp.concatenate(
        [block_rows(array, lax.rem(y + k, 4), core, rows) for k in (2, 1, 3, 0)], axis=0
    )


def add_other_core(place, value, got, n, k):
    rows = value.shape[0] // 4
    at = pl.multiple_of(lax.rem(place[1] + k, 4) * rows, rows)
    return value[n * rows : (n + 1) * rows] + got[pl.ds(at, rows), :].astype(F32)


def keep_out_kernel(place, hidden, d, got, own, plus, minus, far):
    value = over_rows(own_blocks(place, hidden, own.shape[0]), d[...])
    far[...] = add_other_core(place, value, got, 0, 2).astype(BF16)
    plus[...] = add_other_core(place, value, got, 1, 1).astype(BF16)
    minus[...] = add_other_core(place, value, got, 2, 3).astype(BF16)
    own[...] = add_other_core(place, value, got, 3, 0)


def keep_in_kernel(
    place, x, din, got, plus_out, minus_out, far_out, own, plus, minus, top, bottom
):
    rows, width = plus_out.shape
    half = rows // 2
    plus[0] = plus_out[...]
    minus[0] = minus_out[...]
    top[0] = far_out[:half]
    bottom[0] = far_out[half:]
    value = over_rows(own_blocks(place, x, own.shape[0]), din[...])
    far = fold(add_other_core(place, value, got, 0, 2), rows, width).astype(BF16)
    top[1] = far[:half]
    bottom[1] = far[half:]
    plus[1] = fold(add_other_core(place, value, got, 1, 1), rows, width).astype(BF16)
    minus[1] = fold(add_other_core(place, value, got, 2, 3), rows, width).astype(BF16)
    own[...] = add_other_core(place, value, got, 3, 0)


def relay_kernel(plus, minus, from_before, from_after, plus_out, minus_out):
    half = from_before.shape[1]
    for which in range(plus.shape[0]):
        plus_out[which, :half] = (
            plus[which, :half].astype(F32) + from_before[which].astype(F32)
        ).astype(BF16)
        plus_out[which, half:] = plus[which, half:]
        minus_out[which, :half] = minus[which, :half]
        minus_out[which, half:] = (
            minus[which, half:].astype(F32) + from_after[which].astype(F32)
        ).astype(BF16)


def finish_kernel(own_out, own_in, from_before, from_after, share_out, share_in):
    total = [from_before[k].astype(F32) + from_after[k].astype(F32) for k in range(2)]
    share_out[...] = own_out[...] + total[0]
    share_in[...] = own_in[...] + unfold(total[1], share_in.shape[0])


def planes_kernel(got, out):
    yn, comps, zn, xn = out.shape
    peers = got.shape[0]
    xl = xn // peers
    f = comps * xl
    for zh in range(zn // 2):
        for c in range(comps):
            base = zh * f + c * xl
            block = jnp.concatenate(
                [got[q, base : base + xl, :] for q in range(peers)], axis=0
            ).astype(F32)
            turned = block.T
            out[:, c, 2 * zh, :] = turned[0:yn]
            out[:, c, 2 * zh + 1, :] = turned[yn : 2 * yn]


def exchange(array, axis):
    return lax.all_to_all(array, axis, split_axis=0, concat_axis=0, tiled=True)


def swap_cores(array):
    size = lax.axis_size("px")
    return lax.ppermute(array, "px", [(i, i ^ 1) for i in range(size)])


def shift_chips(forward, backward):
    size = lax.axis_size("px")
    up = [(i, (i + 2) % size) for i in range(size)]
    down = [(j, i) for i, j in up]
    return lax.ppermute(forward, "px", up), lax.ppermute(backward, "px", down)


def per_device(velocity, viscosity, implicit_inverse, row_index, row_counts, weight_in, weight_out):
    yn, zn, comps, xn = velocity.shape
    peers = lax.axis_size("pz")
    position = lax.axis_index("px")
    place = jnp.stack([position & 1, position >> 1]).astype(jnp.int32)
    total_y = yn * peers
    xl = xn // peers
    f = comps * xl
    lanes = 2 * yn
    members, slots = row_index.shape[3:]

    sent = call(
        columns_kernel,
        shaped((peers, 2 * (f + xl) + HALO_ROWS, lanes), BF16),
        (
            velocity.transpose(0, 2, 1, 3),
            viscosity,
            row_index.reshape(members, slots).T,
            row_counts.reshape(1, members),
        ),
        scratch=[
            pltpu.VMEM((yn, comps, zn, xn), F32),
            pltpu.VMEM((yn, zn, xn), F32),
            pltpu.VMEM((slots, members), jnp.int32),
            pltpu.VMEM((1, members), jnp.int32),
            pltpu.VMEM((peers * HALO_ROWS, lanes), F32),
            pltpu.SemaphoreType.DMA((4,)),
        ],
        far_in=range(4),
    )
    inverse = implicit_inverse.astype(BF16)
    got = exchange(sent, "pz")
    solve_flops = 2 * zn * f * total_y * total_y
    edge = shaped((f, total_y), BF16)
    x_edge = shaped((zn * comps, total_y), F32)
    ids_all = shaped((peers, 8, lanes), jnp.int32)
    v, w, xlo, xhi, zlo, zhi, ids = call(
        spread_kernel,
        (shaped((zn * f, total_y), BF16), shaped((zn * xl, total_y), BF16))
        + (x_edge, x_edge, edge, edge, ids_all),
        (got,),
    )
    zlo, zhi = shift((zhi, zlo), ("px", "tr"))
    message = shaped((members, f, peers * slots), BF16)
    both = shaped((members, 2 * f, peers * slots), BF16)
    sample_flops = 2 * peers * f * 256 * members * slots
    sampling = [
        pltpu.VMEM((peers, 2 * f, lanes), BF16),
        pltpu.VMEM((peers, f, members * slots), F32),
        pltpu.VMEM(message.shape, BF16),
    ]
    blocks = shaped((peers // 2, 2, 2 * f, lanes), BF16)
    half_blocks = shaped((peers // 2, 2 * f, lanes), BF16)
    sampling[0] = pltpu.VMEM(blocks.shape, BF16)
    u, packed, z_first, z_last, x_first, x_last = call(
        first_kernel,
        (shaped((zn * f, total_y), F32), blocks, edge, edge, x_edge, x_edge),
        (v, w, xlo, xhi, zlo, zhi, inverse),
        scratch=[pltpu.VMEM((zn * f, total_y), BF16)],
        flops=solve_flops,
    )
    zlo, zhi = shift((z_last, z_first), ("px", "tr"))
    xlo, xhi = shift((x_last, x_first), "pz")
    sent = call(
        sample_kernel,
        both,
        (packed, ids),
        scratch=sampling[1:] + [pltpu.SemaphoreType.DMA((6,))],
        flops=sample_flops,
        far_out=(0,),
    )
    packed, sent = call(
        second_kernel,
        (blocks, both),
        (u, w, ids, zlo, zhi, xlo, xhi, inverse, sent),
        scratch=[pltpu.VMEM((zn * f, total_y), BF16), pltpu.VMEM((zn * f, total_y), F32)]
        + sampling
        + [pltpu.SemaphoreType.DMA((7,))],
        flops=solve_flops + sample_flops,
        far_in=(8,),
        far_out=(0, 1),
        aliases={8: 1},
    )
    sent, place = lax.optimization_barrier((sent, place))
    rows_all = exchange(sent, ("pz", "tr"))

    member_in = weight_in[0]
    member_out = weight_out[0]
    width, hid = member_in.shape
    batch = 2 * peers * slots
    spots = lax.axis_size("px")
    loss_scale = 1.0 / math.sqrt(spots * batch)
    matmul_flops = 2 * hid * width * batch

    def forward(*refs):
        forward_kernel(loss_scale, *refs)

    x, hidden, slope, d, away_out = call(
        forward,
        (
            shaped((width, batch), BF16),
            shaped((hid, batch), BF16),
            shaped((hid, batch), BF16),
            shaped((width, batch), BF16),
            shaped((hid // 2, width), BF16),
        ),
        (place, rows_all, member_in, member_out),
        flops=matmul_flops * 5 // 2,
    )
    got_out = swap_cores(away_out)
    din, away_in = call(
        delta_in_kernel,
        (shaped((hid, batch), BF16), shaped((width // 2, hid), BF16)),
        (place, d, slope, member_out, x),
        flops=matmul_flops * 3 // 2,
    )
    got_in = swap_cores(away_in)

    rows_out, rows_in = hid // spots, width // spots
    block = shaped((rows_out, width), BF16)
    own_out, plus, minus, far = call(
        keep_out_kernel,
        (shaped((rows_out, width), F32), block, block, block),
        (place, hidden, d, got_out),
        flops=matmul_flops // 2,
    )
    block = shaped((2, rows_out, width), BF16)
    part = shaped((2, rows_out // 2, width), BF16)
    own_in, plus, minus, top, bottom = call(
        keep_in_kernel,
        (shaped((rows_in, hid), F32), block, block, part, part),
        (place, x, din, got_in, plus, minus, far),
        flops=matmul_flops // 2,
    )
    packed, top = lax.optimization_barrier((packed, top))
    arrived = shift_chips(top, bottom)
    planes = exchange(packed.reshape(peers, 2 * f, lanes), "pz")
    plus, minus = call(relay_kernel, (block, block), (plus, minus, *arrived))
    arrived = shift_chips(plus, minus)
    share_out, share_in = call(
        finish_kernel,
        (shaped((rows_out, width), F32), shaped((rows_in, hid), F32)),
        (own_out, own_in, *arrived),
    )
    result = call(planes_kernel, shaped((yn, comps, zn, xn), F32), (planes,))
    return (result.transpose(0, 2, 1, 3), share_in[None], share_out[None])


def solution(mesh):
    in_specs = (
        P("pz", ("px", "tr"), None, None),
        P("pz", ("px", "tr"), None),
        P(),
        P("px", "pz", "tr", None, None),
        P("px", "pz", "tr", None),
        P(("pz", "tr"), None, None),
        P(("pz", "tr"), None, None),
    )
    out_specs = (
        P("pz", ("px", "tr"), None, None),
        P(("pz", "tr"), "px", None),
        P(("pz", "tr"), "px", None),
    )
    return jax.shard_map(
        per_device, mesh=mesh, in_specs=in_specs, out_specs=out_specs, check_vma=False
    )
```

```python
import math

import jax
import jax.numpy as jnp
from jax import lax
from jax.experimental import pallas as pl
from jax.experimental.pallas import tpu as pltpu
from jax.sharding import PartitionSpec as P

diffusion_factor = 0.08
F32 = jnp.float32
BF16 = jnp.bfloat16
MIB = 1 << 20


def call(kernel, out_shape, args, scratch=(), flops=1e6, far_in=(), far_out=(), aliases=None):
    outs = jax.tree.leaves(out_shape)
    size = lambda x: math.prod(x.shape) * jnp.dtype(x.dtype).itemsize
    near = [x for k, x in enumerate(args) if k not in far_in]
    near += [x for k, x in enumerate(outs) if k not in far_out]
    held = sum(size(x) for x in near) + sum(size(x) for x in scratch if x.dtype in (F32, BF16, jnp.int32))

    def spec(k, far, scalar=False):
        space = pltpu.HBM if k in far else pltpu.SMEM if scalar else pltpu.VMEM
        return pl.BlockSpec(memory_space=space)

    out_specs = tuple(spec(k, far_out) for k in range(len(outs)))
    args = [
        pltpu.with_memory_space_constraint(x, pltpu.HBM) if k in far_in else x
        for k, x in enumerate(args)
    ]
    pinned = tuple(
        pltpu.HBM(x.shape, x.dtype) if k in far_out else x for k, x in enumerate(outs)
    )
    return pl.pallas_call(
        kernel,
        out_shape=pinned if isinstance(out_shape, tuple) else pinned[0],
        in_specs=[spec(k, far_in, x.ndim == 1) for k, x in enumerate(args)],
        out_specs=out_specs if isinstance(out_shape, tuple) else out_specs[0],
        scratch_shapes=list(scratch),
        input_output_aliases=aliases or {},
        compiler_params=pltpu.CompilerParams(vmem_limit_bytes=held + 6 * MIB),
        cost_estimate=pl.CostEstimate(
            flops=int(flops),
            bytes_accessed=int(sum(size(x) for x in list(args) + outs)),
            transcendentals=0,
        ),
    )(*args)


class Copies:
    def __init__(self, sems):
        self.sems, self.used, self.open = sems, 0, []

    def start(self, source, target):
        copy = pltpu.make_async_copy(source, target, self.sems.at[self.used])
        copy.start()
        self.used += 1
        self.open.append(copy)
        return copy

    def finish(self):
        for copy in self.open:
            copy.wait()
        self.open = []

    def wait(self, copy):
        copy.wait()
        self.open.remove(copy)


def shaped(shape, dtype):
    return jax.ShapeDtypeStruct(shape, dtype)


def swap_pairs(first, second, axis, stride=1):
    size = math.prod(lax.axis_size(a) for a in ((axis,) if isinstance(axis, str) else axis))
    place = lambda i: (i // stride) % 2
    above = [(i, (i + stride) % size) for i in range(size) if place(i) == 0]
    below = [(i, (i + stride) % size) for i in range(size) if place(i) == 1]
    both = lambda pairs: pairs + [(j, i) for i, j in pairs]
    return lax.ppermute(first, axis, both(above)), lax.ppermute(second, axis, both(below))


def even_odd(odd, even_value, odd_value):
    return jnp.where(odd == 1, odd_value, even_value)


HALO_ROWS = 24
GROUP = 8


def columns_kernel(v_far, w_far, index_far, counts_far, out, v, w, index, counts, edge, sems):
    copies = Copies(sems)
    for far, near in ((index_far, index), (counts_far, counts), (w_far, w), (v_far, v)):
        copies.start(far, near)
    copies.finish()
    yn, comps, zn, xn = v.shape
    peers = out.shape[0]
    xl = xn // peers
    lanes_of = out.shape[2]
    half = (comps + 1) * xl
    for zh in range(zn // 2):
        for c in range(comps + 1):
            pair = [w[:, z, :] if c == comps else v[:, c, z, :] for z in (2 * zh, 2 * zh + 1)]
            turned = jnp.concatenate(pair, axis=0).T
            base = zh * half + c * xl
            for q in range(peers):
                out[q, base : base + xl, :] = turned[q * xl : (q + 1) * xl].astype(BF16)
            if c == comps:
                continue
            for q in range(peers):
                before = (q * xl - 1) % xn
                after = (q + 1) * xl % xn
                r = q * HALO_ROWS + zh * comps + c
                edge[r : r + 1] = turned[before : before + 1]
                edge[r + zn // 2 * comps : r + zn // 2 * comps + 1] = turned[after : after + 1]
    start = zn // 2 * half
    slots, members = index.shape
    slot = lax.broadcasted_iota(jnp.int32, (slots, members), 0)
    live = jnp.where(slot < counts[...], index[...], -1).astype(F32)
    sides = lanes_of // members
    rows = slots // sides
    numbers = jnp.concatenate([live[k * rows : (k + 1) * rows] for k in range(sides)], axis=1)
    numbers = jnp.concatenate([numbers, jnp.zeros((8 - rows, lanes_of), F32)], axis=0)
    for q in range(peers):
        edge[(q + 1) * HALO_ROWS - 8 : (q + 1) * HALO_ROWS] = numbers
        out[q, start : start + HALO_ROWS, :] = edge[
            q * HALO_ROWS : (q + 1) * HALO_ROWS
        ].astype(BF16)


def solve(e, a):
    return lax.dot_general(
        e[...], a[...], (((1,), (1,)), ((), ())), preferred_element_type=F32
    )


def pack_columns(u, packed, zn):
    pairs, _, rows, lanes = packed.shape
    f = rows // (zn // 2)
    yn = lanes // 2
    low = lax.broadcasted_iota(jnp.int32, (f, lanes), 1) < yn
    for j in range(pairs):
        for zh in range(zn // 2):
            first = u[(2 * zh) * f : (2 * zh + 1) * f, j * lanes : (j + 1) * lanes]
            second = u[(2 * zh + 1) * f : (2 * zh + 2) * f, j * lanes : (j + 1) * lanes]
            even = jnp.where(low, first, pltpu.roll(second, yn, 1))
            odd = jnp.where(low, pltpu.roll(first, yn, 1), second)
            packed[j, 0, zh * f : (zh + 1) * f, :] = even.astype(BF16)
            packed[j, 1, zh * f : (zh + 1) * f, :] = odd.astype(BF16)


def spread_kernel(place, got, v, w, xlo, xhi, z_first, z_second, ids):
    peers, rows, lanes = got.shape
    table = got[:, rows - 8 :, :].astype(F32).reshape(peers * 8, lanes).astype(BF16)
    members = 32
    per = lanes // GROUP
    source = lax.broadcasted_iota(jnp.int32, (lanes, lanes), 0)
    lane = lax.broadcasted_iota(jnp.int32, (lanes, lanes), 1)
    late = lax.broadcasted_iota(jnp.int32, (1, lanes), 1) % GROUP >= GROUP // 2
    halves = members // per
    for mh in range(halves):
        wanted = (lane % (GROUP // 2)) * members + mh * per + lane // GROUP
        moved = jnp.dot(
            table, jnp.where(source == wanted, 1.0, 0.0).astype(BF16), preferred_element_type=F32
        )
        for q in range(peers):
            for kg in range(3):
                r = q * 8 + 2 * kg
                line = jnp.where(late, moved[r + 1 : r + 2], moved[r : r + 1])
                at = kg * halves + mh
                ids[q, at : at + 1, :] = line.astype(jnp.int32)
    yn = lanes // 2
    zn = 4
    half = (rows - HALO_ROWS) // 2
    xl = w.shape[0] // zn
    f = half - xl
    comps = f // xl
    low = lax.broadcasted_iota(jnp.int32, (rows, lanes), 1) < yn
    for j in range(peers // 2):
        one = got[2 * j].astype(F32)
        two = got[2 * j + 1].astype(F32)
        sides = (
            jnp.where(low, one, pltpu.roll(two, yn, 1)),
            jnp.where(low, pltpu.roll(one, yn, 1), two),
        )
        at = slice(j * lanes, (j + 1) * lanes)
        for zh in range(zn // 2):
            for side in range(2):
                z = 2 * zh + side
                whole = sides[side]
                v[z * f : (z + 1) * f, at] = whole[zh * half : zh * half + f].astype(BF16)
                w[z * xl : (z + 1) * xl, at] = whole[zh * half + f : (zh + 1) * half].astype(BF16)
                r = zn // 2 * half + zh * comps
                xlo[z * comps : (z + 1) * comps, at] = whole[r : r + comps]
                r = r + zn // 2 * comps
                xhi[z * comps : (z + 1) * comps, at] = whole[r : r + comps]
    low_edge, high_edge = v[0:f].astype(F32), v[(zn - 1) * f : zn * f].astype(F32)
    z_first[...] = even_odd(place[2], high_edge, low_edge).astype(BF16)
    z_second[...] = even_odd(place[2], low_edge, high_edge).astype(BF16)


def explicit_plane(z, u, w, zlo, zhi, x_before, x_after, e):
    f, cols = zlo.shape
    zn = u.shape[0] // f
    xl = w.shape[0] // zn
    comps = f // xl
    row = lax.broadcasted_iota(jnp.int32, (xl, cols), 0)
    lane = lax.broadcasted_iota(jnp.int32, (xl, cols), 1)
    factor = diffusion_factor * w[z * xl : (z + 1) * xl].astype(F32)
    for c in range(comps):
        r = z * comps + c
        at = slice(r * xl, (r + 1) * xl)
        cur = u[at].astype(F32)
        if z > 0:
            total = u[(r - comps) * xl : (r - comps + 1) * xl].astype(F32)
        else:
            total = zlo[c * xl : (c + 1) * xl]
        if z < zn - 1:
            total = total + u[(r + comps) * xl : (r + comps + 1) * xl].astype(F32)
        else:
            total = total + zhi[c * xl : (c + 1) * xl]
        total = total + jnp.where(row == 0, x_before[r : r + 1], pltpu.roll(cur, 1, 0))
        total = total + jnp.where(row == xl - 1, x_after[r : r + 1], pltpu.roll(cur, xl - 1, 0))
        total = total + jnp.where(lane == 0, 0.0, pltpu.roll(cur, 1, 1))
        total = total + jnp.where(lane == cols - 1, 0.0, pltpu.roll(cur, cols - 1, 1))
        e[at] = (cur + factor * (total - 6.0 * cur)).astype(BF16)


def sides(odd, first, second):
    first, second = (x[...].astype(F32) for x in (first, second))
    return even_odd(odd, second, first), even_odd(odd, first, second)


def first_kernel(
    place, v, w, xlo, xhi, z_in, z_in_other, a,
    u, packed, z_first, z_second, x_first, x_second, e,
):
    x_before, x_after = xlo[...], xhi[...]
    z_before, z_after = sides(place[2], z_in, z_in_other)
    zn = 4
    for z in range(zn):
        explicit_plane(z, v, w, z_before, z_after, x_before, x_after, e)
    u[...] = solve(e, a)
    f = z_in.shape[0]
    low_edge, high_edge = u[0:f], u[(zn - 1) * f : zn * f]
    z_first[...] = even_odd(place[2], high_edge, low_edge).astype(BF16)
    z_second[...] = even_odd(place[2], low_edge, high_edge).astype(BF16)
    xl = w.shape[0] // zn
    for r in range(u.shape[0] // xl):
        low_row, high_row = u[r * xl : r * xl + 1], u[(r + 1) * xl - 1 : (r + 1) * xl]
        x_first[r : r + 1] = even_odd(place[3], high_row, low_row)
        x_second[r : r + 1] = even_odd(place[3], low_row, high_row)
    pack_columns(u, packed, zn)


def sample_kernel(packed, ids, sent_far, picked, sent, sems):
    copies = Copies(sems)
    sample(packed, ids, picked, sent, message_part(copies, sent, sent_far, 0))
    copies.finish()


def message_part(copies, sent, far, which):
    f = sent.shape[1]

    def ready(part):
        members, _, lanes = part
        copies.start(sent.at[part], far.at[members, pl.ds(which * f, f), lanes])

    return ready


def second_kernel(
    place, u, w, ids, z_in, z_in_other, x_in, x_in_other, a, sent_in, packed_far, sent_far,
    e, after, packed, picked, sent, sems,
):
    del sent_in
    copies = Copies(sems)
    zn = u.shape[0] // z_in.shape[0]
    z_before, z_after = sides(place[2], z_in, z_in_other)
    x_before, x_after = sides(place[3], x_in, x_in_other)
    for z in range(zn):
        explicit_plane(z, u, w, z_before, z_after, x_before, x_after, e)
    after[...] = solve(e, a)
    pack_columns(after, packed, zn)
    copies.start(packed, packed_far)
    sample(packed, ids, picked, sent, message_part(copies, sent, sent_far, 1))
    copies.finish()


def sample(packed, ids, picked, out, ready):
    pairs, _, rows, lanes = packed.shape
    peers = 2 * pairs
    f = rows // 2
    yn = lanes // 2
    blocks = picked.shape[2] // lanes
    r = lax.broadcasted_iota(jnp.int32, (2 * lanes, lanes), 0)
    row_id = (r % yn) * 4 + r // yn
    for q in range(peers):
        at = (q // 2, q % 2)
        table = jnp.concatenate([packed[(*at, slice(0, f))], packed[(*at, slice(f, rows))]], axis=1)
        wanted = pltpu.roll(ids[q], (GROUP * q) % lanes, 1) if q else ids[q]
        for b in range(blocks):
            hot = jnp.where(row_id == wanted[b : b + 1], 1.0, 0.0).astype(BF16)
            picked[q, :, b * lanes : (b + 1) * lanes] = jnp.dot(
                table, hot, preferred_element_type=F32
            )
    group = lax.broadcasted_iota(jnp.int32, (f, lanes), 1) // GROUP
    per = lanes // GROUP
    halves = out.shape[0] // per
    for b in range(blocks):
        kg, mh = b // halves, b % halves
        held = [picked[q, :, b * lanes : (b + 1) * lanes] for q in range(peers)]
        step = 1
        while step < peers:
            take = (group // step) % 2 == 1
            held = [jnp.where(take, held[(i + step) % peers], held[i]) for i in range(peers)]
            step *= 2
        for ml in range(per):
            out[mh * per + ml, :, kg * lanes : (kg + 1) * lanes] = held[(-ml) % peers].astype(BF16)
        ready((pl.ds(mh * per, per), slice(None), pl.ds(kg * lanes, lanes)))


def gather_rows(got, start, turned, comps=3):
    sources, both, slots = got.shape
    sides = 2
    peers = sources // sides
    xl = both // 2 // comps
    for q in range(peers):
        for side in range(sides):
            for c in range(comps):
                at = (c * peers + q) * xl
                turned[at : at + xl, side * slots : (side + 1) * slots] = got[
                    q * sides + side, start + c * xl : start + (c + 1) * xl
                ]


CONTRACT_ROWS = (((1,), (1,)), ((), ()))


def over_rows(left, right):
    return lax.dot_general(left, right, CONTRACT_ROWS, preferred_element_type=F32)


def over_first(left, right):
    return lax.dot_general(left, right, (((0,), (0,)), ((), ())), preferred_element_type=F32)


def forward_kernel(
    scale, place, got, w_in_far, w_out_far, x, hidden, slope, d, away, w_in, w_out, sems
):
    copies = Copies(sems)
    f = got.shape[1] // 2
    wide = 512
    arriving = []
    for i in range(hidden.shape[0] // wide):
        part = (slice(None), pl.ds(i * wide, wide))
        arriving.append(copies.start(w_in_far.at[part], w_in.at[part]))
    copies.start(w_out_far, w_out)
    gather_rows(got, 0, x)
    gather_rows(got, f, d)
    for i in range(hidden.shape[0] // wide):
        at = slice(i * wide, (i + 1) * wide)
        copies.wait(arriving[i])
        pre = over_first(w_in[:, at], x[...])
        logistic = jax.nn.sigmoid(pre)
        hidden[at, :] = (pre * logistic).astype(BF16)
        slope[at, :] = (logistic * (1.0 + pre * (1.0 - logistic))).astype(slope.dtype)
    copies.finish()
    predicted = over_first(w_out[...], hidden[...])
    d[...] = ((predicted - d[...].astype(F32)) * scale).astype(BF16)
    away_blocks(hidden, d, place[0], away, away.shape[0] // 4)


def block_rows(array, y, core, rows):
    return array[pl.ds(pl.multiple_of((2 * y + core) * rows, rows), rows), :]


def away_blocks(array, right, core, away, rows):
    left = jnp.concatenate([block_rows(array, y, 1 - core, rows) for y in range(4)], axis=0)
    away[...] = over_rows(left, right[...]).astype(BF16)


def delta_in_kernel(place, d, slope, w_out, x, din, away):
    wide = 512
    for i in range(din.shape[0] // wide):
        at = slice(i * wide, (i + 1) * wide)
        back = jnp.dot(w_out[at, :], d[...], preferred_element_type=F32)
        din[at, :] = (back * slope[at, :].astype(F32)).astype(BF16)
    away_blocks(x, din, place[0], away, away.shape[0] // 4)


def fold(block, rows, width):
    extra = rows - block.shape[0]
    pieces = [block[g * extra : (g + 1) * extra, width:] for g in range(block.shape[0] // extra)]
    return jnp.concatenate([block[:, :width], jnp.concatenate(pieces, axis=1)], axis=0)


def unfold(block, rows):
    extra = block.shape[0] - rows
    count = rows // extra
    wide = block.shape[1] // count
    pieces = [block[rows:, g * wide : (g + 1) * wide] for g in range(count)]
    return jnp.concatenate([block[:rows], jnp.concatenate(pieces, axis=0)], axis=1)


def own_blocks(place, array, rows):
    core, y = place[0], place[1]
    return jnp.concatenate(
        [block_rows(array, lax.rem(y + k, 4), core, rows) for k in (2, 1, 3, 0)], axis=0
    )


def add_other_core(place, value, got, n, k):
    rows = value.shape[0] // 4
    at = pl.multiple_of(lax.rem(place[1] + k, 4) * rows, rows)
    return value[n * rows : (n + 1) * rows] + got[pl.ds(at, rows), :].astype(F32)


def keep_out_kernel(place, hidden, d, got, own, plus, minus, far):
    value = over_rows(own_blocks(place, hidden, own.shape[0]), d[...])
    far[...] = add_other_core(place, value, got, 0, 2).astype(BF16)
    plus[...] = add_other_core(place, value, got, 1, 1).astype(BF16)
    minus[...] = add_other_core(place, value, got, 2, 3).astype(BF16)
    own[...] = add_other_core(place, value, got, 3, 0)


def keep_in_kernel(
    place, x, din, got, plus_out, minus_out, far_out, own, plus, minus, first, second
):
    rows, width = plus_out.shape
    half = rows // 2
    plus[0] = plus_out[...]
    minus[0] = minus_out[...]
    odd = place[1] % 2
    halves = [far_out[:half].astype(F32), far_out[half:].astype(F32)]
    first[0] = even_odd(odd, *halves).astype(BF16)
    second[0] = even_odd(odd, *halves[::-1]).astype(BF16)
    value = over_rows(own_blocks(place, x, own.shape[0]), din[...])
    far = fold(add_other_core(place, value, got, 0, 2), rows, width)
    halves = [far[:half], far[half:]]
    first[1] = even_odd(odd, *halves).astype(BF16)
    second[1] = even_odd(odd, *halves[::-1]).astype(BF16)
    plus[1] = fold(add_other_core(place, value, got, 1, 1), rows, width).astype(BF16)
    minus[1] = fold(add_other_core(place, value, got, 2, 3), rows, width).astype(BF16)
    own[...] = add_other_core(place, value, got, 3, 0)


def relay_kernel(place, plus, minus, got_first, got_second, first, second):
    half = got_first.shape[1]
    odd = place[1] % 2
    for which in range(plus.shape[0]):
        before, after = sides(odd, got_first[which], got_second[which])
        up = [plus[which, :half].astype(F32) + before, plus[which, half:].astype(F32)]
        down = [minus[which, :half].astype(F32), minus[which, half:].astype(F32) + after]
        for part, at in enumerate((slice(0, half), slice(half, 2 * half))):
            first[which, at] = even_odd(odd, up[part], down[part]).astype(BF16)
            second[which, at] = even_odd(odd, down[part], up[part]).astype(BF16)


def finish_kernel(own_out, own_in, from_before, from_after, share_out, share_in):
    total = [from_before[k].astype(F32) + from_after[k].astype(F32) for k in range(2)]
    share_out[...] = own_out[...] + total[0]
    share_in[...] = own_in[...] + unfold(total[1], share_in.shape[0])


def planes_kernel(got, out):
    yn, comps, zn, xn = out.shape
    peers = got.shape[0]
    xl = xn // peers
    f = comps * xl
    for zh in range(zn // 2):
        for c in range(comps):
            base = zh * f + c * xl
            block = jnp.concatenate(
                [got[q, base : base + xl, :] for q in range(peers)], axis=0
            ).astype(F32)
            turned = block.T
            out[:, c, 2 * zh, :] = turned[0:yn]
            out[:, c, 2 * zh + 1, :] = turned[yn : 2 * yn]


def copy_kernel(source_far, target_far, sems):
    copies = Copies(sems)
    copies.start(source_far, target_far)
    copies.finish()


def exchange(array, axis):
    return lax.all_to_all(array, axis, split_axis=0, concat_axis=0, tiled=True)


def swap_cores(array):
    size = lax.axis_size("px")
    return lax.ppermute(array, "px", [(i, i ^ 1) for i in range(size)])


def per_device(velocity, viscosity, implicit_inverse, row_index, row_counts, weight_in, weight_out):
    yn, zn, comps, xn = velocity.shape
    peers = lax.axis_size("pz")
    at_px, at_pz = lax.axis_index("px"), lax.axis_index("pz")
    place = jnp.stack([at_px & 1, at_px >> 1, lax.axis_index("tr"), at_pz & 1]).astype(jnp.int32)
    total_y = yn * peers
    xl = xn // peers
    f = comps * xl
    lanes = 2 * yn
    members, slots = row_index.shape[3:]

    sent = call(
        columns_kernel,
        shaped((peers, 2 * (f + xl) + HALO_ROWS, lanes), BF16),
        (
            velocity.transpose(0, 2, 1, 3),
            viscosity,
            row_index.reshape(members, slots).T,
            row_counts.reshape(1, members),
        ),
        scratch=[
            pltpu.VMEM((yn, comps, zn, xn), F32),
            pltpu.VMEM((yn, zn, xn), F32),
            pltpu.VMEM((slots, members), jnp.int32),
            pltpu.VMEM((1, members), jnp.int32),
            pltpu.VMEM((peers * HALO_ROWS, lanes), F32),
            pltpu.SemaphoreType.DMA((4,)),
        ],
        far_in=range(4),
    )
    inverse = implicit_inverse.astype(BF16)
    got = exchange(sent, "pz")
    solve_flops = 2 * zn * f * total_y * total_y
    edge = shaped((f, total_y), BF16)
    x_edge = shaped((zn * comps, total_y), F32)
    ids_all = shaped((peers, 8, lanes), jnp.int32)
    v, w, xlo, xhi, zlo, zhi, ids = call(
        spread_kernel,
        (shaped((zn * f, total_y), BF16), shaped((zn * xl, total_y), BF16))
        + (x_edge, x_edge, edge, edge, ids_all),
        (place, got),
    )
    zlo, zhi = swap_pairs(zlo, zhi, ("px", "tr"))
    message = shaped((members, f, peers * slots), BF16)
    both = shaped((members, 2 * f, peers * slots), BF16)
    sample_flops = 2 * peers * f * 256 * members * slots
    sampling = [
        pltpu.VMEM((peers, 2 * f, lanes), BF16),
        pltpu.VMEM((peers, f, members * slots), F32),
        pltpu.VMEM(message.shape, BF16),
    ]
    blocks = shaped((peers // 2, 2, 2 * f, lanes), BF16)
    half_blocks = shaped((peers // 2, 2 * f, lanes), BF16)
    sampling[0] = pltpu.VMEM(blocks.shape, BF16)
    u, packed, z_first, z_last, x_first, x_last = call(
        first_kernel,
        (shaped((zn * f, total_y), F32), blocks, edge, edge, x_edge, x_edge),
        (place, v, w, xlo, xhi, zlo, zhi, inverse),
        scratch=[pltpu.VMEM((zn * f, total_y), BF16)],
        flops=solve_flops,
    )
    zlo, zhi = swap_pairs(z_first, z_last, ("px", "tr"))
    xlo, xhi = swap_pairs(x_first, x_last, "pz")
    sent = call(
        sample_kernel,
        both,
        (packed, ids),
        scratch=sampling[1:] + [pltpu.SemaphoreType.DMA((6,))],
        flops=sample_flops,
        far_out=(0,),
    )
    packed, sent = call(
        second_kernel,
        (blocks, both),
        (place, u, w, ids, zlo, zhi, xlo, xhi, inverse, sent),
        scratch=[pltpu.VMEM((zn * f, total_y), BF16), pltpu.VMEM((zn * f, total_y), F32)]
        + sampling
        + [pltpu.SemaphoreType.DMA((7,))],
        flops=solve_flops + sample_flops,
        far_in=(9,),
        far_out=(0, 1),
        aliases={9: 1},
    )
    rows_all = exchange(sent, ("pz", "tr"))
    packed = call(
        copy_kernel,
        shaped((peers, 2 * f, lanes), BF16),
        (packed.reshape(peers, 2 * f, lanes),),
        scratch=[pltpu.SemaphoreType.DMA((1,))],
        flops=6e9,
        far_in=(0,),
        far_out=(0,),
    )
    packed, rows_all = lax.optimization_barrier((packed, rows_all))

    member_in = weight_in[0]
    member_out = weight_out[0]
    width, hid = member_in.shape
    batch = 2 * peers * slots
    spots = lax.axis_size("px")
    loss_scale = 1.0 / math.sqrt(spots * batch)
    matmul_flops = 2 * hid * width * batch

    def forward(*refs):
        forward_kernel(loss_scale, *refs)

    x, hidden, slope, d, away_out = call(
        forward,
        (
            shaped((width, batch), BF16),
            shaped((hid, batch), BF16),
            shaped((hid, batch), BF16),
            shaped((width, batch), BF16),
            shaped((hid // 2, width), BF16),
        ),
        (place, rows_all, member_in, member_out),
        scratch=[
            pltpu.VMEM((width, hid), BF16),
            pltpu.VMEM((hid, width), BF16),
            pltpu.SemaphoreType.DMA((3,)),
        ],
        flops=matmul_flops * 5 // 2,
        far_in=(2, 3),
    )
    got_out = swap_cores(away_out)
    din, away_in = call(
        delta_in_kernel,
        (shaped((hid, batch), BF16), shaped((width // 2, hid), BF16)),
        (place, d, slope, member_out, x),
        flops=matmul_flops * 3 // 2,
    )
    got_in = swap_cores(away_in)

    rows_out, rows_in = hid // spots, width // spots
    block = shaped((rows_out, width), BF16)
    own_out, plus, minus, far = call(
        keep_out_kernel,
        (shaped((rows_out, width), F32), block, block, block),
        (place, hidden, d, got_out),
        flops=matmul_flops // 2,
    )
    block = shaped((2, rows_out, width), BF16)
    part = shaped((2, rows_out // 2, width), BF16)
    own_in, plus, minus, top, bottom = call(
        keep_in_kernel,
        (shaped((rows_in, hid), F32), block, block, part, part),
        (place, x, din, got_in, plus, minus, far),
        flops=matmul_flops // 2,
    )
    packed, top = lax.optimization_barrier((packed, top))
    arrived = swap_pairs(top, bottom, "px", 2)
    planes = exchange(packed, "pz")
    sent = call(relay_kernel, (block, block), (place, plus, minus, *arrived))
    arrived = swap_pairs(*sent, "px", 2)
    share_out, share_in = call(
        finish_kernel,
        (shaped((rows_out, width), F32), shaped((rows_in, hid), F32)),
        (own_out, own_in, *arrived),
    )
    result = call(planes_kernel, shaped((yn, comps, zn, xn), F32), (planes,))
    return (result.transpose(0, 2, 1, 3), share_in[None], share_out[None])


def solution(mesh):
    in_specs = (
        P("pz", ("px", "tr"), None, None),
        P("pz", ("px", "tr"), None),
        P(),
        P("px", "pz", "tr", None, None),
        P("px", "pz", "tr", None),
        P(("pz", "tr"), None, None),
        P(("pz", "tr"), None, None),
    )
    out_specs = (
        P("pz", ("px", "tr"), None, None),
        P(("pz", "tr"), "px", None),
        P(("pz", "tr"), "px", None),
    )
    return jax.shard_map(
        per_device, mesh=mesh, in_specs=in_specs, out_specs=out_specs, check_vma=False
    )
```

```python
import math

import jax
import jax.numpy as jnp
from jax import lax
from jax.experimental import pallas as pl
from jax.experimental.pallas import tpu as pltpu
from jax.sharding import PartitionSpec as P

diffusion_factor = 0.08
F32 = jnp.float32
BF16 = jnp.bfloat16
MIB = 1 << 20


def call(kernel, out_shape, args, scratch=(), flops=1e6, far_in=(), far_out=(), aliases=None):
    outs = jax.tree.leaves(out_shape)
    size = lambda x: math.prod(x.shape) * jnp.dtype(x.dtype).itemsize
    near = [x for k, x in enumerate(args) if k not in far_in]
    near += [x for k, x in enumerate(outs) if k not in far_out]
    held = sum(size(x) for x in near) + sum(size(x) for x in scratch if x.dtype in (F32, BF16, jnp.int32))

    def spec(k, far, scalar=False):
        space = pltpu.HBM if k in far else pltpu.SMEM if scalar else pltpu.VMEM
        return pl.BlockSpec(memory_space=space)

    out_specs = tuple(spec(k, far_out) for k in range(len(outs)))
    args = [
        pltpu.with_memory_space_constraint(x, pltpu.HBM) if k in far_in else x
        for k, x in enumerate(args)
    ]
    pinned = tuple(
        pltpu.HBM(x.shape, x.dtype) if k in far_out else x for k, x in enumerate(outs)
    )
    return pl.pallas_call(
        kernel,
        out_shape=pinned if isinstance(out_shape, tuple) else pinned[0],
        in_specs=[spec(k, far_in, x.ndim == 1) for k, x in enumerate(args)],
        out_specs=out_specs if isinstance(out_shape, tuple) else out_specs[0],
        scratch_shapes=list(scratch),
        input_output_aliases=aliases or {},
        compiler_params=pltpu.CompilerParams(vmem_limit_bytes=held + 6 * MIB),
        cost_estimate=pl.CostEstimate(
            flops=int(flops),
            bytes_accessed=int(sum(size(x) for x in list(args) + outs)),
            transcendentals=0,
        ),
    )(*args)


class Copies:
    def __init__(self, sems):
        self.sems, self.used, self.open = sems, 0, []

    def start(self, source, target):
        copy = pltpu.make_async_copy(source, target, self.sems.at[self.used])
        copy.start()
        self.used += 1
        self.open.append(copy)
        return copy

    def finish(self):
        for copy in self.open:
            copy.wait()
        self.open = []

    def wait(self, copy):
        copy.wait()
        self.open.remove(copy)


def shaped(shape, dtype):
    return jax.ShapeDtypeStruct(shape, dtype)


def shift(array, axis, wrap=True):
    last, first = array
    size = lax.axis_size(axis)
    up = [(i, (i + 1) % size) for i in range(size if wrap else size - 1)]
    down = [(j, i) for i, j in up]
    return lax.ppermute(last, axis, up), lax.ppermute(first, axis, down)


HALO_ROWS = 24
GROUP = 8


def columns_kernel(v_far, w_far, index_far, counts_far, out, v, w, index, counts, edge, sems):
    copies = Copies(sems)
    for far, near in ((index_far, index), (counts_far, counts), (w_far, w), (v_far, v)):
        copies.start(far, near)
    copies.finish()
    yn, comps, zn, xn = v.shape
    peers = out.shape[0]
    xl = xn // peers
    lanes_of = out.shape[2]
    half = (comps + 1) * xl
    for zh in range(zn // 2):
        for c in range(comps + 1):
            pair = [w[:, z, :] if c == comps else v[:, c, z, :] for z in (2 * zh, 2 * zh + 1)]
            turned = jnp.concatenate(pair, axis=0).T
            base = zh * half + c * xl
            for q in range(peers):
                out[q, base : base + xl, :] = turned[q * xl : (q + 1) * xl].astype(BF16)
            if c == comps:
                continue
            for q in range(peers):
                before = (q * xl - 1) % xn
                after = (q + 1) * xl % xn
                r = q * HALO_ROWS + zh * comps + c
                edge[r : r + 1] = turned[before : before + 1]
                edge[r + zn // 2 * comps : r + zn // 2 * comps + 1] = turned[after : after + 1]
    start = zn // 2 * half
    slots, members = index.shape
    slot = lax.broadcasted_iota(jnp.int32, (slots, members), 0)
    live = jnp.where(slot < counts[...], index[...], -1).astype(F32)
    sides = lanes_of // members
    rows = slots // sides
    numbers = jnp.concatenate([live[k * rows : (k + 1) * rows] for k in range(sides)], axis=1)
    numbers = jnp.concatenate([numbers, jnp.zeros((8 - rows, lanes_of), F32)], axis=0)
    for q in range(peers):
        edge[(q + 1) * HALO_ROWS - 8 : (q + 1) * HALO_ROWS] = numbers
        out[q, start : start + HALO_ROWS, :] = edge[
            q * HALO_ROWS : (q + 1) * HALO_ROWS
        ].astype(BF16)


def solve(e, a):
    return lax.dot_general(
        e[...], a[...], (((1,), (1,)), ((), ())), preferred_element_type=F32
    )


def pack_columns(u, packed, zn):
    pairs, _, rows, lanes = packed.shape
    f = rows // (zn // 2)
    yn = lanes // 2
    low = lax.broadcasted_iota(jnp.int32, (f, lanes), 1) < yn
    for j in range(pairs):
        for zh in range(zn // 2):
            first = u[(2 * zh) * f : (2 * zh + 1) * f, j * lanes : (j + 1) * lanes]
            second = u[(2 * zh + 1) * f : (2 * zh + 2) * f, j * lanes : (j + 1) * lanes]
            even = jnp.where(low, first, pltpu.roll(second, yn, 1))
            odd = jnp.where(low, pltpu.roll(first, yn, 1), second)
            packed[j, 0, zh * f : (zh + 1) * f, :] = even.astype(BF16)
            packed[j, 1, zh * f : (zh + 1) * f, :] = odd.astype(BF16)


def spread_kernel(got, v, w, xlo, xhi, zlo, zhi, ids):
    peers, rows, lanes = got.shape
    table = got[:, rows - 8 :, :].astype(F32).reshape(peers * 8, lanes).astype(BF16)
    members = 32
    per = lanes // GROUP
    source = lax.broadcasted_iota(jnp.int32, (lanes, lanes), 0)
    lane = lax.broadcasted_iota(jnp.int32, (lanes, lanes), 1)
    late = lax.broadcasted_iota(jnp.int32, (1, lanes), 1) % GROUP >= GROUP // 2
    halves = members // per
    for mh in range(halves):
        wanted = (lane % (GROUP // 2)) * members + mh * per + lane // GROUP
        moved = jnp.dot(
            table, jnp.where(source == wanted, 1.0, 0.0).astype(BF16), preferred_element_type=F32
        )
        for q in range(peers):
            for kg in range(3):
                r = q * 8 + 2 * kg
                line = jnp.where(late, moved[r + 1 : r + 2], moved[r : r + 1])
                at = kg * halves + mh
                ids[q, at : at + 1, :] = line.astype(jnp.int32)
    yn = lanes // 2
    zn = 4
    half = (rows - HALO_ROWS) // 2
    xl = w.shape[0] // zn
    f = half - xl
    comps = f // xl
    low = lax.broadcasted_iota(jnp.int32, (rows, lanes), 1) < yn
    for j in range(peers // 2):
        one = got[2 * j].astype(F32)
        two = got[2 * j + 1].astype(F32)
        sides = (
            jnp.where(low, one, pltpu.roll(two, yn, 1)),
            jnp.where(low, pltpu.roll(one, yn, 1), two),
        )
        at = slice(j * lanes, (j + 1) * lanes)
        for zh in range(zn // 2):
            for side in range(2):
                z = 2 * zh + side
                whole = sides[side]
                v[z * f : (z + 1) * f, at] = whole[zh * half : zh * half + f].astype(BF16)
                w[z * xl : (z + 1) * xl, at] = whole[zh * half + f : (zh + 1) * half].astype(BF16)
                r = zn // 2 * half + zh * comps
                xlo[z * comps : (z + 1) * comps, at] = whole[r : r + comps]
                r = r + zn // 2 * comps
                xhi[z * comps : (z + 1) * comps, at] = whole[r : r + comps]
    zlo[...] = v[0:f]
    zhi[...] = v[(zn - 1) * f : zn * f]


def explicit_plane(z, u, w, zlo, zhi, x_before, x_after, e):
    f, cols = zlo.shape
    zn = u.shape[0] // f
    xl = w.shape[0] // zn
    comps = f // xl
    row = lax.broadcasted_iota(jnp.int32, (xl, cols), 0)
    lane = lax.broadcasted_iota(jnp.int32, (xl, cols), 1)
    factor = diffusion_factor * w[z * xl : (z + 1) * xl].astype(F32)
    for c in range(comps):
        r = z * comps + c
        at = slice(r * xl, (r + 1) * xl)
        cur = u[at].astype(F32)
        if z > 0:
            total = u[(r - comps) * xl : (r - comps + 1) * xl].astype(F32)
        else:
            total = zlo[c * xl : (c + 1) * xl].astype(F32)
        if z < zn - 1:
            total = total + u[(r + comps) * xl : (r + comps + 1) * xl].astype(F32)
        else:
            total = total + zhi[c * xl : (c + 1) * xl].astype(F32)
        total = total + jnp.where(row == 0, x_before[r : r + 1], pltpu.roll(cur, 1, 0))
        total = total + jnp.where(row == xl - 1, x_after[r : r + 1], pltpu.roll(cur, xl - 1, 0))
        total = total + jnp.where(lane == 0, 0.0, pltpu.roll(cur, 1, 1))
        total = total + jnp.where(lane == cols - 1, 0.0, pltpu.roll(cur, cols - 1, 1))
        e[at] = (cur + factor * (total - 6.0 * cur)).astype(BF16)


def first_kernel(
    v, w, xlo, xhi, zlo, zhi, a, u, packed, z_first, z_last, x_first, x_last, e
):
    x_before, x_after = xlo[...], xhi[...]
    zn = 4
    for z in range(zn):
        explicit_plane(z, v, w, zlo, zhi, x_before, x_after, e)
    u[...] = solve(e, a)
    f = zlo.shape[0]
    z_first[...] = u[0:f].astype(BF16)
    z_last[...] = u[(zn - 1) * f : zn * f].astype(BF16)
    xl = w.shape[0] // zn
    groups = u.shape[0] // xl
    for r in range(groups):
        x_first[r : r + 1] = u[r * xl : r * xl + 1]
        x_last[r : r + 1] = u[(r + 1) * xl - 1 : (r + 1) * xl]
    pack_columns(u, packed, zn)


def sample_kernel(packed, ids, sent_far, picked, sent, sems):
    copies = Copies(sems)
    sample(packed, ids, picked, sent, message_part(copies, sent, sent_far, 0))
    copies.finish()


def message_part(copies, sent, far, which):
    f = sent.shape[1]

    def ready(part):
        members, _, lanes = part
        copies.start(sent.at[part], far.at[members, pl.ds(which * f, f), lanes])

    return ready


def second_kernel(
    u, w, ids, zlo, zhi, xlo, xhi, a, sent_in, packed_far, sent_far,
    e, after, packed, picked, sent, sems,
):
    del sent_in
    copies = Copies(sems)
    zn = u.shape[0] // zlo.shape[0]
    x_before, x_after = xlo[...], xhi[...]
    for z in range(zn):
        explicit_plane(z, u, w, zlo, zhi, x_before, x_after, e)
    after[...] = solve(e, a)
    pack_columns(after, packed, zn)
    copies.start(packed, packed_far)
    sample(packed, ids, picked, sent, message_part(copies, sent, sent_far, 1))
    copies.finish()


def sample(packed, ids, picked, out, ready):
    pairs, _, rows, lanes = packed.shape
    peers = 2 * pairs
    f = rows // 2
    yn = lanes // 2
    blocks = picked.shape[2] // lanes
    r = lax.broadcasted_iota(jnp.int32, (2 * lanes, lanes), 0)
    row_id = (r % yn) * 4 + r // yn
    for q in range(peers):
        at = (q // 2, q % 2)
        table = jnp.concatenate([packed[(*at, slice(0, f))], packed[(*at, slice(f, rows))]], axis=1)
        wanted = pltpu.roll(ids[q], (GROUP * q) % lanes, 1) if q else ids[q]
        for b in range(blocks):
            hot = jnp.where(row_id == wanted[b : b + 1], 1.0, 0.0).astype(BF16)
            picked[q, :, b * lanes : (b + 1) * lanes] = jnp.dot(
                table, hot, preferred_element_type=F32
            )
    group = lax.broadcasted_iota(jnp.int32, (f, lanes), 1) // GROUP
    per = lanes // GROUP
    halves = out.shape[0] // per
    for b in range(blocks):
        kg, mh = b // halves, b % halves
        held = [picked[q, :, b * lanes : (b + 1) * lanes] for q in range(peers)]
        step = 1
        while step < peers:
            take = (group // step) % 2 == 1
            held = [jnp.where(take, held[(i + step) % peers], held[i]) for i in range(peers)]
            step *= 2
        for ml in range(per):
            out[mh * per + ml, :, kg * lanes : (kg + 1) * lanes] = held[(-ml) % peers].astype(BF16)
        ready((pl.ds(mh * per, per), slice(None), pl.ds(kg * lanes, lanes)))


def gather_rows(got, start, turned, comps=3):
    sources, both, slots = got.shape
    sides = 2
    peers = sources // sides
    xl = both // 2 // comps
    for q in range(peers):
        for side in range(sides):
            for c in range(comps):
                at = (c * peers + q) * xl
                turned[at : at + xl, side * slots : (side + 1) * slots] = got[
                    q * sides + side, start + c * xl : start + (c + 1) * xl
                ]


CONTRACT_ROWS = (((1,), (1,)), ((), ()))


def over_rows(left, right):
    return lax.dot_general(left, right, CONTRACT_ROWS, preferred_element_type=F32)


def over_first(left, right):
    return lax.dot_general(left, right, (((0,), (0,)), ((), ())), preferred_element_type=F32)


def forward_kernel(
    scale, place, got, w_in_far, w_out_far, x, hidden, slope, d, away, w_in, w_out, sems
):
    copies = Copies(sems)
    f = got.shape[1] // 2
    wide = 512
    count = hidden.shape[0] // wide
    parts = [(slice(None), pl.ds(i * wide, wide)) for i in range(count)]
    arriving = copies.start(w_in_far.at[parts[0]], w_in.at[parts[0]])
    gather_rows(got, 0, x)
    for i in range(count):
        at = slice(i * wide, (i + 1) * wide)
        copies.wait(arriving)
        if i + 1 < count:
            arriving = copies.start(w_in_far.at[parts[i + 1]], w_in.at[parts[i + 1]])
        else:
            copies.start(w_out_far, w_out)
        pre = over_first(w_in[:, at], x[...])
        logistic = jax.nn.sigmoid(pre)
        hidden[at, :] = (pre * logistic).astype(BF16)
        slope[at, :] = (logistic * (1.0 + pre * (1.0 - logistic))).astype(slope.dtype)
    gather_rows(got, f, d)
    copies.finish()
    predicted = over_first(w_out[...], hidden[...])
    d[...] = ((predicted - d[...].astype(F32)) * scale).astype(BF16)
    away_blocks(hidden, d, place[0], away, away.shape[0] // 4)


def block_rows(array, y, core, rows):
    return array[pl.ds(pl.multiple_of((2 * y + core) * rows, rows), rows), :]


def away_blocks(array, right, core, away, rows):
    left = jnp.concatenate([block_rows(array, y, 1 - core, rows) for y in range(4)], axis=0)
    away[...] = over_rows(left, right[...]).astype(BF16)


def delta_in_kernel(place, d, slope, w_out, x, din, away):
    wide = 512
    for i in range(din.shape[0] // wide):
        at = slice(i * wide, (i + 1) * wide)
        back = jnp.dot(w_out[at, :], d[...], preferred_element_type=F32)
        din[at, :] = (back * slope[at, :].astype(F32)).astype(BF16)
    away_blocks(x, din, place[0], away, away.shape[0] // 4)


def fold(block, rows, width):
    extra = rows - block.shape[0]
    pieces = [block[g * extra : (g + 1) * extra, width:] for g in range(block.shape[0] // extra)]
    return jnp.concatenate([block[:, :width], jnp.concatenate(pieces, axis=1)], axis=0)


def unfold(block, rows):
    extra = block.shape[0] - rows
    count = rows // extra
    wide = block.shape[1] // count
    pieces = [block[rows:, g * wide : (g + 1) * wide] for g in range(count)]
    return jnp.concatenate([block[:rows], jnp.concatenate(pieces, axis=0)], axis=1)


def own_blocks(place, array, rows):
    core, y = place[0], place[1]
    return jnp.concatenate(
        [block_rows(array, lax.rem(y + k, 4), core, rows) for k in (2, 1, 3, 0)], axis=0
    )


def add_other_core(place, value, got, n, k):
    rows = value.shape[0] // 4
    at = pl.multiple_of(lax.rem(place[1] + k, 4) * rows, rows)
    return value[n * rows : (n + 1) * rows] + got[pl.ds(at, rows), :].astype(F32)


def keep_out_kernel(place, hidden, d, got, own, plus, minus, far):
    value = over_rows(own_blocks(place, hidden, own.shape[0]), d[...])
    far[...] = add_other_core(place, value, got, 0, 2).astype(BF16)
    plus[...] = add_other_core(place, value, got, 1, 1).astype(BF16)
    minus[...] = add_other_core(place, value, got, 2, 3).astype(BF16)
    own[...] = add_other_core(place, value, got, 3, 0)


def keep_in_kernel(
    place, x, din, got, plus_out, minus_out, far_out, own, plus, minus, top, bottom
):
    rows, width = plus_out.shape
    half = rows // 2
    plus[0] = plus_out[...]
    minus[0] = minus_out[...]
    top[0] = far_out[:half]
    bottom[0] = far_out[half:]
    value = over_rows(own_blocks(place, x, own.shape[0]), din[...])
    far = fold(add_other_core(place, value, got, 0, 2), rows, width).astype(BF16)
    top[1] = far[:half]
    bottom[1] = far[half:]
    plus[1] = fold(add_other_core(place, value, got, 1, 1), rows, width).astype(BF16)
    minus[1] = fold(add_other_core(place, value, got, 2, 3), rows, width).astype(BF16)
    own[...] = add_other_core(place, value, got, 3, 0)


def relay_kernel(plus, minus, from_before, from_after, plus_out, minus_out):
    half = from_before.shape[1]
    for which in range(plus.shape[0]):
        plus_out[which, :half] = (
            plus[which, :half].astype(F32) + from_before[which].astype(F32)
        ).astype(BF16)
        plus_out[which, half:] = plus[which, half:]
        minus_out[which, :half] = minus[which, :half]
        minus_out[which, half:] = (
            minus[which, half:].astype(F32) + from_after[which].astype(F32)
        ).astype(BF16)


def finish_kernel(own_out, own_in, from_before, from_after, share_out, share_in):
    total = [from_before[k].astype(F32) + from_after[k].astype(F32) for k in range(2)]
    share_out[...] = own_out[...] + total[0]
    share_in[...] = own_in[...] + unfold(total[1], share_in.shape[0])


def planes_kernel(got, out):
    yn, comps, zn, xn = out.shape
    peers = got.shape[0]
    xl = xn // peers
    f = comps * xl
    for zh in range(zn // 2):
        for c in range(comps):
            base = zh * f + c * xl
            block = jnp.concatenate(
                [got[q, base : base + xl, :] for q in range(peers)], axis=0
            ).astype(F32)
            turned = block.T
            out[:, c, 2 * zh, :] = turned[0:yn]
            out[:, c, 2 * zh + 1, :] = turned[yn : 2 * yn]


def exchange(array, axis):
    return lax.all_to_all(array, axis, split_axis=0, concat_axis=0, tiled=True)


def swap_cores(array):
    size = lax.axis_size("px")
    return lax.ppermute(array, "px", [(i, i ^ 1) for i in range(size)])


def shift_chips(forward, backward):
    size = lax.axis_size("px")
    up = [(i, (i + 2) % size) for i in range(size)]
    down = [(j, i) for i, j in up]
    return lax.ppermute(forward, "px", up), lax.ppermute(backward, "px", down)


def per_device(velocity, viscosity, implicit_inverse, row_index, row_counts, weight_in, weight_out):
    yn, zn, comps, xn = velocity.shape
    peers = lax.axis_size("pz")
    position = lax.axis_index("px")
    place = jnp.stack([position & 1, position >> 1]).astype(jnp.int32)
    total_y = yn * peers
    xl = xn // peers
    f = comps * xl
    lanes = 2 * yn
    members, slots = row_index.shape[3:]

    sent = call(
        columns_kernel,
        shaped((peers, 2 * (f + xl) + HALO_ROWS, lanes), BF16),
        (
            velocity.transpose(0, 2, 1, 3),
            viscosity,
            row_index.reshape(members, slots).T,
            row_counts.reshape(1, members),
        ),
        scratch=[
            pltpu.VMEM((yn, comps, zn, xn), F32),
            pltpu.VMEM((yn, zn, xn), F32),
            pltpu.VMEM((slots, members), jnp.int32),
            pltpu.VMEM((1, members), jnp.int32),
            pltpu.VMEM((peers * HALO_ROWS, lanes), F32),
            pltpu.SemaphoreType.DMA((4,)),
        ],
        far_in=range(4),
    )
    inverse = implicit_inverse.astype(BF16)
    got = exchange(sent, "pz")
    solve_flops = 2 * zn * f * total_y * total_y
    edge = shaped((f, total_y), BF16)
    x_edge = shaped((zn * comps, total_y), F32)
    ids_all = shaped((peers, 8, lanes), jnp.int32)
    v, w, xlo, xhi, zlo, zhi, ids = call(
        spread_kernel,
        (shaped((zn * f, total_y), BF16), shaped((zn * xl, total_y), BF16))
        + (x_edge, x_edge, edge, edge, ids_all),
        (got,),
    )
    zlo, zhi = shift((zhi, zlo), ("px", "tr"))
    message = shaped((members, f, peers * slots), BF16)
    both = shaped((members, 2 * f, peers * slots), BF16)
    sample_flops = 2 * peers * f * 256 * members * slots
    sampling = [
        pltpu.VMEM((peers, 2 * f, lanes), BF16),
        pltpu.VMEM((peers, f, members * slots), F32),
        pltpu.VMEM(message.shape, BF16),
    ]
    blocks = shaped((peers // 2, 2, 2 * f, lanes), BF16)
    half_blocks = shaped((peers // 2, 2 * f, lanes), BF16)
    sampling[0] = pltpu.VMEM(blocks.shape, BF16)
    u, packed, z_first, z_last, x_first, x_last = call(
        first_kernel,
        (shaped((zn * f, total_y), F32), blocks, edge, edge, x_edge, x_edge),
        (v, w, xlo, xhi, zlo, zhi, inverse),
        scratch=[pltpu.VMEM((zn * f, total_y), BF16)],
        flops=solve_flops,
    )
    zlo, zhi = shift((z_last, z_first), ("px", "tr"))
    xlo, xhi = shift((x_last, x_first), "pz")
    sent = call(
        sample_kernel,
        both,
        (packed, ids),
        scratch=sampling[1:] + [pltpu.SemaphoreType.DMA((6,))],
        flops=sample_flops,
        far_out=(0,),
    )
    packed, sent = call(
        second_kernel,
        (blocks, both),
        (u, w, ids, zlo, zhi, xlo, xhi, inverse, sent),
        scratch=[pltpu.VMEM((zn * f, total_y), BF16), pltpu.VMEM((zn * f, total_y), F32)]
        + sampling
        + [pltpu.SemaphoreType.DMA((7,))],
        flops=solve_flops + sample_flops,
        far_in=(8,),
        far_out=(0, 1),
        aliases={8: 1},
    )
    rows_all = exchange(sent, ("pz", "tr"))

    member_in = weight_in[0]
    member_out = weight_out[0]
    width, hid = member_in.shape
    batch = 2 * peers * slots
    spots = lax.axis_size("px")
    loss_scale = 1.0 / math.sqrt(spots * batch)
    matmul_flops = 2 * hid * width * batch

    def forward(*refs):
        forward_kernel(loss_scale, *refs)

    x, hidden, slope, d, away_out = call(
        forward,
        (
            shaped((width, batch), BF16),
            shaped((hid, batch), BF16),
            shaped((hid, batch), BF16),
            shaped((width, batch), BF16),
            shaped((hid // 2, width), BF16),
        ),
        (place, rows_all, member_in, member_out),
        scratch=[
            pltpu.VMEM((width, hid), BF16),
            pltpu.VMEM((hid, width), BF16),
            pltpu.SemaphoreType.DMA((3,)),
        ],
        flops=matmul_flops * 5 // 2,
        far_in=(2, 3),
    )
    got_out = swap_cores(away_out)
    din, away_in = call(
        delta_in_kernel,
        (shaped((hid, batch), BF16), shaped((width // 2, hid), BF16)),
        (place, d, slope, member_out, x),
        flops=matmul_flops * 3 // 2,
    )
    got_in = swap_cores(away_in)

    rows_out, rows_in = hid // spots, width // spots
    block = shaped((rows_out, width), BF16)
    own_out, plus, minus, far = call(
        keep_out_kernel,
        (shaped((rows_out, width), F32), block, block, block),
        (place, hidden, d, got_out),
        flops=matmul_flops // 2,
    )
    block = shaped((2, rows_out, width), BF16)
    part = shaped((2, rows_out // 2, width), BF16)
    own_in, plus, minus, top, bottom = call(
        keep_in_kernel,
        (shaped((rows_in, hid), F32), block, block, part, part),
        (place, x, din, got_in, plus, minus, far),
        flops=matmul_flops // 2,
    )
    packed, top = lax.optimization_barrier((packed, top))
    arrived = shift_chips(top, bottom)
    planes = exchange(packed.reshape(peers, 2 * f, lanes), "pz")
    plus, minus = call(relay_kernel, (block, block), (plus, minus, *arrived), flops=6e9)
    arrived = shift_chips(plus, minus)
    share_out, share_in = call(
        finish_kernel,
        (shaped((rows_out, width), F32), shaped((rows_in, hid), F32)),
        (own_out, own_in, *arrived),
        flops=1e6,
    )
    result = call(planes_kernel, shaped((yn, comps, zn, xn), F32), (planes,))
    return (result.transpose(0, 2, 1, 3), share_in[None], share_out[None])


def solution(mesh):
    in_specs = (
        P("pz", ("px", "tr"), None, None),
        P("pz", ("px", "tr"), None),
        P(),
        P("px", "pz", "tr", None, None),
        P("px", "pz", "tr", None),
        P(("pz", "tr"), None, None),
        P(("pz", "tr"), None, None),
    )
    out_specs = (
        P("pz", ("px", "tr"), None, None),
        P(("pz", "tr"), "px", None),
        P(("pz", "tr"), "px", None),
    )
    return jax.shard_map(
        per_device, mesh=mesh, in_specs=in_specs, out_specs=out_specs, check_vma=False
    )
```

```python
import math

import jax
import jax.numpy as jnp
from jax import lax
from jax.experimental import pallas as pl
from jax.experimental.pallas import tpu as pltpu
from jax.sharding import PartitionSpec as P

diffusion_factor = 0.08
F32 = jnp.float32
BF16 = jnp.bfloat16
MIB = 1 << 20


def call(kernel, out_shape, args, scratch=(), flops=1e6, far_in=(), far_out=(), aliases=None):
    outs = jax.tree.leaves(out_shape)
    size = lambda x: math.prod(x.shape) * jnp.dtype(x.dtype).itemsize
    near = [x for k, x in enumerate(args) if k not in far_in]
    near += [x for k, x in enumerate(outs) if k not in far_out]
    held = sum(size(x) for x in near) + sum(size(x) for x in scratch if x.dtype in (F32, BF16, jnp.int32))

    def spec(k, far, scalar=False):
        space = pltpu.HBM if k in far else pltpu.SMEM if scalar else pltpu.VMEM
        return pl.BlockSpec(memory_space=space)

    out_specs = tuple(spec(k, far_out) for k in range(len(outs)))
    args = [
        pltpu.with_memory_space_constraint(x, pltpu.HBM) if k in far_in else x
        for k, x in enumerate(args)
    ]
    pinned = tuple(
        pltpu.HBM(x.shape, x.dtype) if k in far_out else x for k, x in enumerate(outs)
    )
    return pl.pallas_call(
        kernel,
        out_shape=pinned if isinstance(out_shape, tuple) else pinned[0],
        in_specs=[spec(k, far_in, x.ndim == 1) for k, x in enumerate(args)],
        out_specs=out_specs if isinstance(out_shape, tuple) else out_specs[0],
        scratch_shapes=list(scratch),
        input_output_aliases=aliases or {},
        compiler_params=pltpu.CompilerParams(vmem_limit_bytes=held + 6 * MIB),
        cost_estimate=pl.CostEstimate(
            flops=int(flops),
            bytes_accessed=int(sum(size(x) for x in list(args) + outs)),
            transcendentals=0,
        ),
    )(*args)


class Copies:
    def __init__(self, sems):
        self.sems, self.used, self.open = sems, 0, []

    def start(self, source, target):
        copy = pltpu.make_async_copy(source, target, self.sems.at[self.used])
        copy.start()
        self.used += 1
        self.open.append(copy)
        return copy

    def finish(self):
        for copy in self.open:
            copy.wait()
        self.open = []

    def wait(self, copy):
        copy.wait()
        self.open.remove(copy)


def shaped(shape, dtype):
    return jax.ShapeDtypeStruct(shape, dtype)


def shift(array, axis, wrap=True):
    last, first = array
    size = lax.axis_size(axis)
    up = [(i, (i + 1) % size) for i in range(size if wrap else size - 1)]
    down = [(j, i) for i, j in up]
    return lax.ppermute(last, axis, up), lax.ppermute(first, axis, down)


HALO_ROWS = 24
GROUP = 8


def columns_kernel(v_far, w_far, index_far, counts_far, out, v, w, index, counts, edge, sems):
    copies = Copies(sems)
    for far, near in ((index_far, index), (counts_far, counts), (w_far, w), (v_far, v)):
        copies.start(far, near)
    copies.finish()
    yn, comps, zn, xn = v.shape
    peers = out.shape[0]
    xl = xn // peers
    lanes_of = out.shape[2]
    half = (comps + 1) * xl
    for zh in range(zn // 2):
        for c in range(comps + 1):
            pair = [w[:, z, :] if c == comps else v[:, c, z, :] for z in (2 * zh, 2 * zh + 1)]
            turned = jnp.concatenate(pair, axis=0).T
            base = zh * half + c * xl
            for q in range(peers):
                out[q, base : base + xl, :] = turned[q * xl : (q + 1) * xl].astype(BF16)
            if c == comps:
                continue
            for q in range(peers):
                before = (q * xl - 1) % xn
                after = (q + 1) * xl % xn
                r = q * HALO_ROWS + zh * comps + c
                edge[r : r + 1] = turned[before : before + 1]
                edge[r + zn // 2 * comps : r + zn // 2 * comps + 1] = turned[after : after + 1]
    start = zn // 2 * half
    slots, members = index.shape
    slot = lax.broadcasted_iota(jnp.int32, (slots, members), 0)
    live = jnp.where(slot < counts[...], index[...], -1).astype(F32)
    sides = lanes_of // members
    rows = slots // sides
    numbers = jnp.concatenate([live[k * rows : (k + 1) * rows] for k in range(sides)], axis=1)
    numbers = jnp.concatenate([numbers, jnp.zeros((8 - rows, lanes_of), F32)], axis=0)
    for q in range(peers):
        edge[(q + 1) * HALO_ROWS - 8 : (q + 1) * HALO_ROWS] = numbers
        out[q, start : start + HALO_ROWS, :] = edge[
            q * HALO_ROWS : (q + 1) * HALO_ROWS
        ].astype(BF16)


def solve(e, a):
    return lax.dot_general(
        e[...], a[...], (((1,), (1,)), ((), ())), preferred_element_type=F32
    )


def pack_columns(u, packed, zn):
    pairs, _, rows, lanes = packed.shape
    f = rows // (zn // 2)
    yn = lanes // 2
    low = lax.broadcasted_iota(jnp.int32, (f, lanes), 1) < yn
    for j in range(pairs):
        for zh in range(zn // 2):
            first = u[(2 * zh) * f : (2 * zh + 1) * f, j * lanes : (j + 1) * lanes]
            second = u[(2 * zh + 1) * f : (2 * zh + 2) * f, j * lanes : (j + 1) * lanes]
            even = jnp.where(low, first, pltpu.roll(second, yn, 1))
            odd = jnp.where(low, pltpu.roll(first, yn, 1), second)
            packed[j, 0, zh * f : (zh + 1) * f, :] = even.astype(BF16)
            packed[j, 1, zh * f : (zh + 1) * f, :] = odd.astype(BF16)


def spread_kernel(got, v, w, xlo, xhi, zlo, zhi, ids):
    peers, rows, lanes = got.shape
    table = got[:, rows - 8 :, :].astype(F32).reshape(peers * 8, lanes).astype(BF16)
    members = 32
    per = lanes // GROUP
    source = lax.broadcasted_iota(jnp.int32, (lanes, lanes), 0)
    lane = lax.broadcasted_iota(jnp.int32, (lanes, lanes), 1)
    late = lax.broadcasted_iota(jnp.int32, (1, lanes), 1) % GROUP >= GROUP // 2
    halves = members // per
    for mh in range(halves):
        wanted = (lane % (GROUP // 2)) * members + mh * per + lane // GROUP
        moved = jnp.dot(
            table, jnp.where(source == wanted, 1.0, 0.0).astype(BF16), preferred_element_type=F32
        )
        for q in range(peers):
            for kg in range(3):
                r = q * 8 + 2 * kg
                line = jnp.where(late, moved[r + 1 : r + 2], moved[r : r + 1])
                at = kg * halves + mh
                ids[q, at : at + 1, :] = line.astype(jnp.int32)
    yn = lanes // 2
    zn = 4
    half = (rows - HALO_ROWS) // 2
    xl = w.shape[0] // zn
    f = half - xl
    comps = f // xl
    low = lax.broadcasted_iota(jnp.int32, (rows, lanes), 1) < yn
    for j in range(peers // 2):
        one = got[2 * j].astype(F32)
        two = got[2 * j + 1].astype(F32)
        sides = (
            jnp.where(low, one, pltpu.roll(two, yn, 1)),
            jnp.where(low, pltpu.roll(one, yn, 1), two),
        )
        at = slice(j * lanes, (j + 1) * lanes)
        for zh in range(zn // 2):
            for side in range(2):
                z = 2 * zh + side
                whole = sides[side]
                v[z * f : (z + 1) * f, at] = whole[zh * half : zh * half + f].astype(BF16)
                w[z * xl : (z + 1) * xl, at] = whole[zh * half + f : (zh + 1) * half].astype(BF16)
                r = zn // 2 * half + zh * comps
                xlo[z * comps : (z + 1) * comps, at] = whole[r : r + comps]
                r = r + zn // 2 * comps
                xhi[z * comps : (z + 1) * comps, at] = whole[r : r + comps]
    zlo[...] = v[0:f]
    zhi[...] = v[(zn - 1) * f : zn * f]


def explicit_plane(z, u, w, zlo, zhi, x_before, x_after, e):
    f, cols = zlo.shape
    zn = u.shape[0] // f
    xl = w.shape[0] // zn
    comps = f // xl
    row = lax.broadcasted_iota(jnp.int32, (xl, cols), 0)
    lane = lax.broadcasted_iota(jnp.int32, (xl, cols), 1)
    factor = diffusion_factor * w[z * xl : (z + 1) * xl].astype(F32)
    for c in range(comps):
        r = z * comps + c
        at = slice(r * xl, (r + 1) * xl)
        cur = u[at].astype(F32)
        if z > 0:
            total = u[(r - comps) * xl : (r - comps + 1) * xl].astype(F32)
        else:
            total = zlo[c * xl : (c + 1) * xl].astype(F32)
        if z < zn - 1:
            total = total + u[(r + comps) * xl : (r + comps + 1) * xl].astype(F32)
        else:
            total = total + zhi[c * xl : (c + 1) * xl].astype(F32)
        total = total + jnp.where(row == 0, x_before[r : r + 1], pltpu.roll(cur, 1, 0))
        total = total + jnp.where(row == xl - 1, x_after[r : r + 1], pltpu.roll(cur, xl - 1, 0))
        total = total + jnp.where(lane == 0, 0.0, pltpu.roll(cur, 1, 1))
        total = total + jnp.where(lane == cols - 1, 0.0, pltpu.roll(cur, cols - 1, 1))
        e[at] = (cur + factor * (total - 6.0 * cur)).astype(BF16)


def first_kernel(
    v, w, xlo, xhi, zlo, zhi, a, u, packed, z_first, z_last, x_first, x_last, e
):
    x_before, x_after = xlo[...], xhi[...]
    zn = 4
    for z in range(zn):
        explicit_plane(z, v, w, zlo, zhi, x_before, x_after, e)
    u[...] = solve(e, a)
    f = zlo.shape[0]
    z_first[...] = u[0:f].astype(BF16)
    z_last[...] = u[(zn - 1) * f : zn * f].astype(BF16)
    xl = w.shape[0] // zn
    groups = u.shape[0] // xl
    for r in range(groups):
        x_first[r : r + 1] = u[r * xl : r * xl + 1]
        x_last[r : r + 1] = u[(r + 1) * xl - 1 : (r + 1) * xl]
    pack_columns(u, packed, zn)


def sample_kernel(packed, ids, sent_far, picked, sent, sems):
    copies = Copies(sems)
    sample(packed, ids, picked, sent, message_part(copies, sent, sent_far, 0))
    copies.finish()


def message_part(copies, sent, far, which):
    f = sent.shape[1]

    def ready(part):
        members, _, lanes = part
        copies.start(sent.at[part], far.at[members, pl.ds(which * f, f), lanes])

    return ready


def second_kernel(
    u, w, ids, zlo, zhi, xlo, xhi, a, sent_in, packed_far, sent_far,
    e, after, packed, picked, sent, sems,
):
    del sent_in
    copies = Copies(sems)
    zn = u.shape[0] // zlo.shape[0]
    x_before, x_after = xlo[...], xhi[...]
    for z in range(zn):
        explicit_plane(z, u, w, zlo, zhi, x_before, x_after, e)
    after[...] = solve(e, a)
    pack_columns(after, packed, zn)
    copies.start(packed, packed_far)
    sample(packed, ids, picked, sent, message_part(copies, sent, sent_far, 1))
    copies.finish()


def sample(packed, ids, picked, out, ready):
    pairs, _, rows, lanes = packed.shape
    peers = 2 * pairs
    f = rows // 2
    yn = lanes // 2
    blocks = picked.shape[2] // lanes
    r = lax.broadcasted_iota(jnp.int32, (2 * lanes, lanes), 0)
    row_id = (r % yn) * 4 + r // yn
    for q in range(peers):
        at = (q // 2, q % 2)
        table = jnp.concatenate([packed[(*at, slice(0, f))], packed[(*at, slice(f, rows))]], axis=1)
        wanted = pltpu.roll(ids[q], (GROUP * q) % lanes, 1) if q else ids[q]
        for b in range(blocks):
            hot = jnp.where(row_id == wanted[b : b + 1], 1.0, 0.0).astype(BF16)
            picked[q, :, b * lanes : (b + 1) * lanes] = jnp.dot(
                table, hot, preferred_element_type=F32
            )
    group = lax.broadcasted_iota(jnp.int32, (f, lanes), 1) // GROUP
    per = lanes // GROUP
    halves = out.shape[0] // per
    for b in range(blocks):
        kg, mh = b // halves, b % halves
        held = [picked[q, :, b * lanes : (b + 1) * lanes] for q in range(peers)]
        step = 1
        while step < peers:
            take = (group // step) % 2 == 1
            held = [jnp.where(take, held[(i + step) % peers], held[i]) for i in range(peers)]
            step *= 2
        for ml in range(per):
            out[mh * per + ml, :, kg * lanes : (kg + 1) * lanes] = held[(-ml) % peers].astype(BF16)
        ready((pl.ds(mh * per, per), slice(None), pl.ds(kg * lanes, lanes)))


def gather_rows(got, start, turned, comps=3):
    sources, both, slots = got.shape
    sides = 2
    peers = sources // sides
    xl = both // 2 // comps
    for q in range(peers):
        for side in range(sides):
            for c in range(comps):
                at = (c * peers + q) * xl
                turned[at : at + xl, side * slots : (side + 1) * slots] = got[
                    q * sides + side, start + c * xl : start + (c + 1) * xl
                ]


CONTRACT_ROWS = (((1,), (1,)), ((), ()))


def over_rows(left, right):
    return lax.dot_general(left, right, CONTRACT_ROWS, preferred_element_type=F32)


def over_first(left, right):
    return lax.dot_general(left, right, (((0,), (0,)), ((), ())), preferred_element_type=F32)


def forward_kernel(
    scale, place, got, w_in_far, w_out_far, x, hidden, slope, d, away, w_in, w_out, sems
):
    copies = Copies(sems)
    f = got.shape[1] // 2
    wide = 512
    count = hidden.shape[0] // wide
    parts = [(slice(None), pl.ds(i * wide, wide)) for i in range(count)]
    arriving = copies.start(w_in_far.at[parts[0]], w_in.at[parts[0]])
    gather_rows(got, 0, x)
    for i in range(count):
        at = slice(i * wide, (i + 1) * wide)
        copies.wait(arriving)
        if i + 1 < count:
            arriving = copies.start(w_in_far.at[parts[i + 1]], w_in.at[parts[i + 1]])
        else:
            copies.start(w_out_far, w_out)
        pre = over_first(w_in[:, at], x[...])
        logistic = jax.nn.sigmoid(pre)
        hidden[at, :] = (pre * logistic).astype(BF16)
        slope[at, :] = (logistic * (1.0 + pre * (1.0 - logistic))).astype(slope.dtype)
    gather_rows(got, f, d)
    copies.finish()
    predicted = over_first(w_out[...], hidden[...])
    d[...] = ((predicted - d[...].astype(F32)) * scale).astype(BF16)
    away_blocks(hidden, d, place[0], away, away.shape[0] // 4)


def block_rows(array, y, core, rows):
    return array[pl.ds(pl.multiple_of((2 * y + core) * rows, rows), rows), :]


def away_blocks(array, right, core, away, rows):
    left = jnp.concatenate([block_rows(array, y, 1 - core, rows) for y in range(4)], axis=0)
    away[...] = over_rows(left, right[...]).astype(BF16)


def delta_in_kernel(place, d, slope, w_out, x, din, away):
    wide = 512
    for i in range(din.shape[0] // wide):
        at = slice(i * wide, (i + 1) * wide)
        back = jnp.dot(w_out[at, :], d[...], preferred_element_type=F32)
        din[at, :] = (back * slope[at, :].astype(F32)).astype(BF16)
    away_blocks(x, din, place[0], away, away.shape[0] // 4)


def fold(block, rows, width):
    extra = rows - block.shape[0]
    pieces = [block[g * extra : (g + 1) * extra, width:] for g in range(block.shape[0] // extra)]
    return jnp.concatenate([block[:, :width], jnp.concatenate(pieces, axis=1)], axis=0)


def unfold(block, rows):
    extra = block.shape[0] - rows
    count = rows // extra
    wide = block.shape[1] // count
    pieces = [block[rows:, g * wide : (g + 1) * wide] for g in range(count)]
    return jnp.concatenate([block[:rows], jnp.concatenate(pieces, axis=0)], axis=1)


def own_blocks(place, array, rows):
    core, y = place[0], place[1]
    return jnp.concatenate(
        [block_rows(array, lax.rem(y + k, 4), core, rows) for k in (2, 1, 3, 0)], axis=0
    )


def add_other_core(place, value, got, n, k):
    rows = value.shape[0] // 4
    at = pl.multiple_of(lax.rem(place[1] + k, 4) * rows, rows)
    return value[n * rows : (n + 1) * rows] + got[pl.ds(at, rows), :].astype(F32)


def keep_out_kernel(place, hidden, d, got, own, plus, minus, far):
    value = over_rows(own_blocks(place, hidden, own.shape[0]), d[...])
    far[...] = add_other_core(place, value, got, 0, 2).astype(BF16)
    plus[...] = add_other_core(place, value, got, 1, 1).astype(BF16)
    minus[...] = add_other_core(place, value, got, 2, 3).astype(BF16)
    own[...] = add_other_core(place, value, got, 3, 0)


def keep_in_kernel(
    place, x, din, got, plus_out, minus_out, far_out, own, up, down, plus, minus
):
    rows, width = plus_out.shape
    half = rows // 2

    def put(which, far_block, plus_block, minus_block):
        up[which, :half] = far_block[:half]
        up[which, half:] = plus_block[half:]
        down[which, :half] = minus_block[:half]
        down[which, half:] = far_block[half:]
        plus[which] = plus_block[:half]
        minus[which] = minus_block[half:]

    put(0, far_out[...], plus_out[...], minus_out[...])
    value = over_rows(own_blocks(place, x, own.shape[0]), din[...])
    put(
        1,
        *(
            fold(add_other_core(place, value, got, n, k), rows, width).astype(BF16)
            for n, k in ((0, 2), (1, 1), (2, 3))
        ),
    )
    own[...] = add_other_core(place, value, got, 3, 0)


def relay_kernel(plus, minus, from_before, from_after, up, down):
    half = plus.shape[1]
    for which in range(plus.shape[0]):
        before = from_before[which, :half].astype(F32)
        after = from_after[which, half:].astype(F32)
        up[which] = (plus[which].astype(F32) + before).astype(BF16)
        down[which] = (minus[which].astype(F32) + after).astype(BF16)


def finish_kernel(
    own_out, own_in, first_before, first_after, last_before, last_after, share_out, share_in
):
    half = last_before.shape[1]
    total = []
    for k in range(2):
        upper = first_after[k, :half].astype(F32) + last_before[k].astype(F32)
        lower = first_before[k, half:].astype(F32) + last_after[k].astype(F32)
        total.append(jnp.concatenate([upper, lower], axis=0))
    share_out[...] = own_out[...] + total[0]
    share_in[...] = own_in[...] + unfold(total[1], share_in.shape[0])


def planes_kernel(got, out):
    yn, comps, zn, xn = out.shape
    peers = got.shape[0]
    xl = xn // peers
    f = comps * xl
    for zh in range(zn // 2):
        for c in range(comps):
            base = zh * f + c * xl
            block = jnp.concatenate(
                [got[q, base : base + xl, :] for q in range(peers)], axis=0
            ).astype(F32)
            turned = block.T
            out[:, c, 2 * zh, :] = turned[0:yn]
            out[:, c, 2 * zh + 1, :] = turned[yn : 2 * yn]


def exchange(array, axis):
    return lax.all_to_all(array, axis, split_axis=0, concat_axis=0, tiled=True)


def swap_cores(array):
    size = lax.axis_size("px")
    return lax.ppermute(array, "px", [(i, i ^ 1) for i in range(size)])


def shift_chips(forward, backward):
    size = lax.axis_size("px")
    up = [(i, (i + 2) % size) for i in range(size)]
    down = [(j, i) for i, j in up]
    return lax.ppermute(forward, "px", up), lax.ppermute(backward, "px", down)


def per_device(velocity, viscosity, implicit_inverse, row_index, row_counts, weight_in, weight_out):
    yn, zn, comps, xn = velocity.shape
    peers = lax.axis_size("pz")
    position = lax.axis_index("px")
    place = jnp.stack([position & 1, position >> 1]).astype(jnp.int32)
    total_y = yn * peers
    xl = xn // peers
    f = comps * xl
    lanes = 2 * yn
    members, slots = row_index.shape[3:]

    sent = call(
        columns_kernel,
        shaped((peers, 2 * (f + xl) + HALO_ROWS, lanes), BF16),
        (
            velocity.transpose(0, 2, 1, 3),
            viscosity,
            row_index.reshape(members, slots).T,
            row_counts.reshape(1, members),
        ),
        scratch=[
            pltpu.VMEM((yn, comps, zn, xn), F32),
            pltpu.VMEM((yn, zn, xn), F32),
            pltpu.VMEM((slots, members), jnp.int32),
            pltpu.VMEM((1, members), jnp.int32),
            pltpu.VMEM((peers * HALO_ROWS, lanes), F32),
            pltpu.SemaphoreType.DMA((4,)),
        ],
        far_in=range(4),
    )
    inverse = implicit_inverse.astype(BF16)
    got = exchange(sent, "pz")
    solve_flops = 2 * zn * f * total_y * total_y
    edge = shaped((f, total_y), BF16)
    x_edge = shaped((zn * comps, total_y), F32)
    ids_all = shaped((peers, 8, lanes), jnp.int32)
    v, w, xlo, xhi, zlo, zhi, ids = call(
        spread_kernel,
        (shaped((zn * f, total_y), BF16), shaped((zn * xl, total_y), BF16))
        + (x_edge, x_edge, edge, edge, ids_all),
        (got,),
    )
    zlo, zhi = shift((zhi, zlo), ("px", "tr"))
    message = shaped((members, f, peers * slots), BF16)
    both = shaped((members, 2 * f, peers * slots), BF16)
    sample_flops = 2 * peers * f * 256 * members * slots
    sampling = [
        pltpu.VMEM((peers, 2 * f, lanes), BF16),
        pltpu.VMEM((peers, f, members * slots), F32),
        pltpu.VMEM(message.shape, BF16),
    ]
    blocks = shaped((peers // 2, 2, 2 * f, lanes), BF16)
    half_blocks = shaped((peers // 2, 2 * f, lanes), BF16)
    sampling[0] = pltpu.VMEM(blocks.shape, BF16)
    u, packed, z_first, z_last, x_first, x_last = call(
        first_kernel,
        (shaped((zn * f, total_y), F32), blocks, edge, edge, x_edge, x_edge),
        (v, w, xlo, xhi, zlo, zhi, inverse),
        scratch=[pltpu.VMEM((zn * f, total_y), BF16)],
        flops=solve_flops,
    )
    zlo, zhi = shift((z_last, z_first), ("px", "tr"))
    xlo, xhi = shift((x_last, x_first), "pz")
    sent = call(
        sample_kernel,
        both,
        (packed, ids),
        scratch=sampling[1:] + [pltpu.SemaphoreType.DMA((6,))],
        flops=sample_flops,
        far_out=(0,),
    )
    packed, sent = call(
        second_kernel,
        (blocks, both),
        (u, w, ids, zlo, zhi, xlo, xhi, inverse, sent),
        scratch=[pltpu.VMEM((zn * f, total_y), BF16), pltpu.VMEM((zn * f, total_y), F32)]
        + sampling
        + [pltpu.SemaphoreType.DMA((7,))],
        flops=solve_flops + sample_flops,
        far_in=(8,),
        far_out=(0, 1),
        aliases={8: 1},
    )
    rows_all = exchange(sent, ("pz", "tr"))

    member_in = weight_in[0]
    member_out = weight_out[0]
    width, hid = member_in.shape
    batch = 2 * peers * slots
    spots = lax.axis_size("px")
    loss_scale = 1.0 / math.sqrt(spots * batch)
    matmul_flops = 2 * hid * width * batch

    def forward(*refs):
        forward_kernel(loss_scale, *refs)

    x, hidden, slope, d, away_out = call(
        forward,
        (
            shaped((width, batch), BF16),
            shaped((hid, batch), BF16),
            shaped((hid, batch), BF16),
            shaped((width, batch), BF16),
            shaped((hid // 2, width), BF16),
        ),
        (place, rows_all, member_in, member_out),
        scratch=[
            pltpu.VMEM((width, hid), BF16),
            pltpu.VMEM((hid, width), BF16),
            pltpu.SemaphoreType.DMA((3,)),
        ],
        flops=matmul_flops * 5 // 2,
        far_in=(2, 3),
    )
    got_out = swap_cores(away_out)
    din, away_in = call(
        delta_in_kernel,
        (shaped((hid, batch), BF16), shaped((width // 2, hid), BF16)),
        (place, d, slope, member_out, x),
        flops=matmul_flops * 3 // 2,
    )
    got_in = swap_cores(away_in)

    rows_out, rows_in = hid // spots, width // spots
    block = shaped((rows_out, width), BF16)
    own_out, plus, minus, far = call(
        keep_out_kernel,
        (shaped((rows_out, width), F32), block, block, block),
        (place, hidden, d, got_out),
        flops=matmul_flops // 2,
    )
    block = shaped((2, rows_out, width), BF16)
    part = shaped((2, rows_out // 2, width), BF16)
    own_in, up, down, plus, minus = call(
        keep_in_kernel,
        (shaped((rows_in, hid), F32), block, block, part, part),
        (place, x, din, got_in, plus, minus, far),
        flops=matmul_flops // 2,
    )
    packed, up = lax.optimization_barrier((packed, up))
    arrived = shift_chips(up, down)
    planes = exchange(packed.reshape(peers, 2 * f, lanes), "pz")
    up, down = call(relay_kernel, (part, part), (plus, minus, *arrived), flops=6e9)
    last = shift_chips(up, down)
    share_out, share_in = call(
        finish_kernel,
        (shaped((rows_out, width), F32), shaped((rows_in, hid), F32)),
        (own_out, own_in, *arrived, *last),
        flops=1e6,
    )
    result = call(planes_kernel, shaped((yn, comps, zn, xn), F32), (planes,))
    return (result.transpose(0, 2, 1, 3), share_in[None], share_out[None])


def solution(mesh):
    in_specs = (
        P("pz", ("px", "tr"), None, None),
        P("pz", ("px", "tr"), None),
        P(),
        P("px", "pz", "tr", None, None),
        P("px", "pz", "tr", None),
        P(("pz", "tr"), None, None),
        P(("pz", "tr"), None, None),
    )
    out_specs = (
        P("pz", ("px", "tr"), None, None),
        P(("pz", "tr"), "px", None),
        P(("pz", "tr"), "px", None),
    )
    return jax.shard_map(
        per_device, mesh=mesh, in_specs=in_specs, out_specs=out_specs, check_vma=False
    )
```

```python
import math

import jax
import jax.numpy as jnp
from jax import lax
from jax.experimental import pallas as pl
from jax.experimental.pallas import tpu as pltpu
from jax.sharding import PartitionSpec as P

diffusion_factor = 0.08
F32 = jnp.float32
BF16 = jnp.bfloat16
MIB = 1 << 20


def call(kernel, out_shape, args, scratch=(), flops=1e6, far_in=(), far_out=(), aliases=None):
    outs = jax.tree.leaves(out_shape)
    size = lambda x: math.prod(x.shape) * jnp.dtype(x.dtype).itemsize
    near = [x for k, x in enumerate(args) if k not in far_in]
    near += [x for k, x in enumerate(outs) if k not in far_out]
    held = sum(size(x) for x in near) + sum(size(x) for x in scratch if x.dtype in (F32, BF16, jnp.int32))

    def spec(k, far, scalar=False):
        space = pltpu.HBM if k in far else pltpu.SMEM if scalar else pltpu.VMEM
        return pl.BlockSpec(memory_space=space)

    out_specs = tuple(spec(k, far_out) for k in range(len(outs)))
    args = [
        pltpu.with_memory_space_constraint(x, pltpu.HBM) if k in far_in else x
        for k, x in enumerate(args)
    ]
    pinned = tuple(
        pltpu.HBM(x.shape, x.dtype) if k in far_out else x for k, x in enumerate(outs)
    )
    return pl.pallas_call(
        kernel,
        out_shape=pinned if isinstance(out_shape, tuple) else pinned[0],
        in_specs=[spec(k, far_in, x.ndim == 1) for k, x in enumerate(args)],
        out_specs=out_specs if isinstance(out_shape, tuple) else out_specs[0],
        scratch_shapes=list(scratch),
        input_output_aliases=aliases or {},
        compiler_params=pltpu.CompilerParams(vmem_limit_bytes=held + 6 * MIB),
        cost_estimate=pl.CostEstimate(
            flops=int(flops),
            bytes_accessed=int(sum(size(x) for x in list(args) + outs)),
            transcendentals=0,
        ),
    )(*args)


class Copies:
    def __init__(self, sems):
        self.sems, self.used, self.open = sems, 0, []

    def start(self, source, target):
        copy = pltpu.make_async_copy(source, target, self.sems.at[self.used])
        copy.start()
        self.used += 1
        self.open.append(copy)
        return copy

    def finish(self):
        for copy in self.open:
            copy.wait()
        self.open = []

    def wait(self, copy):
        copy.wait()
        self.open.remove(copy)


def shaped(shape, dtype):
    return jax.ShapeDtypeStruct(shape, dtype)


def shift(array, axis, wrap=True):
    last, first = array
    size = lax.axis_size(axis)
    up = [(i, (i + 1) % size) for i in range(size if wrap else size - 1)]
    down = [(j, i) for i, j in up]
    return lax.ppermute(last, axis, up), lax.ppermute(first, axis, down)


HALO_ROWS = 40
GROUP = 8


def columns_kernel(v_far, w_far, index_far, counts_far, out, v, w, index, counts, edge, sems):
    copies = Copies(sems)
    for far, near in ((index_far, index), (counts_far, counts), (w_far, w), (v_far, v)):
        copies.start(far, near)
    copies.finish()
    yn, comps, zn, xn = v.shape
    peers = out.shape[0]
    xl = xn // peers
    lanes_of = out.shape[2]
    half = (comps + 1) * xl
    for zh in range(zn // 2):
        for c in range(comps + 1):
            pair = [w[:, z, :] if c == comps else v[:, c, z, :] for z in (2 * zh, 2 * zh + 1)]
            turned = jnp.concatenate(pair, axis=0).T
            base = zh * half + c * xl
            for q in range(peers):
                out[q, base : base + xl, :] = turned[q * xl : (q + 1) * xl].astype(BF16)
            group = zn // 2 * comps
            for q in range(peers):
                columns = [(q * xl + k) % xn for k in (-2, -1, xl, xl + 1)]
                r, step = q * HALO_ROWS + zh * comps + c, group
                if c == comps:
                    r, step = q * HALO_ROWS + 4 * group + zh, zn // 2
                    columns = columns[1:3]
                for k, x in enumerate(columns):
                    edge[r + k * step : r + k * step + 1] = turned[x : x + 1]
    start = zn // 2 * half
    slots, members = index.shape
    slot = lax.broadcasted_iota(jnp.int32, (slots, members), 0)
    live = jnp.where(slot < counts[...], index[...], -1).astype(F32)
    sides = lanes_of // members
    rows = slots // sides
    numbers = jnp.concatenate([live[k * rows : (k + 1) * rows] for k in range(sides)], axis=1)
    numbers = jnp.concatenate([numbers, jnp.zeros((8 - rows, lanes_of), F32)], axis=0)
    for q in range(peers):
        edge[(q + 1) * HALO_ROWS - 12 : (q + 1) * HALO_ROWS - 8] = jnp.zeros((4, lanes_of), F32)
        edge[(q + 1) * HALO_ROWS - 8 : (q + 1) * HALO_ROWS] = numbers
        out[q, start : start + HALO_ROWS, :] = edge[
            q * HALO_ROWS : (q + 1) * HALO_ROWS
        ].astype(BF16)


def solve(e, a):
    return lax.dot_general(
        e[...], a[...], (((1,), (1,)), ((), ())), preferred_element_type=F32
    )


def pack_columns(u, packed, zn):
    pairs, _, rows, lanes = packed.shape
    f = rows // (zn // 2)
    yn = lanes // 2
    low = lax.broadcasted_iota(jnp.int32, (f, lanes), 1) < yn
    for j in range(pairs):
        for zh in range(zn // 2):
            first = u[(2 * zh) * f : (2 * zh + 1) * f, j * lanes : (j + 1) * lanes]
            second = u[(2 * zh + 1) * f : (2 * zh + 2) * f, j * lanes : (j + 1) * lanes]
            even = jnp.where(low, first, pltpu.roll(second, yn, 1))
            odd = jnp.where(low, pltpu.roll(first, yn, 1), second)
            packed[j, 0, zh * f : (zh + 1) * f, :] = even.astype(BF16)
            packed[j, 1, zh * f : (zh + 1) * f, :] = odd.astype(BF16)


def spread_kernel(got, v, w, x_halo, w_halo, zlo, zhi, ids):
    peers, rows, lanes = got.shape
    table = got[:, rows - 8 :, :].astype(F32).reshape(peers * 8, lanes).astype(BF16)
    members = 32
    per = lanes // GROUP
    source = lax.broadcasted_iota(jnp.int32, (lanes, lanes), 0)
    lane = lax.broadcasted_iota(jnp.int32, (lanes, lanes), 1)
    late = lax.broadcasted_iota(jnp.int32, (1, lanes), 1) % GROUP >= GROUP // 2
    halves = members // per
    for mh in range(halves):
        wanted = (lane % (GROUP // 2)) * members + mh * per + lane // GROUP
        moved = jnp.dot(
            table, jnp.where(source == wanted, 1.0, 0.0).astype(BF16), preferred_element_type=F32
        )
        for q in range(peers):
            for kg in range(3):
                r = q * 8 + 2 * kg
                line = jnp.where(late, moved[r + 1 : r + 2], moved[r : r + 1])
                at = kg * halves + mh
                ids[q, at : at + 1, :] = line.astype(jnp.int32)
    yn = lanes // 2
    zn = 4
    half = (rows - HALO_ROWS) // 2
    xl = w.shape[0] // zn
    f = half - xl
    comps = f // xl
    low = lax.broadcasted_iota(jnp.int32, (rows, lanes), 1) < yn
    for j in range(peers // 2):
        one = got[2 * j].astype(F32)
        two = got[2 * j + 1].astype(F32)
        sides = (
            jnp.where(low, one, pltpu.roll(two, yn, 1)),
            jnp.where(low, pltpu.roll(one, yn, 1), two),
        )
        at = slice(j * lanes, (j + 1) * lanes)
        for zh in range(zn // 2):
            for side in range(2):
                z = 2 * zh + side
                whole = sides[side]
                v[z * f : (z + 1) * f, at] = whole[zh * half : zh * half + f].astype(BF16)
                w[z * xl : (z + 1) * xl, at] = whole[zh * half + f : (zh + 1) * half].astype(BF16)
                group = zn // 2 * comps
                for k in range(4):
                    r = zn // 2 * half + k * group + zh * comps
                    to = k * zn * comps + z * comps
                    x_halo[to : to + comps, at] = whole[r : r + comps]
                for k in range(2):
                    r = zn // 2 * half + 4 * group + k * (zn // 2) + zh
                    w_halo[k * zn + z : k * zn + z + 1, at] = whole[r : r + 1]
    for edge, z in ((zlo, 0), (zhi, zn - 1)):
        sides = [x_halo[(k * zn + z) * comps : (k * zn + z + 1) * comps] for k in (1, 2)]
        fill = jnp.zeros((8 - 2 * comps, v.shape[1]), F32)
        plane = v[z * f : (z + 1) * f].astype(F32)
        edge[...] = jnp.concatenate([plane, *sides, fill], axis=0).astype(BF16)


def explicit_plane(z, u, w, zlo, zhi, x_before, x_after, e):
    f, cols = zlo.shape
    zn = u.shape[0] // f
    xl = w.shape[0] // zn
    comps = f // xl
    row = lax.broadcasted_iota(jnp.int32, (xl, cols), 0)
    lane = lax.broadcasted_iota(jnp.int32, (xl, cols), 1)
    factor = diffusion_factor * w[z * xl : (z + 1) * xl].astype(F32)
    for c in range(comps):
        r = z * comps + c
        at = slice(r * xl, (r + 1) * xl)
        cur = u[at].astype(F32)
        if z > 0:
            total = u[(r - comps) * xl : (r - comps + 1) * xl].astype(F32)
        else:
            total = zlo[c * xl : (c + 1) * xl].astype(F32)
        if z < zn - 1:
            total = total + u[(r + comps) * xl : (r + comps + 1) * xl].astype(F32)
        else:
            total = total + zhi[c * xl : (c + 1) * xl].astype(F32)
        total = total + jnp.where(row == 0, x_before[r : r + 1], pltpu.roll(cur, 1, 0))
        total = total + jnp.where(row == xl - 1, x_after[r : r + 1], pltpu.roll(cur, xl - 1, 0))
        total = total + jnp.where(lane == 0, 0.0, pltpu.roll(cur, 1, 1))
        total = total + jnp.where(lane == cols - 1, 0.0, pltpu.roll(cur, cols - 1, 1))
        e[at] = (cur + factor * (total - 6.0 * cur)).astype(BF16)


def explicit_sides(v, x_halo, w_halo, zlo, zhi):
    zn = 4
    rows = x_halo.shape[0] // 4
    comps = rows // zn
    xl = v.shape[0] // rows
    cols = v.shape[1]
    lane = lax.broadcasted_iota(jnp.int32, (rows, cols), 1)
    blocks = [v[r * xl : (r + 1) * xl].astype(F32) for r in range(rows)]
    inner = [
        jnp.concatenate([block[k : k + 1] for block in blocks], axis=0) for k in (0, xl - 1)
    ]
    z_before, z_after = zlo[rows * xl // zn :].astype(F32), zhi[rows * xl // zn :].astype(F32)
    values = []
    for k in range(2):
        cur = x_halo[(k + 1) * rows : (k + 2) * rows]
        total = inner[k] + x_halo[3 * k * rows : (3 * k + 1) * rows]
        part = slice(k * comps, (k + 1) * comps)
        total = total + jnp.concatenate([z_before[part], cur[: rows - comps]], axis=0)
        total = total + jnp.concatenate([cur[comps:], z_after[part]], axis=0)
        total = total + jnp.where(lane == 0, 0.0, pltpu.roll(cur, 1, 1))
        total = total + jnp.where(lane == cols - 1, 0.0, pltpu.roll(cur, cols - 1, 1))
        factor = jnp.concatenate(
            [jnp.broadcast_to(w_halo[r : r + 1], (comps, cols)) for r in range(k * zn, (k + 1) * zn)],
            axis=0,
        )
        values.append(cur + diffusion_factor * factor * (total - 6.0 * cur))
    return values


def first_kernel(
    v, w, x_halo, w_halo, zlo, zhi, a, u, packed, z_first, z_last, x_before_out, x_after_out, e
):
    zn = 4
    rows = x_halo.shape[0] // 4
    count = v.shape[0]
    f = count // zn
    x_before, x_after = x_halo[rows : 2 * rows], x_halo[2 * rows : 3 * rows]
    for z in range(zn):
        explicit_plane(z, v, w, zlo.at[pl.ds(0, f)], zhi.at[pl.ds(0, f)], x_before, x_after, e)
    fill = jnp.zeros((e.shape[0] - count - 2 * rows, v.shape[1]), F32)
    e[count:] = jnp.concatenate(
        [*explicit_sides(v, x_halo, w_halo, zlo, zhi), fill], axis=0
    ).astype(BF16)
    solved = solve(e, a)
    u[...] = solved[:count]
    x_before_out[...] = solved[count : count + rows]
    x_after_out[...] = solved[count + rows : count + 2 * rows]
    z_first[...] = u[0:f].astype(BF16)
    z_last[...] = u[(zn - 1) * f : zn * f].astype(BF16)
    pack_columns(u, packed, zn)


def sample_kernel(packed, ids, sent_far, picked, sent, sems):
    copies = Copies(sems)
    sample(packed, ids, picked, sent, message_part(copies, sent, sent_far, 0))
    copies.finish()


def message_part(copies, sent, far, which):
    f = sent.shape[1]

    def ready(part):
        members, _, lanes = part
        copies.start(sent.at[part], far.at[members, pl.ds(which * f, f), lanes])

    return ready


def second_kernel(
    u, w, ids, zlo, zhi, xlo, xhi, a, sent_in, packed_far, sent_far,
    e, after, packed, picked, sent, sems,
):
    del sent_in
    copies = Copies(sems)
    zn = u.shape[0] // zlo.shape[0]
    x_before, x_after = xlo[...], xhi[...]
    for z in range(zn):
        explicit_plane(z, u, w, zlo, zhi, x_before, x_after, e)
    after[...] = solve(e, a)
    pack_columns(after, packed, zn)
    copies.start(packed, packed_far)
    sample(packed, ids, picked, sent, message_part(copies, sent, sent_far, 1))
    copies.finish()


def sample(packed, ids, picked, out, ready):
    pairs, _, rows, lanes = packed.shape
    peers = 2 * pairs
    f = rows // 2
    yn = lanes // 2
    blocks = picked.shape[2] // lanes
    r = lax.broadcasted_iota(jnp.int32, (2 * lanes, lanes), 0)
    row_id = (r % yn) * 4 + r // yn
    for q in range(peers):
        at = (q // 2, q % 2)
        table = jnp.concatenate([packed[(*at, slice(0, f))], packed[(*at, slice(f, rows))]], axis=1)
        wanted = pltpu.roll(ids[q], (GROUP * q) % lanes, 1) if q else ids[q]
        for b in range(blocks):
            hot = jnp.where(row_id == wanted[b : b + 1], 1.0, 0.0).astype(BF16)
            picked[q, :, b * lanes : (b + 1) * lanes] = jnp.dot(
                table, hot, preferred_element_type=F32
            )
    group = lax.broadcasted_iota(jnp.int32, (f, lanes), 1) // GROUP
    per = lanes // GROUP
    halves = out.shape[0] // per
    for b in range(blocks):
        kg, mh = b // halves, b % halves
        held = [picked[q, :, b * lanes : (b + 1) * lanes] for q in range(peers)]
        step = 1
        while step < peers:
            take = (group // step) % 2 == 1
            held = [jnp.where(take, held[(i + step) % peers], held[i]) for i in range(peers)]
            step *= 2
        for ml in range(per):
            out[mh * per + ml, :, kg * lanes : (kg + 1) * lanes] = held[(-ml) % peers].astype(BF16)
        ready((pl.ds(mh * per, per), slice(None), pl.ds(kg * lanes, lanes)))


def gather_rows(got, start, turned, comps=3):
    sources, both, slots = got.shape
    sides = 2
    peers = sources // sides
    xl = both // 2 // comps
    for q in range(peers):
        for side in range(sides):
            for c in range(comps):
                at = (c * peers + q) * xl
                turned[at : at + xl, side * slots : (side + 1) * slots] = got[
                    q * sides + side, start + c * xl : start + (c + 1) * xl
                ]


CONTRACT_ROWS = (((1,), (1,)), ((), ()))


def over_rows(left, right):
    return lax.dot_general(left, right, CONTRACT_ROWS, preferred_element_type=F32)


def over_first(left, right):
    return lax.dot_general(left, right, (((0,), (0,)), ((), ())), preferred_element_type=F32)


def forward_kernel(
    scale, place, got, w_in_far, w_out_far, x, hidden, slope, d, away, w_in, w_out, sems
):
    copies = Copies(sems)
    f = got.shape[1] // 2
    wide = 512
    count = hidden.shape[0] // wide
    parts = [(slice(None), pl.ds(i * wide, wide)) for i in range(count)]
    arriving = copies.start(w_in_far.at[parts[0]], w_in.at[parts[0]])
    gather_rows(got, 0, x)
    for i in range(count):
        at = slice(i * wide, (i + 1) * wide)
        copies.wait(arriving)
        if i + 1 < count:
            arriving = copies.start(w_in_far.at[parts[i + 1]], w_in.at[parts[i + 1]])
        else:
            copies.start(w_out_far, w_out)
        pre = over_first(w_in[:, at], x[...])
        logistic = jax.nn.sigmoid(pre)
        hidden[at, :] = (pre * logistic).astype(BF16)
        slope[at, :] = (logistic * (1.0 + pre * (1.0 - logistic))).astype(slope.dtype)
    gather_rows(got, f, d)
    copies.finish()
    predicted = over_first(w_out[...], hidden[...])
    d[...] = ((predicted - d[...].astype(F32)) * scale).astype(BF16)
    away_blocks(hidden, d, place[0], away, away.shape[0] // 4)


def block_rows(array, y, core, rows):
    return array[pl.ds(pl.multiple_of((2 * y + core) * rows, rows), rows), :]


def away_blocks(array, right, core, away, rows):
    left = jnp.concatenate([block_rows(array, y, 1 - core, rows) for y in range(4)], axis=0)
    away[...] = over_rows(left, right[...]).astype(BF16)


def delta_in_kernel(place, d, slope, w_out, x, din, away):
    wide = 512
    for i in range(din.shape[0] // wide):
        at = slice(i * wide, (i + 1) * wide)
        back = jnp.dot(w_out[at, :], d[...], preferred_element_type=F32)
        din[at, :] = (back * slope[at, :].astype(F32)).astype(BF16)
    away_blocks(x, din, place[0], away, away.shape[0] // 4)


def fold(block, rows, width):
    extra = rows - block.shape[0]
    pieces = [block[g * extra : (g + 1) * extra, width:] for g in range(block.shape[0] // extra)]
    return jnp.concatenate([block[:, :width], jnp.concatenate(pieces, axis=1)], axis=0)


def unfold(block, rows):
    extra = block.shape[0] - rows
    count = rows // extra
    wide = block.shape[1] // count
    pieces = [block[rows:, g * wide : (g + 1) * wide] for g in range(count)]
    return jnp.concatenate([block[:rows], jnp.concatenate(pieces, axis=0)], axis=1)


def own_blocks(place, array, rows):
    core, y = place[0], place[1]
    return jnp.concatenate(
        [block_rows(array, lax.rem(y + k, 4), core, rows) for k in (2, 1, 3, 0)], axis=0
    )


def add_other_core(place, value, got, n, k):
    rows = value.shape[0] // 4
    at = pl.multiple_of(lax.rem(place[1] + k, 4) * rows, rows)
    return value[n * rows : (n + 1) * rows] + got[pl.ds(at, rows), :].astype(F32)


def keep_out_kernel(place, hidden, d, got, own, plus, minus, far):
    value = over_rows(own_blocks(place, hidden, own.shape[0]), d[...])
    far[...] = add_other_core(place, value, got, 0, 2).astype(BF16)
    plus[...] = add_other_core(place, value, got, 1, 1).astype(BF16)
    minus[...] = add_other_core(place, value, got, 2, 3).astype(BF16)
    own[...] = add_other_core(place, value, got, 3, 0)


def keep_in_kernel(
    place, x, din, got, plus_out, minus_out, far_out, own, up, down, plus, minus
):
    rows, width = plus_out.shape
    half = rows // 2

    def put(which, far_block, plus_block, minus_block):
        up[which, :half] = far_block[:half]
        up[which, half:] = plus_block[half:]
        down[which, :half] = minus_block[:half]
        down[which, half:] = far_block[half:]
        plus[which] = plus_block[:half]
        minus[which] = minus_block[half:]

    put(0, far_out[...], plus_out[...], minus_out[...])
    value = over_rows(own_blocks(place, x, own.shape[0]), din[...])
    put(
        1,
        *(
            fold(add_other_core(place, value, got, n, k), rows, width).astype(BF16)
            for n, k in ((0, 2), (1, 1), (2, 3))
        ),
    )
    own[...] = add_other_core(place, value, got, 3, 0)


def relay_kernel(plus, minus, from_before, from_after, up, down):
    half = plus.shape[1]
    for which in range(plus.shape[0]):
        before = from_before[which, :half].astype(F32)
        after = from_after[which, half:].astype(F32)
        up[which] = (plus[which].astype(F32) + before).astype(BF16)
        down[which] = (minus[which].astype(F32) + after).astype(BF16)


def finish_kernel(
    own_out, own_in, first_before, first_after, last_before, last_after, share_out, share_in
):
    half = last_before.shape[1]
    total = []
    for k in range(2):
        upper = first_after[k, :half].astype(F32) + last_before[k].astype(F32)
        lower = first_before[k, half:].astype(F32) + last_after[k].astype(F32)
        total.append(jnp.concatenate([upper, lower], axis=0))
    share_out[...] = own_out[...] + total[0]
    share_in[...] = own_in[...] + unfold(total[1], share_in.shape[0])


def planes_kernel(got, out):
    yn, comps, zn, xn = out.shape
    peers = got.shape[0]
    xl = xn // peers
    f = comps * xl
    for zh in range(zn // 2):
        for c in range(comps):
            base = zh * f + c * xl
            block = jnp.concatenate(
                [got[q, base : base + xl, :] for q in range(peers)], axis=0
            ).astype(F32)
            turned = block.T
            out[:, c, 2 * zh, :] = turned[0:yn]
            out[:, c, 2 * zh + 1, :] = turned[yn : 2 * yn]


def exchange(array, axis):
    return lax.all_to_all(array, axis, split_axis=0, concat_axis=0, tiled=True)


def swap_cores(array):
    size = lax.axis_size("px")
    return lax.ppermute(array, "px", [(i, i ^ 1) for i in range(size)])


def shift_chips(forward, backward):
    size = lax.axis_size("px")
    up = [(i, (i + 2) % size) for i in range(size)]
    down = [(j, i) for i, j in up]
    return lax.ppermute(forward, "px", up), lax.ppermute(backward, "px", down)


def per_device(velocity, viscosity, implicit_inverse, row_index, row_counts, weight_in, weight_out):
    yn, zn, comps, xn = velocity.shape
    peers = lax.axis_size("pz")
    position = lax.axis_index("px")
    place = jnp.stack([position & 1, position >> 1]).astype(jnp.int32)
    total_y = yn * peers
    xl = xn // peers
    f = comps * xl
    lanes = 2 * yn
    members, slots = row_index.shape[3:]

    sent = call(
        columns_kernel,
        shaped((peers, 2 * (f + xl) + HALO_ROWS, lanes), BF16),
        (
            velocity.transpose(0, 2, 1, 3),
            viscosity,
            row_index.reshape(members, slots).T,
            row_counts.reshape(1, members),
        ),
        scratch=[
            pltpu.VMEM((yn, comps, zn, xn), F32),
            pltpu.VMEM((yn, zn, xn), F32),
            pltpu.VMEM((slots, members), jnp.int32),
            pltpu.VMEM((1, members), jnp.int32),
            pltpu.VMEM((peers * HALO_ROWS, lanes), F32),
            pltpu.SemaphoreType.DMA((4,)),
        ],
        far_in=range(4),
    )
    inverse = implicit_inverse.astype(BF16)
    got = exchange(sent, "pz")
    solve_flops = 2 * zn * f * total_y * total_y
    edge = shaped((f, total_y), BF16)
    x_edge = shaped((zn * comps, total_y), F32)
    ids_all = shaped((peers, 8, lanes), jnp.int32)
    wide_edge = shaped((f + 8, total_y), BF16)
    v, w, x_halo, w_halo, zlo, zhi, ids = call(
        spread_kernel,
        (shaped((zn * f, total_y), BF16), shaped((zn * xl, total_y), BF16))
        + (shaped((4 * zn * comps, total_y), F32), shaped((2 * zn, total_y), F32))
        + (wide_edge, wide_edge, ids_all),
        (got,),
    )
    zlo, zhi = shift((zhi, zlo), ("px", "tr"))
    message = shaped((members, f, peers * slots), BF16)
    both = shaped((members, 2 * f, peers * slots), BF16)
    sample_flops = 2 * peers * f * 256 * members * slots
    sampling = [
        pltpu.VMEM((peers, 2 * f, lanes), BF16),
        pltpu.VMEM((peers, f, members * slots), F32),
        pltpu.VMEM(message.shape, BF16),
    ]
    blocks = shaped((peers // 2, 2, 2 * f, lanes), BF16)
    half_blocks = shaped((peers // 2, 2 * f, lanes), BF16)
    sampling[0] = pltpu.VMEM(blocks.shape, BF16)
    u, packed, z_first, z_last, xlo, xhi = call(
        first_kernel,
        (shaped((zn * f, total_y), F32), blocks, edge, edge, x_edge, x_edge),
        (v, w, x_halo, w_halo, zlo, zhi, inverse),
        scratch=[pltpu.VMEM((zn * f + 32, total_y), BF16)],
        flops=solve_flops,
    )
    zlo, zhi = shift((z_last, z_first), ("px", "tr"))
    sent = call(
        sample_kernel,
        both,
        (packed, ids),
        scratch=sampling[1:] + [pltpu.SemaphoreType.DMA((6,))],
        flops=sample_flops,
        far_out=(0,),
    )
    packed, sent = call(
        second_kernel,
        (blocks, both),
        (u, w, ids, zlo, zhi, xlo, xhi, inverse, sent),
        scratch=[pltpu.VMEM((zn * f, total_y), BF16), pltpu.VMEM((zn * f, total_y), F32)]
        + sampling
        + [pltpu.SemaphoreType.DMA((7,))],
        flops=solve_flops + sample_flops,
        far_in=(8,),
        far_out=(0, 1),
        aliases={8: 1},
    )
    rows_all = exchange(sent, ("pz", "tr"))

    member_in = weight_in[0]
    member_out = weight_out[0]
    width, hid = member_in.shape
    batch = 2 * peers * slots
    spots = lax.axis_size("px")
    loss_scale = 1.0 / math.sqrt(spots * batch)
    matmul_flops = 2 * hid * width * batch

    def forward(*refs):
        forward_kernel(loss_scale, *refs)

    x, hidden, slope, d, away_out = call(
        forward,
        (
            shaped((width, batch), BF16),
            shaped((hid, batch), BF16),
            shaped((hid, batch), BF16),
            shaped((width, batch), BF16),
            shaped((hid // 2, width), BF16),
        ),
        (place, rows_all, member_in, member_out),
        scratch=[
            pltpu.VMEM((width, hid), BF16),
            pltpu.VMEM((hid, width), BF16),
            pltpu.SemaphoreType.DMA((3,)),
        ],
        flops=matmul_flops * 5 // 2,
        far_in=(2, 3),
    )
    got_out = swap_cores(away_out)
    din, away_in = call(
        delta_in_kernel,
        (shaped((hid, batch), BF16), shaped((width // 2, hid), BF16)),
        (place, d, slope, member_out, x),
        flops=matmul_flops * 3 // 2,
    )
    got_in = swap_cores(away_in)

    rows_out, rows_in = hid // spots, width // spots
    block = shaped((rows_out, width), BF16)
    own_out, plus, minus, far = call(
        keep_out_kernel,
        (shaped((rows_out, width), F32), block, block, block),
        (place, hidden, d, got_out),
        flops=matmul_flops // 2,
    )
    block = shaped((2, rows_out, width), BF16)
    part = shaped((2, rows_out // 2, width), BF16)
    own_in, up, down, plus, minus = call(
        keep_in_kernel,
        (shaped((rows_in, hid), F32), block, block, part, part),
        (place, x, din, got_in, plus, minus, far),
        flops=matmul_flops // 2,
    )
    packed, up = lax.optimization_barrier((packed, up))
    arrived = shift_chips(up, down)
    planes = exchange(packed.reshape(peers, 2 * f, lanes), "pz")
    up, down = call(relay_kernel, (part, part), (plus, minus, *arrived), flops=6e9)
    last = shift_chips(up, down)
    share_out, share_in = call(
        finish_kernel,
        (shaped((rows_out, width), F32), shaped((rows_in, hid), F32)),
        (own_out, own_in, *arrived, *last),
        flops=1e6,
    )
    result = call(planes_kernel, shaped((yn, comps, zn, xn), F32), (planes,))
    return (result.transpose(0, 2, 1, 3), share_in[None], share_out[None])


def solution(mesh):
    in_specs = (
        P("pz", ("px", "tr"), None, None),
        P("pz", ("px", "tr"), None),
        P(),
        P("px", "pz", "tr", None, None),
        P("px", "pz", "tr", None),
        P(("pz", "tr"), None, None),
        P(("pz", "tr"), None, None),
    )
    out_specs = (
        P("pz", ("px", "tr"), None, None),
        P(("pz", "tr"), "px", None),
        P(("pz", "tr"), "px", None),
    )
    return jax.shard_map(
        per_device, mesh=mesh, in_specs=in_specs, out_specs=out_specs, check_vma=False
    )
```

```python
import math

import jax
import jax.numpy as jnp
from jax import lax
from jax.experimental import pallas as pl
from jax.experimental.pallas import tpu as pltpu
from jax.sharding import PartitionSpec as P

diffusion_factor = 0.08
F32 = jnp.float32
BF16 = jnp.bfloat16
MIB = 1 << 20


def call(kernel, out_shape, args, scratch=(), flops=1e6, far_in=(), far_out=(), aliases=None):
    outs = jax.tree.leaves(out_shape)
    size = lambda x: math.prod(x.shape) * jnp.dtype(x.dtype).itemsize
    near = [x for k, x in enumerate(args) if k not in far_in]
    near += [x for k, x in enumerate(outs) if k not in far_out]
    held = sum(size(x) for x in near) + sum(size(x) for x in scratch if x.dtype in (F32, BF16, jnp.int32))

    def spec(k, far, scalar=False):
        space = pltpu.HBM if k in far else pltpu.SMEM if scalar else pltpu.VMEM
        return pl.BlockSpec(memory_space=space)

    out_specs = tuple(spec(k, far_out) for k in range(len(outs)))
    args = [
        pltpu.with_memory_space_constraint(x, pltpu.HBM) if k in far_in else x
        for k, x in enumerate(args)
    ]
    pinned = tuple(
        pltpu.HBM(x.shape, x.dtype) if k in far_out else x for k, x in enumerate(outs)
    )
    return pl.pallas_call(
        kernel,
        out_shape=pinned if isinstance(out_shape, tuple) else pinned[0],
        in_specs=[spec(k, far_in, x.ndim == 1) for k, x in enumerate(args)],
        out_specs=out_specs if isinstance(out_shape, tuple) else out_specs[0],
        scratch_shapes=list(scratch),
        input_output_aliases=aliases or {},
        compiler_params=pltpu.CompilerParams(vmem_limit_bytes=held + 6 * MIB),
        cost_estimate=pl.CostEstimate(
            flops=int(flops),
            bytes_accessed=int(sum(size(x) for x in list(args) + outs)),
            transcendentals=0,
        ),
    )(*args)


class Copies:
    def __init__(self, sems):
        self.sems, self.used, self.open = sems, 0, []

    def start(self, source, target):
        copy = pltpu.make_async_copy(source, target, self.sems.at[self.used])
        copy.start()
        self.used += 1
        self.open.append(copy)
        return copy

    def finish(self):
        for copy in self.open:
            copy.wait()
        self.open = []

    def wait(self, copy):
        copy.wait()
        self.open.remove(copy)


def shaped(shape, dtype):
    return jax.ShapeDtypeStruct(shape, dtype)


def shift(array, axis, wrap=True):
    last, first = array
    size = lax.axis_size(axis)
    up = [(i, (i + 1) % size) for i in range(size if wrap else size - 1)]
    down = [(j, i) for i, j in up]
    return lax.ppermute(last, axis, up), lax.ppermute(first, axis, down)


HALO_ROWS = 40
GROUP = 8


def columns_kernel(v_far, w_far, index_far, counts_far, out, v, w, index, counts, edge, sems):
    copies = Copies(sems)
    for far, near in ((index_far, index), (counts_far, counts), (w_far, w), (v_far, v)):
        copies.start(far, near)
    copies.finish()
    yn, comps, zn, xn = v.shape
    peers = out.shape[0]
    xl = xn // peers
    lanes_of = out.shape[2]
    half = (comps + 1) * xl
    for zh in range(zn // 2):
        for c in range(comps + 1):
            pair = [w[:, z, :] if c == comps else v[:, c, z, :] for z in (2 * zh, 2 * zh + 1)]
            turned = jnp.concatenate(pair, axis=0).T
            base = zh * half + c * xl
            for q in range(peers):
                out[q, base : base + xl, :] = turned[q * xl : (q + 1) * xl].astype(BF16)
            group = zn // 2 * comps
            for q in range(peers):
                columns = [(q * xl + k) % xn for k in (-2, -1, xl, xl + 1)]
                r, step = q * HALO_ROWS + zh * comps + c, group
                if c == comps:
                    r, step = q * HALO_ROWS + 4 * group + zh, zn // 2
                    columns = columns[1:3]
                for k, x in enumerate(columns):
                    edge[r + k * step : r + k * step + 1] = turned[x : x + 1]
    start = zn // 2 * half
    slots, members = index.shape
    slot = lax.broadcasted_iota(jnp.int32, (slots, members), 0)
    live = jnp.where(slot < counts[...], index[...], -1).astype(F32)
    sides = lanes_of // members
    rows = slots // sides
    numbers = jnp.concatenate([live[k * rows : (k + 1) * rows] for k in range(sides)], axis=1)
    numbers = jnp.concatenate([numbers, jnp.zeros((8 - rows, lanes_of), F32)], axis=0)
    for q in range(peers):
        edge[(q + 1) * HALO_ROWS - 12 : (q + 1) * HALO_ROWS - 8] = jnp.zeros((4, lanes_of), F32)
        edge[(q + 1) * HALO_ROWS - 8 : (q + 1) * HALO_ROWS] = numbers
        out[q, start : start + HALO_ROWS, :] = edge[
            q * HALO_ROWS : (q + 1) * HALO_ROWS
        ].astype(BF16)


def solve(e, a):
    return lax.dot_general(
        e[...], a[...], (((1,), (1,)), ((), ())), preferred_element_type=F32
    )


def pack_columns(u, packed, zn):
    pairs, _, rows, lanes = packed.shape
    f = rows // (zn // 2)
    yn = lanes // 2
    low = lax.broadcasted_iota(jnp.int32, (f, lanes), 1) < yn
    for j in range(pairs):
        for zh in range(zn // 2):
            first = u[(2 * zh) * f : (2 * zh + 1) * f, j * lanes : (j + 1) * lanes]
            second = u[(2 * zh + 1) * f : (2 * zh + 2) * f, j * lanes : (j + 1) * lanes]
            even = jnp.where(low, first, pltpu.roll(second, yn, 1))
            odd = jnp.where(low, pltpu.roll(first, yn, 1), second)
            packed[j, 0, zh * f : (zh + 1) * f, :] = even.astype(BF16)
            packed[j, 1, zh * f : (zh + 1) * f, :] = odd.astype(BF16)


def spread_kernel(got, v, w, x_halo, w_halo, zlo, zhi, ids):
    peers, rows, lanes = got.shape
    table = got[:, rows - 8 :, :].astype(F32).reshape(peers * 8, lanes).astype(BF16)
    members = 32
    per = lanes // GROUP
    source = lax.broadcasted_iota(jnp.int32, (lanes, lanes), 0)
    lane = lax.broadcasted_iota(jnp.int32, (lanes, lanes), 1)
    late = lax.broadcasted_iota(jnp.int32, (1, lanes), 1) % GROUP >= GROUP // 2
    halves = members // per
    for mh in range(halves):
        wanted = (lane % (GROUP // 2)) * members + mh * per + lane // GROUP
        moved = jnp.dot(
            table, jnp.where(source == wanted, 1.0, 0.0).astype(BF16), preferred_element_type=F32
        )
        for q in range(peers):
            for kg in range(3):
                r = q * 8 + 2 * kg
                line = jnp.where(late, moved[r + 1 : r + 2], moved[r : r + 1])
                at = kg * halves + mh
                ids[q, at : at + 1, :] = line.astype(jnp.int32)
    yn = lanes // 2
    zn = 4
    half = (rows - HALO_ROWS) // 2
    xl = w.shape[0] // zn
    f = half - xl
    comps = f // xl
    low = lax.broadcasted_iota(jnp.int32, (rows, lanes), 1) < yn
    for j in range(peers // 2):
        one = got[2 * j].astype(F32)
        two = got[2 * j + 1].astype(F32)
        sides = (
            jnp.where(low, one, pltpu.roll(two, yn, 1)),
            jnp.where(low, pltpu.roll(one, yn, 1), two),
        )
        at = slice(j * lanes, (j + 1) * lanes)
        for zh in range(zn // 2):
            for side in range(2):
                z = 2 * zh + side
                whole = sides[side]
                v[z * f : (z + 1) * f, at] = whole[zh * half : zh * half + f].astype(BF16)
                w[z * xl : (z + 1) * xl, at] = whole[zh * half + f : (zh + 1) * half].astype(BF16)
                group = zn // 2 * comps
                for k in range(4):
                    r = zn // 2 * half + k * group + zh * comps
                    to = k * zn * comps + z * comps
                    x_halo[to : to + comps, at] = whole[r : r + comps]
                for k in range(2):
                    r = zn // 2 * half + 4 * group + k * (zn // 2) + zh
                    w_halo[k * zn + z : k * zn + z + 1, at] = whole[r : r + 1]
    for edge, z in ((zlo, 0), (zhi, zn - 1)):
        sides = [x_halo[(k * zn + z) * comps : (k * zn + z + 1) * comps] for k in (1, 2)]
        fill = jnp.zeros((8 - 2 * comps, v.shape[1]), F32)
        plane = v[z * f : (z + 1) * f].astype(F32)
        edge[...] = jnp.concatenate([plane, *sides, fill], axis=0).astype(BF16)


def explicit_plane(z, u, w, zlo, zhi, x_before, x_after, e):
    f, cols = zlo.shape
    zn = u.shape[0] // f
    xl = w.shape[0] // zn
    comps = f // xl
    row = lax.broadcasted_iota(jnp.int32, (xl, cols), 0)
    lane = lax.broadcasted_iota(jnp.int32, (xl, cols), 1)
    factor = diffusion_factor * w[z * xl : (z + 1) * xl].astype(F32)
    for c in range(comps):
        r = z * comps + c
        at = slice(r * xl, (r + 1) * xl)
        cur = u[at].astype(F32)
        if z > 0:
            total = u[(r - comps) * xl : (r - comps + 1) * xl].astype(F32)
        else:
            total = zlo[c * xl : (c + 1) * xl].astype(F32)
        if z < zn - 1:
            total = total + u[(r + comps) * xl : (r + comps + 1) * xl].astype(F32)
        else:
            total = total + zhi[c * xl : (c + 1) * xl].astype(F32)
        total = total + jnp.where(row == 0, x_before[r : r + 1], pltpu.roll(cur, 1, 0))
        total = total + jnp.where(row == xl - 1, x_after[r : r + 1], pltpu.roll(cur, xl - 1, 0))
        total = total + jnp.where(lane == 0, 0.0, pltpu.roll(cur, 1, 1))
        total = total + jnp.where(lane == cols - 1, 0.0, pltpu.roll(cur, cols - 1, 1))
        e[at] = (cur + factor * (total - 6.0 * cur)).astype(BF16)


def explicit_sides(v, x_halo, w_halo, zlo, zhi):
    zn = 4
    rows = x_halo.shape[0] // 4
    comps = rows // zn
    xl = v.shape[0] // rows
    cols = v.shape[1]
    lane = lax.broadcasted_iota(jnp.int32, (rows, cols), 1)
    blocks = [v[r * xl : (r + 1) * xl].astype(F32) for r in range(rows)]
    inner = [
        jnp.concatenate([block[k : k + 1] for block in blocks], axis=0) for k in (0, xl - 1)
    ]
    z_before, z_after = zlo[rows * xl // zn :].astype(F32), zhi[rows * xl // zn :].astype(F32)
    values = []
    for k in range(2):
        cur = x_halo[(k + 1) * rows : (k + 2) * rows]
        total = inner[k] + x_halo[3 * k * rows : (3 * k + 1) * rows]
        part = slice(k * comps, (k + 1) * comps)
        total = total + jnp.concatenate([z_before[part], cur[: rows - comps]], axis=0)
        total = total + jnp.concatenate([cur[comps:], z_after[part]], axis=0)
        total = total + jnp.where(lane == 0, 0.0, pltpu.roll(cur, 1, 1))
        total = total + jnp.where(lane == cols - 1, 0.0, pltpu.roll(cur, cols - 1, 1))
        factor = jnp.concatenate(
            [jnp.broadcast_to(w_halo[r : r + 1], (comps, cols)) for r in range(k * zn, (k + 1) * zn)],
            axis=0,
        )
        values.append(cur + diffusion_factor * factor * (total - 6.0 * cur))
    return values


def first_kernel(
    v, w, x_halo, w_halo, zlo, zhi, a, u, z_first, z_last, x_before_out, x_after_out, e
):
    zn = 4
    rows = x_halo.shape[0] // 4
    count = v.shape[0]
    f = count // zn
    x_before, x_after = x_halo[rows : 2 * rows], x_halo[2 * rows : 3 * rows]
    for z in range(zn):
        explicit_plane(z, v, w, zlo.at[pl.ds(0, f)], zhi.at[pl.ds(0, f)], x_before, x_after, e)
    fill = jnp.zeros((e.shape[0] - count - 2 * rows, v.shape[1]), F32)
    e[count:] = jnp.concatenate(
        [*explicit_sides(v, x_halo, w_halo, zlo, zhi), fill], axis=0
    ).astype(BF16)
    solved = solve(e, a)
    u[...] = solved[:count]
    x_before_out[...] = solved[count : count + rows]
    x_after_out[...] = solved[count + rows : count + 2 * rows]
    z_first[...] = u[0:f].astype(BF16)
    z_last[...] = u[(zn - 1) * f : zn * f].astype(BF16)


def sample_kernel(u, ids, sent_far, packed, picked, sent, sems):
    copies = Copies(sems)
    pack_columns(u, packed, 4)
    sample(packed, ids, picked, sent, message_part(copies, sent, sent_far, 0))
    copies.finish()


def message_part(copies, sent, far, which):
    f = sent.shape[1]

    def ready(part):
        members, _, lanes = part
        copies.start(sent.at[part], far.at[members, pl.ds(which * f, f), lanes])

    return ready


def second_kernel(
    u, w, ids, zlo, zhi, xlo, xhi, a, sent_in, packed_far, sent_far,
    e, after, packed, picked, sent, sems,
):
    del sent_in
    copies = Copies(sems)
    zn = u.shape[0] // zlo.shape[0]
    x_before, x_after = xlo[...], xhi[...]
    for z in range(zn):
        explicit_plane(z, u, w, zlo, zhi, x_before, x_after, e)
    after[...] = solve(e, a)
    pack_columns(after, packed, zn)
    copies.start(packed, packed_far)
    sample(packed, ids, picked, sent, message_part(copies, sent, sent_far, 1))
    copies.finish()


def sample(packed, ids, picked, out, ready):
    pairs, _, rows, lanes = packed.shape
    peers = 2 * pairs
    f = rows // 2
    yn = lanes // 2
    blocks = picked.shape[2] // lanes
    r = lax.broadcasted_iota(jnp.int32, (2 * lanes, lanes), 0)
    row_id = (r % yn) * 4 + r // yn
    for q in range(peers):
        at = (q // 2, q % 2)
        table = jnp.concatenate([packed[(*at, slice(0, f))], packed[(*at, slice(f, rows))]], axis=1)
        wanted = pltpu.roll(ids[q], (GROUP * q) % lanes, 1) if q else ids[q]
        for b in range(blocks):
            hot = jnp.where(row_id == wanted[b : b + 1], 1.0, 0.0).astype(BF16)
            picked[q, :, b * lanes : (b + 1) * lanes] = jnp.dot(
                table, hot, preferred_element_type=F32
            )
    group = lax.broadcasted_iota(jnp.int32, (f, lanes), 1) // GROUP
    per = lanes // GROUP
    halves = out.shape[0] // per
    for b in range(blocks):
        kg, mh = b // halves, b % halves
        held = [picked[q, :, b * lanes : (b + 1) * lanes] for q in range(peers)]
        step = 1
        while step < peers:
            take = (group // step) % 2 == 1
            held = [jnp.where(take, held[(i + step) % peers], held[i]) for i in range(peers)]
            step *= 2
        for ml in range(per):
            out[mh * per + ml, :, kg * lanes : (kg + 1) * lanes] = held[(-ml) % peers].astype(BF16)
        ready((pl.ds(mh * per, per), slice(None), pl.ds(kg * lanes, lanes)))


def gather_rows(got, start, turned, comps=3):
    sources, both, slots = got.shape
    sides = 2
    peers = sources // sides
    xl = both // 2 // comps
    for q in range(peers):
        for side in range(sides):
            for c in range(comps):
                at = (c * peers + q) * xl
                turned[at : at + xl, side * slots : (side + 1) * slots] = got[
                    q * sides + side, start + c * xl : start + (c + 1) * xl
                ]


CONTRACT_ROWS = (((1,), (1,)), ((), ()))


def over_rows(left, right):
    return lax.dot_general(left, right, CONTRACT_ROWS, preferred_element_type=F32)


def over_first(left, right):
    return lax.dot_general(left, right, (((0,), (0,)), ((), ())), preferred_element_type=F32)


def forward_kernel(
    scale, place, got, w_in_far, w_out_far, x, hidden, slope, d, away, w_in, w_out, sems
):
    copies = Copies(sems)
    f = got.shape[1] // 2
    count = 2
    bounds = [0, hidden.shape[0] // 4, hidden.shape[0]]
    parts = [(slice(None), pl.ds(i, j - i)) for i, j in zip(bounds, bounds[1:])]
    arriving = copies.start(w_in_far.at[parts[0]], w_in.at[parts[0]])
    gather_rows(got, 0, x)
    for i in range(count):
        at = slice(bounds[i], bounds[i + 1])
        copies.wait(arriving)
        if i + 1 < count:
            arriving = copies.start(w_in_far.at[parts[i + 1]], w_in.at[parts[i + 1]])
        else:
            copies.start(w_out_far, w_out)
        pre = over_first(w_in[:, at], x[...])
        logistic = jax.nn.sigmoid(pre)
        hidden[at, :] = (pre * logistic).astype(BF16)
        slope[at, :] = (logistic * (1.0 + pre * (1.0 - logistic))).astype(slope.dtype)
    gather_rows(got, f, d)
    copies.finish()
    predicted = over_first(w_out[...], hidden[...])
    d[...] = ((predicted - d[...].astype(F32)) * scale).astype(BF16)
    away_blocks(hidden, d, place[0], away, away.shape[0] // 4)


def block_rows(array, y, core, rows):
    return array[pl.ds(pl.multiple_of((2 * y + core) * rows, rows), rows), :]


def away_blocks(array, right, core, away, rows):
    left = jnp.concatenate([block_rows(array, y, 1 - core, rows) for y in range(4)], axis=0)
    away[...] = over_rows(left, right[...]).astype(BF16)


def delta_in_kernel(place, d, slope, w_out, x, din, away):
    wide = 512
    for i in range(din.shape[0] // wide):
        at = slice(i * wide, (i + 1) * wide)
        back = jnp.dot(w_out[at, :], d[...], preferred_element_type=F32)
        din[at, :] = (back * slope[at, :].astype(F32)).astype(BF16)
    away_blocks(x, din, place[0], away, away.shape[0] // 4)


def fold(block, rows, width):
    extra = rows - block.shape[0]
    pieces = [block[g * extra : (g + 1) * extra, width:] for g in range(block.shape[0] // extra)]
    return jnp.concatenate([block[:, :width], jnp.concatenate(pieces, axis=1)], axis=0)


def unfold(block, rows):
    extra = block.shape[0] - rows
    count = rows // extra
    wide = block.shape[1] // count
    pieces = [block[rows:, g * wide : (g + 1) * wide] for g in range(count)]
    return jnp.concatenate([block[:rows], jnp.concatenate(pieces, axis=0)], axis=1)


def own_blocks(place, array, rows):
    core, y = place[0], place[1]
    return jnp.concatenate(
        [block_rows(array, lax.rem(y + k, 4), core, rows) for k in (2, 1, 3, 0)], axis=0
    )


def add_other_core(place, value, got, n, k):
    rows = value.shape[0] // 4
    at = pl.multiple_of(lax.rem(place[1] + k, 4) * rows, rows)
    return value[n * rows : (n + 1) * rows] + got[pl.ds(at, rows), :].astype(F32)


def keep_out_kernel(place, hidden, d, got, own, plus, minus, far):
    value = over_rows(own_blocks(place, hidden, own.shape[0]), d[...])
    far[...] = add_other_core(place, value, got, 0, 2).astype(BF16)
    plus[...] = add_other_core(place, value, got, 1, 1).astype(BF16)
    minus[...] = add_other_core(place, value, got, 2, 3).astype(BF16)
    own[...] = add_other_core(place, value, got, 3, 0)


def keep_in_kernel(
    place, x, din, got, plus_out, minus_out, far_out, own, up, down, plus, minus
):
    rows, width = plus_out.shape
    half = rows // 2

    def put(which, far_block, plus_block, minus_block):
        up[which, :half] = far_block[:half]
        up[which, half:] = plus_block[half:]
        down[which, :half] = minus_block[:half]
        down[which, half:] = far_block[half:]
        plus[which] = plus_block[:half]
        minus[which] = minus_block[half:]

    put(0, far_out[...], plus_out[...], minus_out[...])
    value = over_rows(own_blocks(place, x, own.shape[0]), din[...])
    put(
        1,
        *(
            fold(add_other_core(place, value, got, n, k), rows, width).astype(BF16)
            for n, k in ((0, 2), (1, 1), (2, 3))
        ),
    )
    own[...] = add_other_core(place, value, got, 3, 0)


def relay_kernel(plus, minus, from_before, from_after, up, down):
    half = plus.shape[1]
    for which in range(plus.shape[0]):
        before = from_before[which, :half].astype(F32)
        after = from_after[which, half:].astype(F32)
        up[which] = (plus[which].astype(F32) + before).astype(BF16)
        down[which] = (minus[which].astype(F32) + after).astype(BF16)


def finish_kernel(
    own_out, own_in, first_before, first_after, last_before, last_after, share_out, share_in
):
    half = last_before.shape[1]
    total = []
    for k in range(2):
        upper = first_after[k, :half].astype(F32) + last_before[k].astype(F32)
        lower = first_before[k, half:].astype(F32) + last_after[k].astype(F32)
        total.append(jnp.concatenate([upper, lower], axis=0))
    share_out[...] = own_out[...] + total[0]
    share_in[...] = own_in[...] + unfold(total[1], share_in.shape[0])


def planes_kernel(got, out):
    yn, comps, zn, xn = out.shape
    peers = got.shape[0]
    xl = xn // peers
    f = comps * xl
    for zh in range(zn // 2):
        for c in range(comps):
            base = zh * f + c * xl
            block = jnp.concatenate(
                [got[q, base : base + xl, :] for q in range(peers)], axis=0
            ).astype(F32)
            turned = block.T
            out[:, c, 2 * zh, :] = turned[0:yn]
            out[:, c, 2 * zh + 1, :] = turned[yn : 2 * yn]


def exchange(array, axis):
    return lax.all_to_all(array, axis, split_axis=0, concat_axis=0, tiled=True)


def swap_cores(array):
    size = lax.axis_size("px")
    return lax.ppermute(array, "px", [(i, i ^ 1) for i in range(size)])


def shift_chips(forward, backward):
    size = lax.axis_size("px")
    up = [(i, (i + 2) % size) for i in range(size)]
    down = [(j, i) for i, j in up]
    return lax.ppermute(forward, "px", up), lax.ppermute(backward, "px", down)


def per_device(velocity, viscosity, implicit_inverse, row_index, row_counts, weight_in, weight_out):
    yn, zn, comps, xn = velocity.shape
    peers = lax.axis_size("pz")
    position = lax.axis_index("px")
    place = jnp.stack([position & 1, position >> 1]).astype(jnp.int32)
    total_y = yn * peers
    xl = xn // peers
    f = comps * xl
    lanes = 2 * yn
    members, slots = row_index.shape[3:]

    sent = call(
        columns_kernel,
        shaped((peers, 2 * (f + xl) + HALO_ROWS, lanes), BF16),
        (
            velocity.transpose(0, 2, 1, 3),
            viscosity,
            row_index.reshape(members, slots).T,
            row_counts.reshape(1, members),
        ),
        scratch=[
            pltpu.VMEM((yn, comps, zn, xn), F32),
            pltpu.VMEM((yn, zn, xn), F32),
            pltpu.VMEM((slots, members), jnp.int32),
            pltpu.VMEM((1, members), jnp.int32),
            pltpu.VMEM((peers * HALO_ROWS, lanes), F32),
            pltpu.SemaphoreType.DMA((4,)),
        ],
        far_in=range(4),
    )
    inverse = implicit_inverse.astype(BF16)
    got = exchange(sent, "pz")
    solve_flops = 2 * zn * f * total_y * total_y
    edge = shaped((f, total_y), BF16)
    x_edge = shaped((zn * comps, total_y), F32)
    ids_all = shaped((peers, 8, lanes), jnp.int32)
    wide_edge = shaped((f + 8, total_y), BF16)
    v, w, x_halo, w_halo, zlo, zhi, ids = call(
        spread_kernel,
        (shaped((zn * f, total_y), BF16), shaped((zn * xl, total_y), BF16))
        + (shaped((4 * zn * comps, total_y), F32), shaped((2 * zn, total_y), F32))
        + (wide_edge, wide_edge, ids_all),
        (got,),
    )
    zlo, zhi = shift((zhi, zlo), ("px", "tr"))
    message = shaped((members, f, peers * slots), BF16)
    both = shaped((members, 2 * f, peers * slots), BF16)
    sample_flops = 2 * peers * f * 256 * members * slots
    sampling = [
        pltpu.VMEM((peers, 2 * f, lanes), BF16),
        pltpu.VMEM((peers, f, members * slots), F32),
        pltpu.VMEM(message.shape, BF16),
    ]
    blocks = shaped((peers // 2, 2, 2 * f, lanes), BF16)
    half_blocks = shaped((peers // 2, 2 * f, lanes), BF16)
    sampling[0] = pltpu.VMEM(blocks.shape, BF16)
    u, z_first, z_last, xlo, xhi = call(
        first_kernel,
        (shaped((zn * f, total_y), F32), edge, edge, x_edge, x_edge),
        (v, w, x_halo, w_halo, zlo, zhi, inverse),
        scratch=[pltpu.VMEM((zn * f + 32, total_y), BF16)],
        flops=solve_flops,
    )
    zlo, zhi = shift((z_last, z_first), ("px", "tr"))
    sent = call(
        sample_kernel,
        both,
        (u, ids),
        scratch=sampling + [pltpu.SemaphoreType.DMA((6,))],
        flops=sample_flops,
        far_out=(0,),
    )
    packed, sent = call(
        second_kernel,
        (blocks, both),
        (u, w, ids, zlo, zhi, xlo, xhi, inverse, sent),
        scratch=[pltpu.VMEM((zn * f, total_y), BF16), pltpu.VMEM((zn * f, total_y), F32)]
        + sampling
        + [pltpu.SemaphoreType.DMA((7,))],
        flops=solve_flops + sample_flops,
        far_in=(8,),
        far_out=(0, 1),
        aliases={8: 1},
    )
    rows_all = exchange(sent, ("pz", "tr"))

    member_in = weight_in[0]
    member_out = weight_out[0]
    width, hid = member_in.shape
    batch = 2 * peers * slots
    spots = lax.axis_size("px")
    loss_scale = 1.0 / math.sqrt(spots * batch)
    matmul_flops = 2 * hid * width * batch

    def forward(*refs):
        forward_kernel(loss_scale, *refs)

    x, hidden, slope, d, away_out = call(
        forward,
        (
            shaped((width, batch), BF16),
            shaped((hid, batch), BF16),
            shaped((hid, batch), BF16),
            shaped((width, batch), BF16),
            shaped((hid // 2, width), BF16),
        ),
        (place, rows_all, member_in, member_out),
        scratch=[
            pltpu.VMEM((width, hid), BF16),
            pltpu.VMEM((hid, width), BF16),
            pltpu.SemaphoreType.DMA((3,)),
        ],
        flops=matmul_flops * 5 // 2,
        far_in=(2, 3),
    )
    got_out = swap_cores(away_out)
    din, away_in = call(
        delta_in_kernel,
        (shaped((hid, batch), BF16), shaped((width // 2, hid), BF16)),
        (place, d, slope, member_out, x),
        flops=matmul_flops * 3 // 2,
    )
    got_in = swap_cores(away_in)

    rows_out, rows_in = hid // spots, width // spots
    block = shaped((rows_out, width), BF16)
    own_out, plus, minus, far = call(
        keep_out_kernel,
        (shaped((rows_out, width), F32), block, block, block),
        (place, hidden, d, got_out),
        flops=matmul_flops // 2,
    )
    block = shaped((2, rows_out, width), BF16)
    part = shaped((2, rows_out // 2, width), BF16)
    own_in, up, down, plus, minus = call(
        keep_in_kernel,
        (shaped((rows_in, hid), F32), block, block, part, part),
        (place, x, din, got_in, plus, minus, far),
        flops=matmul_flops // 2,
    )
    packed, up = lax.optimization_barrier((packed, up))
    arrived = shift_chips(up, down)
    planes = exchange(packed.reshape(peers, 2 * f, lanes), "pz")
    up, down = call(relay_kernel, (part, part), (plus, minus, *arrived), flops=6e9)
    last = shift_chips(up, down)
    share_out, share_in = call(
        finish_kernel,
        (shaped((rows_out, width), F32), shaped((rows_in, hid), F32)),
        (own_out, own_in, *arrived, *last),
        flops=1e6,
    )
    result = call(planes_kernel, shaped((yn, comps, zn, xn), F32), (planes,))
    return (result.transpose(0, 2, 1, 3), share_in[None], share_out[None])


def solution(mesh):
    in_specs = (
        P("pz", ("px", "tr"), None, None),
        P("pz", ("px", "tr"), None),
        P(),
        P("px", "pz", "tr", None, None),
        P("px", "pz", "tr", None),
        P(("pz", "tr"), None, None),
        P(("pz", "tr"), None, None),
    )
    out_specs = (
        P("pz", ("px", "tr"), None, None),
        P(("pz", "tr"), "px", None),
        P(("pz", "tr"), "px", None),
    )
    return jax.shard_map(
        per_device, mesh=mesh, in_specs=in_specs, out_specs=out_specs, check_vma=False
    )
```
